32 devices in a mesh: dp: 16 (over z, x, core), tensor: 2 (over y).
Axes of the slice: x: 2, y: 2, z: 4, core: 2. Of those that a mesh axis runs over, the one named last changes fastest.
Arguments:
- inputs: float32 [8192, 1024], P('dp'), may hold values from -6 to 6
- ln1_gain: float32 [1024], replicated, may hold values from 0.1 to 1.9
- ln1_bias: float32 [1024], replicated, may hold values from -2.5 to 2.5
- w_query: bfloat16 [1024, 1024], P(None, 'tensor'), may hold values from -0.1875 to 0.1875
- w_key: bfloat16 [1024, 1024], P(None, 'tensor'), may hold values from -0.1875 to 0.1875
- w_value: bfloat16 [1024, 1024], P(None, 'tensor'), may hold values from -0.1875 to 0.1875
- w_out: bfloat16 [1024, 1024], P('tensor'), may hold values from -6 to 6
- ln2_gain: float32 [1024], replicated, may hold values from 0.1 to 1.9
- ln2_bias: float32 [1024], replicated, may hold values from -2.5 to 2.5
- w_up: bfloat16 [1024, 4096], P(None, 'tensor'), may hold values from -0.1875 to 0.1875
- w_down: bfloat16 [4096, 1024], P('tensor'), may hold values from -0.09375 to 0.09375
- teacher: float32 [8192, 1024], P('dp'), may hold values from -5 to 5
- valid_mask: int32 [8192], P('dp'), may hold values from 0 to 1, as said below
Outputs:
- output: float32 [8192, 1024], P('dp')
- loss_value: float32 [], replicated
- input_grad: float32 [8192, 1024], P('dp')
- grad_ln1_gain: float32 [1024], P('dp')
- grad_ln1_bias: float32 [1024], P('dp')
- grad_query: float32 [1024, 1024], P('dp', 'tensor')
- grad_key: float32 [1024, 1024], P('dp', 'tensor')
- grad_value: float32 [1024, 1024], P('dp', 'tensor')
- grad_out: float32 [1024, 1024], P('tensor', 'dp')
- grad_ln2_gain: float32 [1024], P('dp')
- grad_ln2_bias: float32 [1024], P('dp')
- grad_up: float32 [1024, 4096], P('dp', 'tensor')
- grad_down: float32 [4096, 1024], P('tensor', 'dp')
The draws below stay inside these ranges and needn't reach their ends.
Inputs may be any that keep to these rules, and one draw needn't show every extreme that they name: `valid_mask`: the first token of each block of 512 rows is valid.
All inputs are finite; a program needn't handle non-finite values.
Results may differ from the reference program's by a relative error of at most 0.015.
Values may be sent and summed in bfloat16 or wider, within the bound.
A program may use at most 192 MiB of HBM per device.

```python
import jax
import jax.numpy as jnp
from jax import lax

D = 1024
FF = 4096
HEADS = 8
HEAD_DIM = 128
SEQ_LEN = 8192
TOK_DEV = 512
SEQS = 1
TOKENS = 8192


def draw_valid_mask(key, part):
    row_ids = jnp.arange(TOKENS, dtype=jnp.int32)
    owners = row_ids // TOK_DEV
    blocks = TOKENS // TOK_DEV
    threshold = 300 + 600 * owners // max(blocks - 1, 1)
    tickets = jax.random.randint(jax.random.fold_in(key, 7), (TOKENS,), 0, 1000, dtype=jnp.int32)
    chosen = (tickets < threshold).astype(jnp.int32)
    leading = (row_ids % TOK_DEV == 0).astype(jnp.int32)
    return jnp.maximum(chosen, leading)


def draw_teacher(key, part):
    values = 2.0 * jax.random.normal(jax.random.fold_in(key, 11), (TOKENS, D), jnp.float32)
    return jnp.clip(values, -5.0, 5.0)


def levels(key, extent, split, low, high):
    def one(axis_at, blocks):
        steps = jax.random.uniform(jax.random.fold_in(jax.random.fold_in(key, 6), axis_at), (blocks,), jnp.float32, low / len(split), high / len(split))
        return jnp.repeat(jnp.exp(steps), extent[axis_at] // blocks).reshape((-1,) + (1,) * (len(extent) - axis_at - 1))

    factor_of = one(*split[0])
    for cut in split[1:]:
        factor_of = factor_of * one(*cut)
    return factor_of


def scatter_about(stream_key, dims, deviation, limit, split=(), kind=jnp.bfloat16):
    loudness = levels(stream_key, dims, split, -0.22, 0.18) if split else 1.0
    array = jax.random.normal(stream_key, dims, jnp.float32) * deviation * loudness
    return jnp.minimum(jnp.maximum(array, -limit), limit).astype(kind)


def setup_inputs(seed: int = 0) -> dict:
    key_list = jax.random.split(jax.random.key(seed), 14)
    inputs = scatter_about(key_list[0], (TOKENS, D), 1.0, 6.0, ((0, 16),), jnp.float32)
    ln1_gain = jnp.clip(1.0 + 0.18 * jax.random.normal(key_list[1], (D,), jnp.float32), 0.1, 1.9)
    ln1_bias = scatter_about(key_list[2], (D,), 0.5, 2.5, (), jnp.float32)
    w_query = scatter_about(key_list[3], (D, D), D ** -0.5, 0.1875, ((1, 2),))
    w_key = scatter_about(key_list[4], (D, D), D ** -0.5, 0.1875, ((1, 2),))
    w_value = scatter_about(key_list[5], (D, D), D ** -0.5, 0.1875, ((1, 2),))
    w_out = scatter_about(key_list[6], (D, D), (max(1, 4 * D // SEQ_LEN)) ** -0.5, 6.0, ((0, 2),))
    ln2_gain = jnp.clip(1.0 + 0.18 * jax.random.normal(key_list[7], (D,), jnp.float32), 0.1, 1.9)
    ln2_bias = scatter_about(key_list[8], (D,), 0.5, 2.5, (), jnp.float32)
    w_up = scatter_about(key_list[9], (D, FF), D ** -0.5, 0.1875, ((1, 2),))
    w_down = scatter_about(key_list[10], (FF, D), FF ** -0.5, 0.09375, ((0, 2),))
    teacher = draw_teacher(jax.random.fold_in(key_list[13], 71), 0)
    valid_mask = draw_valid_mask(jax.random.fold_in(key_list[13], 71), 0)
    return {"inputs": inputs, "ln1_gain": ln1_gain, "ln1_bias": ln1_bias, "w_query": w_query, "w_key": w_key, "w_value": w_value, "w_out": w_out, "ln2_gain": ln2_gain, "ln2_bias": ln2_bias, "w_up": w_up, "w_down": w_down, "teacher": teacher, "valid_mask": valid_mask}


@jax.custom_vjp
def low(v):
    return lax.optimization_barrier(v.astype(jnp.bfloat16)).astype(jnp.float32)

@jax.custom_vjp
def low_back(v):
    return v

def low_keep(v):
    return (low(v), None)

def low_pass(kept, grad):
    return (grad,)

def back_keep(v):
    return (v, None)

def back_low(kept, grad):
    return (low(grad),)
low.defvjp(low_keep, low_pass)
low_back.defvjp(back_keep, back_low)
EPSILON = 1e-05
NEGATIVE = -1e+30

def matmul(left, right):
    return jnp.dot(left, right, precision=lax.Precision.HIGHEST, preferred_element_type=jnp.float32)

def layer_norm(values, gain_vec, bias_vec):
    average = lax.optimization_barrier(jnp.mean(values, axis=-1, keepdims=True))
    centred = values - average
    spread = lax.optimization_barrier(jnp.mean(centred * centred, axis=-1, keepdims=True))
    return centred * lax.rsqrt(spread + EPSILON) * gain_vec + bias_vec

def attend(queries, keys_all, values_all):
    length = queries.shape[0]
    block_rows = min(512, length)
    block_count = length // block_rows
    key_pos = jnp.arange(length, dtype=jnp.int32)

    def one_block(item_pair):
        q_block, block_start = item_pair
        raw_scores = jnp.einsum('qhe,khe->hqk', q_block, keys_all, precision=lax.Precision.HIGHEST) * HEAD_DIM ** (-0.5)
        scores = low_back(raw_scores)
        q_pos = block_start + jnp.arange(block_rows, dtype=jnp.int32)
        allowed = q_pos[:, None] >= key_pos[None, :]
        masked = jnp.where(allowed[None], scores, NEGATIVE)
        prob_rows = low(jax.nn.softmax(masked, axis=-1))
        return jnp.einsum('hqk,khe->qhe', prob_rows, values_all, precision=lax.Precision.HIGHEST)
    q_blocks = queries.reshape(block_count, block_rows, HEADS, HEAD_DIM)
    starts = jnp.arange(block_count, dtype=jnp.int32) * block_rows
    blocks_out = lax.map(jax.checkpoint(one_block), (q_blocks, starts))
    return blocks_out.reshape(length, HEADS, HEAD_DIM)

def layer_forward(inputs, ln1_gain, ln1_bias, w_query, w_key, w_value, w_out, ln2_gain, ln2_bias, w_up, w_down, teacher, weight_rows, factor):
    length = inputs.shape[0]
    n_one = low(layer_norm(inputs, ln1_gain, ln1_bias))
    queries = low(low_back(matmul(n_one, w_query))).reshape(length, HEADS, HEAD_DIM)
    keys_all = low(low_back(matmul(n_one, w_key))).reshape(length, HEADS, HEAD_DIM)
    values_all = low(low_back(matmul(n_one, w_value))).reshape(length, HEADS, HEAD_DIM)
    attn = attend(queries, keys_all, values_all)
    context = low(low_back(attn)).reshape(length, D)
    hidden = inputs + low_back(matmul(context, w_out))
    n_two = low(layer_norm(hidden, ln2_gain, ln2_bias))
    pre_act = low_back(matmul(n_two, w_up))
    active = low(jnp.maximum(pre_act, 0.0))
    output = hidden + low_back(matmul(active, w_down))
    misfit = output - teacher
    part_loss = jnp.sum(weight_rows[:, None] * misfit * misfit) * factor
    return (output, part_loss)

def reference(inputs, ln1_gain, ln1_bias, w_query, w_key, w_value, w_out, ln2_gain, ln2_bias, w_up, w_down, teacher, valid_mask):
    params = tuple((weight.astype(jnp.float32) for weight in (ln1_gain, ln1_bias, w_query, w_key, w_value, w_out, ln2_gain, ln2_bias, w_up, w_down)))
    weight_rows = valid_mask.astype(jnp.float32)
    valid_count = jnp.sum(weight_rows)
    factor = TOKENS / (2.0 * valid_count)
    seq_inputs = inputs.astype(jnp.float32).reshape(SEQS, SEQ_LEN, D)
    seq_teacher = teacher.astype(jnp.float32).reshape(SEQS, SEQ_LEN, D)
    seq_weights = weight_rows.reshape(SEQS, SEQ_LEN)

    def one_sequence(totals, item_triple):
        seq_x, seq_t, seq_w = item_triple

        def forward(x_in, *weights):
            return layer_forward(x_in, *weights, seq_t, seq_w, factor)
        (output, part_loss), pull_back = jax.vjp(forward, seq_x, *params)
        gradients = pull_back((jnp.zeros_like(output), jnp.ones_like(part_loss)))
        totals = tuple((running + extra for running, extra in zip(totals, gradients[1:])))
        return (totals, (output, part_loss, gradients[0]))
    start_totals = tuple((jnp.zeros_like(weight) for weight in params))
    totals, (outputs, part_losses, input_grads) = lax.scan(one_sequence, start_totals, (seq_inputs, seq_teacher, seq_weights))
    loss_value = jnp.sum(part_losses) / TOKENS
    return (outputs.reshape(TOKENS, D), loss_value, input_grads.reshape(TOKENS, D), totals[0], totals[1], totals[2], totals[3], totals[4], totals[5], totals[6], totals[7], totals[8], totals[9])
```

```python
import functools

import jax
import jax.numpy as jnp
from jax import lax
from jax.experimental import pallas as pl
from jax.experimental.pallas import tpu as pltpu
from jax.sharding import PartitionSpec as P

HEAD_DIM = 128
SEQ_DEV = 16
EPSILON = 1e-05
NEGATIVE = -1e30
LOG_SCALE = 1.4426950408889634 * HEAD_DIM ** (-0.5)
HEAD_SCALE = HEAD_DIM ** (-0.5)
CHUNKS = 4
f32 = jnp.float32
bf16 = jnp.bfloat16


def nn(a, b):
    return lax.dot_general(a, b, (((1,), (0,)), ((), ())), preferred_element_type=f32)


def nt(a, b):
    return lax.dot_general(a, b, (((1,), (1,)), ((), ())), preferred_element_type=f32)


def tn(a, b):
    return lax.dot_general(a, b, (((0,), (0,)), ((), ())), preferred_element_type=f32)


def remote(src, dst, send_sem, recv_sem, device):
    return pltpu.make_async_remote_copy(
        src_ref=src,
        dst_ref=dst,
        send_sem=send_sem,
        recv_sem=recv_sem,
        device_id=device,
        device_id_type=pl.DeviceIdType.MESH,
    )


class Place:
    def __init__(self):
        index = lax.axis_index("dp")
        self.pos = lax.rem(index, SEQ_DEV)
        self.base = index - self.pos
        self.slab = lax.div(self.pos, 4)
        self.seat = lax.rem(self.pos, 4)
        self.side = lax.axis_index("tensor")
        seat = self.seat
        self.core_seat = seat + 1 - 2 * lax.rem(seat, 2)
        self.x_seat = lax.rem(seat + 2, 4)
        self.far_seat = 3 - seat

    def dev(self, slab, seat):
        return {"dp": self.base + slab * 4 + seat, "tensor": self.side}

    def other_side(self):
        return {"dp": self.base + self.pos, "tensor": 1 - self.side}

    def turned(self, slab):
        even = lax.rem(slab, 2) == 0
        return jnp.where(even, self.seat, self.far_seat)

    def peers(self, same, far, near, side):
        found = []
        for step in range(1, 4):
            other = lax.rem(self.slab + step, 4)
            if same:
                found.append(self.dev(other, self.seat))
            if far:
                found.append(self.dev(other, self.far_seat))
        if far:
            found.append(self.dev(self.slab, self.far_seat))
        if near:
            found.append(self.dev(self.slab, self.core_seat))
            found.append(self.dev(self.slab, self.x_seat))
        if side:
            found.append(self.other_side())
        return found


def greet(peers):
    barrier = pltpu.get_barrier_semaphore()
    for peer in peers:
        pl.semaphore_signal(
            barrier, inc=1, device_id=peer, device_id_type=pl.DeviceIdType.MESH
        )
    return functools.partial(pl.semaphore_wait, barrier, len(peers))


def norm_stats(values):
    average = jnp.mean(values, axis=-1, keepdims=True)
    centred = values - average
    inverse = lax.rsqrt(jnp.mean(centred * centred, axis=-1, keepdims=True) + EPSILON)
    return centred * inverse, inverse


class Summed:
    def __init__(self, at, tile, core_in, x_buf, x_in, z_buf, z_in, send, recv):
        self.at, self.tile = at, tile
        self.core_in, self.x_buf, self.x_in = core_in, x_buf, x_in
        self.z_buf, self.z_in = z_buf, z_in
        self.send, self.recv = send, recv

    def hop(self, src, dst, k, device):
        return remote(src, dst, self.send.at[k], self.recv.at[k], device)

    def near(self):
        at = self.at
        return self.hop(self.tile, self.core_in, 0, at.dev(at.slab, at.core_seat))

    def wide(self):
        at = self.at
        return self.hop(self.x_buf, self.x_in, 1, at.dev(at.slab, at.x_seat))

    def far(self, step):
        at = self.at
        device = at.dev(lax.rem(at.slab + step, 4), at.seat)
        return self.hop(self.z_buf, self.z_in.at[at.slab], 1 + step, device)

    def one(self):
        self.near().start()

    def two(self):
        self.near().wait()
        self.x_buf[...] = self.tile[...] + self.core_in[...]
        self.wide().start()

    def three(self):
        self.wide().wait()
        total = self.x_buf[...] + self.x_in[...]
        self.z_buf[...] = total
        self.z_in[self.at.slab] = total
        for step in range(1, 4):
            self.far(step).start()

    def four(self):
        at = self.at
        for step in range(1, 4):
            self.far(step).wait_send()
            source = lax.rem(at.slab - step + 4, 4)
            slot = self.z_in.at[source]
            self.hop(slot, slot, 1 + step, at.dev(source, at.seat)).wait_recv()
        return (self.z_in[0] + self.z_in[1]) + (self.z_in[2] + self.z_in[3])


def summed_scratch(shape):
    return [
        pltpu.VMEM(shape, f32),
        pltpu.VMEM(shape, f32),
        pltpu.VMEM(shape, f32),
        pltpu.VMEM(shape, f32),
        pltpu.VMEM(shape, f32),
        pltpu.VMEM((4,) + shape, f32),
        pltpu.SemaphoreType.DMA((5,)),
        pltpu.SemaphoreType.DMA((5,)),
    ]


def forward_kernel(
    x_ref, gain_ref, bias_ref, wq_ref, wk_ref, wv_ref, wo_ref, mask_ref,
    none_ref, kv_ref, q_ref, ot_ref, ls_ref, ctx_ref, cnt_ref, wo_in_ref,
    kvs, qs, os, top, low,
    z_send, z_recv, q_send, q_recv, c_send, c_recv, x_send, x_recv, f_send, f_recv,
    o_send, o_recv, w_sem,
    tile, core_in, x_buf, x_in, z_buf, z_in, t_send, t_recv,
):
    at = Place()
    rows = x_ref.shape[0]
    slab, seat = at.slab, at.seat
    ready = greet(at.peers(True, True, True, True))

    def block(kv_slab, kv_seat):
        return kv_ref.at[:, pl.ds(pl.multiple_of((kv_slab * 4 + kv_seat) * rows, rows), rows), :]

    normed, _ = norm_stats(x_ref[...])
    n_one = (normed * gain_ref[...] + bias_ref[...]).astype(bf16)
    none_ref[...] = n_one
    query = nn(n_one, wq_ref[...]).astype(bf16)
    for h in range(4):
        qs[h] = query[:, h * HEAD_DIM : (h + 1) * HEAD_DIM]
    for j, w_ref in enumerate((wk_ref, wv_ref)):
        made = nn(n_one, w_ref[...]).astype(bf16)
        for h in range(4):
            kvs[h, j] = made[:, h * HEAD_DIM : (h + 1) * HEAD_DIM]
    count = jnp.sum(mask_ref[...].astype(f32), axis=1, keepdims=True)
    tile[...] = jnp.broadcast_to(count, tile.shape)
    total = Summed(at, tile, core_in, x_buf, x_in, z_buf, z_in, t_send, t_recv)
    ready()

    def order(k):
        down = jnp.where(3 - k > slab, 3 - k, 2 - k)
        up = jnp.where(k < slab, k, k + 1)
        return jnp.where(slab < 2, down, up)

    goal = at.turned(slab)
    even = lax.rem(slab, 2) == 0

    def q_copy(h):
        return remote(qs.at[h], q_ref.at[slab], q_send.at[h], q_recv.at[slab], at.dev(h, goal))

    def kv_copy(h):
        return remote(
            kvs.at[h], block(slab, seat), z_send.at[h], z_recv.at[slab], at.dev(h, seat)
        )

    def near_copy(kv_slab):
        part = block(kv_slab, seat)
        return remote(
            part, part, c_send.at[kv_slab], c_recv.at[kv_slab], at.dev(slab, at.core_seat)
        )

    def wide_copy(kv_slab):
        part = block(kv_slab, seat)
        return remote(part, part, x_send.at[kv_slab], x_recv.at[kv_slab], at.dev(slab, at.x_seat))

    def pass_copy(kv_slab):
        part = block(kv_slab, at.x_seat)
        return remote(
            part, part, f_send.at[kv_slab], f_recv.at[kv_slab], at.dev(slab, at.core_seat)
        )

    for k in range(3):
        q_copy(order(k)).start()

    @pl.when(even)
    def _():
        q_ref[slab] = qs[slab]

    @pl.when(jnp.logical_not(even))
    def _():
        q_copy(slab).start()

    for k in range(3):
        kv_copy(order(k)).start()
    own = pl.ds(pl.multiple_of(at.pos * rows, rows), rows)
    kv_ref[:, own, :] = kvs[slab]
    near_copy(slab).start()
    wide_copy(slab).start()
    w_copy = remote(wo_ref, wo_in_ref, w_sem.at[0], w_sem.at[1], at.other_side())
    w_copy.start()
    total.one()
    top[...] = jnp.full_like(top, NEGATIVE)
    low[...] = jnp.zeros_like(low)
    ot_ref[...] = jnp.zeros_like(ot_ref)

    def relay(kv_slab):
        @pl.when(slab != kv_slab)
        def _():
            part = block(kv_slab, seat)
            remote(
                part, part, z_send.at[kv_slab], z_recv.at[kv_slab], at.dev(kv_slab, seat)
            ).wait_recv()
            near_copy(kv_slab).start()
            wide_copy(kv_slab).start()

    def arrive(kv_slab):
        part = block(kv_slab, at.x_seat)
        remote(
            part, part, x_send.at[kv_slab], x_recv.at[kv_slab], at.dev(slab, at.x_seat)
        ).wait_recv()
        pass_copy(kv_slab).start()
        part = block(kv_slab, at.core_seat)
        remote(
            part, part, c_send.at[kv_slab], c_recv.at[kv_slab], at.dev(slab, at.core_seat)
        ).wait_recv()
        part = block(kv_slab, at.far_seat)
        remote(
            part, part, f_send.at[kv_slab], f_recv.at[kv_slab], at.dev(slab, at.core_seat)
        ).wait_recv()

    def unit(slot, start, size, diagonal):
        keys_at = pl.ds(pl.multiple_of(start, rows), size)
        scores = nt(kv_ref[0, keys_at, :], q_ref[slot]) * LOG_SCALE
        if diagonal:
            allowed = lax.broadcasted_iota(jnp.int32, scores.shape, 0) <= lax.broadcasted_iota(
                jnp.int32, scores.shape, 1
            )
            scores = jnp.where(allowed, scores, NEGATIVE)
        before = top[slot]
        after = jnp.maximum(before, jnp.max(scores, axis=0, keepdims=True))
        prob = jnp.exp2(scores - after)
        shrink = jnp.exp2(before - after)
        low[slot] = low[slot] * shrink + jnp.sum(prob, axis=0, keepdims=True)
        top[slot] = after
        ot_ref[slot] = ot_ref[slot] * shrink + tn(kv_ref[1, keys_at, :], prob.astype(bf16))

    def o_copy(slot):
        return remote(
            os.at[slot], ctx_ref.at[slab], o_send.at[slot], o_recv.at[slab],
            at.dev(slot, at.turned(slot)),
        )

    for step in range(1, 4):
        source = lax.rem(slab + step, 4)
        part = q_ref.at[source]
        remote(
            part, part, q_send.at[source], q_recv.at[source], at.dev(source, seat)
        ).wait_recv()

    @pl.when(jnp.logical_not(even))
    def _():
        part = q_ref.at[slab]
        remote(part, part, q_send.at[slab], q_recv.at[slab], at.dev(slab, seat)).wait_recv()

    relay(0)
    for kv_slab in range(4):
        arrive(kv_slab)
        first = kv_slab * 4 * rows
        mine = at.turned(kv_slab)

        def whole(index, _):
            unit(kv_slab, first + index * rows, rows, False)
            return 0

        lax.fori_loop(0, mine, whole, 0)
        unit(kv_slab, first + mine * rows, rows, True)
        done = ot_ref[kv_slab] / low[kv_slab]
        ot_ref[kv_slab] = done
        ls_ref[kv_slab] = top[kv_slab] + jnp.log2(low[kv_slab])
        os[kv_slab] = done.T.astype(bf16)
        home = jnp.logical_and(slab == kv_slab, even)

        @pl.when(home)
        def _():
            ctx_ref[slab] = os[kv_slab]

        @pl.when(jnp.logical_not(home))
        def _():
            o_copy(kv_slab).start()

        if kv_slab == 0:
            total.two()
        if kv_slab == 1:
            total.three()
        if kv_slab < 3:
            relay(kv_slab + 1)

            def pair(index, _):
                slot = kv_slab + 1 + lax.div(index, 2)
                unit(slot, first + lax.rem(index, 2) * 2 * rows, 2 * rows, False)
                return 0

            lax.fori_loop(0, 2 * (3 - kv_slab), pair, 0)
    cnt_ref[...] = total.four()
    for k in range(3):
        q_copy(order(k)).wait_send()
        kv_copy(order(k)).wait_send()

    @pl.when(jnp.logical_not(even))
    def _():
        q_copy(slab).wait_send()

    for kv_slab in range(4):
        near_copy(kv_slab).wait_send()
        wide_copy(kv_slab).wait_send()
        pass_copy(kv_slab).wait_send()
        home = jnp.logical_and(slab == kv_slab, even)

        @pl.when(jnp.logical_not(home))
        def _():
            o_copy(kv_slab).wait_send()

        part = ctx_ref.at[kv_slab]
        local = jnp.logical_and(slab == kv_slab, even)

        @pl.when(jnp.logical_not(local))
        def _():
            remote(
                part, part, o_send.at[kv_slab], o_recv.at[kv_slab], at.dev(kv_slab, seat)
            ).wait_recv()

    w_copy.wait()


def heads_row(ref, rows_at):
    return jnp.concatenate([ref[h, rows_at, :] for h in range(4)], axis=1)


def middle_kernel(
    token_total,
    ctx_ref, x_hbm, wo_hbm, wo_in_hbm, gain_ref, bias_ref, wup_hbm, wdn_hbm, teach_hbm,
    mask_ref, cnt_ref,
    out_ref, dh_ref, do_ref, gf_ref, go_ref, vec_ref,
    x_buf, wo, wo_in, wup, wdn, teach, load,
    ctx_in, normed_s, inv_s, n2s, acts, gfs, dpres, gas, dcs,
    fs, fr, bs, br,
    e_send, e_recv, f_send, f_recv, b_send, b_recv, d_send, d_recv,
):
    at = Place()
    slab, seat = at.slab, at.seat
    rows = out_ref.shape[0]
    part_rows = rows // CHUNKS
    ready = greet(at.peers(True, True, False, True))
    loads = [
        pltpu.make_async_copy(src, dst, load.at[k])
        for k, (src, dst) in enumerate(
            (
                (wo_hbm, wo), (wo_in_hbm, wo_in), (x_hbm, x_buf), (wup_hbm, wup),
                (wdn_hbm, wdn), (teach_hbm, teach),
            )
        )
    ]
    for copy in loads:
        copy.start()
    ready()

    def e_copy(c):
        part = pl.ds(pl.multiple_of(c * part_rows, part_rows), part_rows)
        return remote(
            ctx_ref.at[:, part, :], ctx_in.at[:, part, :], e_send.at[c], e_recv.at[c],
            at.other_side(),
        )

    def f_copy(c):
        return remote(fs.at[c], fr.at[c], f_send.at[c], f_recv.at[c], at.other_side())

    def b_copy(c):
        return remote(bs.at[c], br.at[c], b_send.at[c], b_recv.at[c], at.other_side())

    for c in range(CHUNKS):
        e_copy(c).start()
    for k in range(3):
        loads[k].wait()

    def forward(c, _):
        part = pl.ds(pl.multiple_of(c * part_rows, part_rows), part_rows)
        e_copy(c).wait()
        hidden = x_buf[part, :] + (
            nn(heads_row(ctx_ref, part), wo[...]) + nn(heads_row(ctx_in, part), wo_in[...])
        )
        out_ref[part, :] = hidden
        normed, inverse = norm_stats(hidden)
        normed_s[part, :] = normed
        inv_s[part, :] = inverse
        n_two = (normed * gain_ref[...] + bias_ref[...]).astype(bf16)
        n2s[part, :] = n_two

        @pl.when(c == 0)
        def _():
            loads[3].wait()
            loads[4].wait()

        active = jnp.maximum(nn(n_two, wup[...]), 0.0).astype(bf16)
        acts[part, :] = active
        fs[c] = nn(active, wdn[...]).astype(bf16)
        f_copy(c).start()
        return 0

    lax.fori_loop(0, CHUNKS, forward, 0)
    loads[5].wait()
    scale = token_total / cnt_ref[0:1, 0:1]
    vec_ref[...] = jnp.zeros_like(vec_ref)

    def back_one(c, _):
        part = pl.ds(pl.multiple_of(c * part_rows, part_rows), part_rows)
        f_copy(c).wait()
        output = out_ref[part, :] + (fs[c].astype(f32) + fr[c].astype(f32))
        out_ref[part, :] = output
        misfit = output - teach[part, :]
        held = misfit * mask_ref[part, :]
        vec_ref[2:3, :] += jnp.sum(held * misfit, axis=0, keepdims=True)
        d_output = scale * held
        dh_ref[part, :] = d_output
        g_ffn = d_output.astype(bf16)
        gfs[part, :] = g_ffn
        d_active = nt(g_ffn, wdn[...])
        d_pre = jnp.where(acts[part, :] > 0, d_active, 0.0).astype(bf16)
        dpres[part, :] = d_pre
        bs[c] = nt(d_pre, wup[...]).astype(bf16)
        b_copy(c).start()
        return 0

    lax.fori_loop(0, CHUNKS, back_one, 0)
    half = gf_ref.shape[2]

    def down_grad(k, _):
        cols = pl.ds(pl.multiple_of(k * half, half), half)
        gf_ref[2 + k] = tn(gfs[...], acts[:, cols]).astype(bf16)
        return 0

    lax.fori_loop(0, 2, down_grad, 0)

    def d_copy(c, h):
        part = pl.ds(pl.multiple_of(c * part_rows, part_rows), part_rows)
        return remote(
            dcs.at[h, part, :], do_ref.at[slab, part, :], d_send.at[c, h], d_recv.at[c, slab],
            at.dev(h, at.turned(slab)),
        )

    even = lax.rem(slab, 2) == 0

    def back_two(c, _):
        part = pl.ds(pl.multiple_of(c * part_rows, part_rows), part_rows)
        b_copy(c).wait()
        d_two = bs[c].astype(f32) + br[c].astype(f32)
        normed = normed_s[part, :]
        scaled = d_two * gain_ref[...]
        first = jnp.mean(scaled, axis=-1, keepdims=True)
        second = jnp.mean(scaled * normed, axis=-1, keepdims=True)
        d_hidden = dh_ref[part, :] + inv_s[part, :] * (scaled - first - normed * second)
        vec_ref[0:1, :] += jnp.sum(d_two * normed, axis=0, keepdims=True)
        vec_ref[1:2, :] += jnp.sum(d_two, axis=0, keepdims=True)
        dh_ref[part, :] = d_hidden
        g_attn = d_hidden.astype(bf16)
        gas[part, :] = g_attn
        d_context = nt(g_attn, wo[...]).astype(bf16)
        for h in range(4):
            dcs[h, part, :] = d_context[:, h * HEAD_DIM : (h + 1) * HEAD_DIM]
            home = jnp.logical_and(slab == h, even)

            @pl.when(home)
            def _():
                do_ref[slab, part, :] = dcs[h, part, :]

            @pl.when(jnp.logical_not(home))
            def _():
                d_copy(c, h).start()

        return 0

    lax.fori_loop(0, CHUNKS, back_two, 0)

    def up_grad(k, _):
        cols = pl.ds(pl.multiple_of(k * half, half), half)
        gf_ref[k] = tn(n2s[...], dpres[:, cols]).astype(bf16)
        return 0

    lax.fori_loop(0, 2, up_grad, 0)
    go_ref[...] = tn(gas[...], heads_row(ctx_ref, slice(None))).astype(bf16)

    def finish(c, _):
        part = pl.ds(pl.multiple_of(c * part_rows, part_rows), part_rows)
        for h in range(4):
            home = jnp.logical_and(slab == h, even)

            @pl.when(jnp.logical_not(home))
            def _():
                d_copy(c, h).wait_send()
                slot = do_ref.at[h, part, :]
                remote(
                    slot, slot, d_send.at[c, h], d_recv.at[c, h], at.dev(h, seat)
                ).wait_recv()

        return 0

    lax.fori_loop(0, CHUNKS, finish, 0)


def backward_kernel(
    kv_ref, q_ref, ot_ref, ls_ref, do_ref,
    dq_ref, dkv_ref,
    grads, acc, delta, near_out, near_in, wide_out, wide_in, home_out, dqs,
    n_send, n_recv, w_send, w_recv, h_send, h_recv, d_send, d_recv,
):
    at = Place()
    slab, seat = at.slab, at.seat
    rows = q_ref.shape[1]
    even = lax.rem(slab, 2) == 0
    ready = greet(at.peers(True, True, True, False))
    acc[...] = jnp.zeros_like(acc)
    for slot in range(4):
        delta[slot] = jnp.sum(do_ref[slot].astype(f32).T * ot_ref[slot], axis=0, keepdims=True)
    ready()

    def unit(slot, start, local, size, diagonal):
        keys_at = pl.ds(pl.multiple_of(start, rows), size)
        keys = kv_ref[0, keys_at, :]
        query = q_ref[slot]
        d_out = do_ref[slot]
        scores = nt(keys, query) * LOG_SCALE - ls_ref[slot]
        if diagonal:
            allowed = lax.broadcasted_iota(jnp.int32, scores.shape, 0) <= lax.broadcasted_iota(
                jnp.int32, scores.shape, 1
            )
            scores = jnp.where(allowed, scores, NEGATIVE)
        prob = jnp.exp2(scores)
        d_probs = nt(kv_ref[1, keys_at, :], d_out)
        d_scores = (prob * (d_probs - delta[slot])).astype(bf16)
        here = pl.ds(pl.multiple_of(local, rows), size)
        grads[1, here, :] += nn(prob.astype(bf16), d_out)
        grads[0, here, :] += nn(d_scores, query)
        acc[slot] += tn(keys, d_scores)

    def block(ref, which):
        return ref[:, pl.ds(pl.multiple_of(which * rows, rows), rows), :]

    def near_copy(kv_slab):
        k = kv_slab
        return remote(
            near_out, near_in.at[k], n_send.at[k], n_recv.at[k], at.dev(slab, at.core_seat)
        )

    def wide_copy(kv_slab):
        k = kv_slab
        return remote(
            wide_out.at[k], wide_in.at[k], w_send.at[k], w_recv.at[k], at.dev(slab, at.x_seat)
        )

    def home_copy(kv_slab):
        k = kv_slab
        return remote(
            home_out.at[k], dkv_ref.at[slab], h_send.at[k], h_recv.at[slab], at.dev(k, seat)
        )

    pair_scale = HEAD_SCALE

    for step, kv_slab in enumerate((3, 2, 1, 0)):
        grads[...] = jnp.zeros_like(grads)
        first = kv_slab * 4 * rows
        mine = at.turned(kv_slab)

        def whole(index, _):
            unit(kv_slab, first + index * rows, index * rows, rows, False)
            return 0

        lax.fori_loop(0, mine, whole, 0)
        unit(kv_slab, first + mine * rows, mine * rows, rows, True)

        def pair(index, _):
            slot = kv_slab + 1 + lax.div(index, 2)
            local = lax.rem(index, 2) * 2 * rows
            unit(slot, first + local, local, 2 * rows, False)
            return 0

        if kv_slab < 3:
            lax.fori_loop(0, 2 * (3 - kv_slab), pair, 0)
            near_copy(kv_slab + 1).wait_send()
        near_out[0] = block(grads, at.core_seat).astype(bf16)
        near_out[1] = block(grads, at.far_seat).astype(bf16)
        near_copy(kv_slab).start()
        near_copy(kv_slab).wait_recv()
        wide_out[kv_slab] = (block(grads, at.x_seat) + near_in[kv_slab, 1].astype(f32)).astype(
            bf16
        )
        wide_copy(kv_slab).start()
        kept = block(grads, seat) + near_in[kv_slab, 0].astype(f32)
        wide_copy(kv_slab).wait_recv()
        kept = kept + wide_in[kv_slab].astype(f32)
        home_out[kv_slab, 0] = (kept[0] * pair_scale).astype(bf16)
        home_out[kv_slab, 1] = kept[1].astype(bf16)

        @pl.when(slab == kv_slab)
        def _():
            dkv_ref[slab] = home_out[kv_slab]

        @pl.when(slab != kv_slab)
        def _():
            home_copy(kv_slab).start()

    near_copy(0).wait_send()

    def d_copy(slot):
        return remote(
            dqs.at[slot], dq_ref.at[slab], d_send.at[slot], d_recv.at[slab],
            at.dev(slot, at.turned(slot)),
        )

    for slot in range(4):
        dqs[slot] = (acc[slot] * HEAD_SCALE).T.astype(bf16)
        home = jnp.logical_and(slab == slot, even)

        @pl.when(home)
        def _():
            dq_ref[slab] = dqs[slot]

        @pl.when(jnp.logical_not(home))
        def _():
            d_copy(slot).start()

    for k in range(4):
        wide_copy(k).wait_send()
        home = jnp.logical_and(slab == k, even)

        @pl.when(slab != k)
        def _():
            home_copy(k).wait_send()
            part = dkv_ref.at[k]
            remote(part, part, h_send.at[k], h_recv.at[k], at.dev(k, seat)).wait_recv()

        @pl.when(jnp.logical_not(home))
        def _():
            d_copy(k).wait_send()
            part = dq_ref.at[k]
            remote(part, part, d_send.at[k], d_recv.at[k], at.dev(k, seat)).wait_recv()


def tail_kernel(
    dq_ref, dkv_ref, n_one_ref, wq_ref, wk_ref, wv_ref, x_ref, gain_ref, dh_ref, vec_ref,
    gf_ref, go_ref,
    ig_ref, rs_ref, vsum_ref,
    ga, rc, s1, rx, s2, rz, bs, br, dcat,
    b_send, b_recv, c_send, c_recv, x_send, x_recv, z_send, z_recv,
    tile, core_in, x_buf, x_in, z_buf, z_in, t_send, t_recv,
):
    at = Place()
    slab, seat = at.slab, at.seat
    core = lax.rem(seat, 2)
    wide = lax.div(seat, 2)
    rows = x_ref.shape[0]
    part_rows = rows // CHUNKS
    pieces = rc.shape[0]
    early = gf_ref.shape[0]
    ready = greet(at.peers(True, False, True, True))

    def source(k):
        return gf_ref.at[k] if k < early else ga.at[k - early]

    def c_copy(k):
        return remote(
            source(k).at[:, :, 1 - core], rc.at[k], c_send.at[k], c_recv.at[k],
            at.dev(slab, at.core_seat),
        )

    def x_copy(k):
        return remote(
            s1.at[k, :, 1 - wide], rx.at[k], x_send.at[k], x_recv.at[k], at.dev(slab, at.x_seat)
        )

    def z_copy(k, step):
        to = lax.rem(slab + step, 4)
        return remote(
            s2.at[k, to], rz.at[k, step - 1], z_send.at[k, step - 1], z_recv.at[k, step - 1],
            at.dev(to, seat),
        )

    def b_copy(c):
        return remote(bs.at[c], br.at[c], b_send.at[c], b_recv.at[c], at.other_side())

    ready()
    for k in range(early):
        c_copy(k).start()
    dcat[0] = heads_row(dq_ref, slice(None))
    for j in range(2):
        dcat[1 + j] = jnp.concatenate([dkv_ref[h, j] for h in range(4)], axis=1)

    def side_part(c, _):
        part = pl.ds(pl.multiple_of(c * part_rows, part_rows), part_rows)
        bs[c] = (
            nt(dcat[0, part, :], wq_ref[...])
            + nt(dcat[1, part, :], wk_ref[...])
            + nt(dcat[2, part, :], wv_ref[...])
        ).astype(bf16)
        b_copy(c).start()
        return 0

    lax.fori_loop(0, CHUNKS, side_part, 0)
    shape = ga.shape[1:5]
    cols = dcat.shape[2]
    ga[0, :, :, :, :, 0:cols] = go_ref[...]
    for j in range(3):
        made = tn(n_one_ref[...], dcat[j]).astype(bf16).reshape(shape + (cols,))
        k, half = divmod(j + 1, 2)
        ga[k, :, :, :, :, half * cols : (half + 1) * cols] = made
    for k in range(early, pieces):
        c_copy(k).start()

    def add_core(k):
        c_copy(k).wait_recv()

        def one(i, _):
            s1[k, i] = (source(k)[i, :, core].astype(f32) + rc[k, i].astype(f32)).astype(bf16)
            return 0

        lax.fori_loop(0, 4, one, 0)
        x_copy(k).start()

    def add_wide(k):
        x_copy(k).wait_recv()

        def one(i, _):
            s2[k, i] = (s1[k, i, wide].astype(f32) + rx[k, i].astype(f32)).astype(bf16)
            return 0

        lax.fori_loop(0, 4, one, 0)
        for step in range(1, 4):
            z_copy(k, step).start()

    def add_far(k):
        for step in range(1, 4):
            z_copy(k, step).wait_recv()
        rs_ref[k] = (s2[k, slab].astype(f32) + rz[k, 0].astype(f32)) + (
            rz[k, 1].astype(f32) + rz[k, 2].astype(f32)
        )

    for k in range(pieces):
        add_core(k)
    tile[...] = vec_ref[...]
    tile[3:5, :] = jnp.zeros_like(tile[3:5, :])

    def side_sum(c, _):
        part = pl.ds(pl.multiple_of(c * part_rows, part_rows), part_rows)
        b_copy(c).wait()
        d_one = bs[c].astype(f32) + br[c].astype(f32)
        normed, inverse = norm_stats(x_ref[part, :])
        scaled = d_one * gain_ref[...]
        first = jnp.mean(scaled, axis=-1, keepdims=True)
        second = jnp.mean(scaled * normed, axis=-1, keepdims=True)
        ig_ref[part, :] = dh_ref[part, :] + inverse * (scaled - first - normed * second)
        tile[3:4, :] += jnp.sum(d_one * normed, axis=0, keepdims=True)
        tile[4:5, :] += jnp.sum(d_one, axis=0, keepdims=True)
        return 0

    lax.fori_loop(0, CHUNKS, side_sum, 0)
    total = Summed(at, tile, core_in, x_buf, x_in, z_buf, z_in, t_send, t_recv)
    total.one()
    for k in range(pieces):
        add_wide(k)
        if k == 0:
            total.two()
        if k == 1:
            total.three()
    for k in range(pieces):
        add_far(k)
    vsum_ref[...] = total.four()
    for k in range(pieces):
        c_copy(k).wait_send()
        x_copy(k).wait_send()
        for step in range(1, 4):
            z_copy(k, step).wait_send()


def in_vmem():
    return pl.BlockSpec(memory_space=pltpu.VMEM)


def in_hbm():
    return pl.BlockSpec(memory_space=pl.ANY)


def dma(*shape):
    return pltpu.SemaphoreType.DMA(shape)


def call(kernel, name, ident, outs, ins, scratch, args, flops=0):
    return pl.pallas_call(
        kernel,
        name=name,
        out_shape=outs,
        in_specs=ins,
        out_specs=tuple(in_vmem() for _ in outs),
        scratch_shapes=scratch,
        compiler_params=pltpu.CompilerParams(
            collective_id=ident, has_side_effects=True, vmem_limit_bytes=62 * 2**20
        ),
        cost_estimate=pl.CostEstimate(flops=flops, bytes_accessed=2**24, transcendentals=0),
    )(*args)


def per_device(
    inputs, ln1_gain, ln1_bias, w_query, w_key, w_value, w_out, ln2_gain, ln2_bias, w_up, w_down,
    teacher, valid_mask,
):
    rows, width = inputs.shape
    local = w_query.shape[1]
    heads = local // HEAD_DIM
    hidden_units = w_up.shape[1]
    dp_size = lax.axis_size("dp")
    single = dp_size == SEQ_DEV
    share = width // SEQ_DEV
    out = jax.ShapeDtypeStruct
    row = lambda vector: vector.reshape(1, width)
    length = rows * SEQ_DEV
    part_rows = rows // CHUNKS

    n_one, kv_all, q_all, o_t, log_sum, ctx, count, wo_in = call(
        forward_kernel, "forward", 1,
        (
            out((rows, width), bf16),
            out((2, length, HEAD_DIM), bf16),
            out((4, rows, HEAD_DIM), bf16),
            out((4, HEAD_DIM, rows), f32),
            out((4, 1, rows), f32),
            out((heads, rows, HEAD_DIM), bf16),
            out((8, 128), f32),
            out((local, width), bf16),
        ),
        [in_vmem()] * 8,
        [
            pltpu.VMEM((heads, 2, rows, HEAD_DIM), bf16),
            pltpu.VMEM((heads, rows, HEAD_DIM), bf16),
            pltpu.VMEM((4, rows, HEAD_DIM), bf16),
            pltpu.VMEM((4, 1, rows), f32),
            pltpu.VMEM((4, 1, rows), f32),
        ]
        + [dma(4)] * 12
        + [dma(2)]
        + summed_scratch((8, 128)),
        (
            inputs, row(ln1_gain), row(ln1_bias), w_query, w_key, w_value, w_out,
            valid_mask.reshape(1, rows),
        ),
    )
    if not single:
        count = jnp.full((8, 128), lax.psum(jnp.sum(valid_mask.astype(f32)), "dp"))
    output, d_hidden, do_all, grad_ffn, grad_out_t, vectors = call(
        functools.partial(middle_kernel, float(rows * dp_size)), "middle", 2,
        (
            out((rows, width), f32),
            out((rows, width), f32),
            out((4, rows, HEAD_DIM), bf16),
            out((4, width, hidden_units // 2), bf16),
            out((width, local), bf16),
            out((8, width), f32),
        ),
        [
            in_vmem(), in_hbm(), in_hbm(), in_hbm(), in_vmem(), in_vmem(), in_hbm(), in_hbm(),
            in_hbm(), in_vmem(), in_vmem(),
        ],
        [
            pltpu.VMEM((rows, width), f32),
            pltpu.VMEM((local, width), bf16),
            pltpu.VMEM((local, width), bf16),
            pltpu.VMEM((width, hidden_units), bf16),
            pltpu.VMEM((hidden_units, width), bf16),
            pltpu.VMEM((rows, width), f32),
            dma(6),
            pltpu.VMEM((heads, rows, HEAD_DIM), bf16),
            pltpu.VMEM((rows, width), f32),
            pltpu.VMEM((rows, 1), f32),
            pltpu.VMEM((rows, width), bf16),
            pltpu.VMEM((rows, hidden_units), bf16),
            pltpu.VMEM((rows, width), bf16),
            pltpu.VMEM((rows, hidden_units), bf16),
            pltpu.VMEM((rows, width), bf16),
            pltpu.VMEM((heads, rows, HEAD_DIM), bf16),
        ]
        + [pltpu.VMEM((CHUNKS, part_rows, width), bf16)] * 4
        + [dma(CHUNKS)] * 6
        + [dma(CHUNKS, 4)] * 2,
        (
            ctx, inputs, w_out, wo_in, row(ln2_gain), row(ln2_bias), w_up, w_down, teacher,
            valid_mask.astype(f32).reshape(rows, 1), count,
        ),
    )
    d_query, d_kv = call(
        backward_kernel, "backward", 3,
        (
            out((heads, rows, HEAD_DIM), bf16),
            out((heads, 2, rows, HEAD_DIM), bf16),
        ),
        [in_vmem()] * 5,
        [
            pltpu.VMEM((2, 4 * rows, HEAD_DIM), f32),
            pltpu.VMEM((4, HEAD_DIM, rows), f32),
            pltpu.VMEM((4, 1, rows), f32),
            pltpu.VMEM((2, 2, rows, HEAD_DIM), bf16),
            pltpu.VMEM((4, 2, 2, rows, HEAD_DIM), bf16),
            pltpu.VMEM((4, 2, rows, HEAD_DIM), bf16),
            pltpu.VMEM((4, 2, rows, HEAD_DIM), bf16),
            pltpu.VMEM((4, 2, rows, HEAD_DIM), bf16),
            pltpu.VMEM((4, rows, HEAD_DIM), bf16),
        ]
        + [dma(4)] * 8,
        (kv_all, q_all, o_t, log_sum, do_all),
    )
    split = (4, 2, 2, share)
    piece = hidden_units // 2
    extra = (4 * local) // piece
    pieces = 4 + extra
    input_grad, scattered, vector_sums = call(
        tail_kernel, "tail", 4,
        (
            out((rows, width), f32),
            out((pieces, share, piece), f32),
            out((8, width), f32),
        ),
        [in_vmem()] * 12,
        [
            pltpu.VMEM((extra,) + split + (piece,), bf16),
            pltpu.VMEM((pieces, 4, 2, share, piece), bf16),
            pltpu.VMEM((pieces, 4, 2, share, piece), bf16),
            pltpu.VMEM((pieces, 4, share, piece), bf16),
            pltpu.VMEM((pieces, 4, share, piece), bf16),
            pltpu.VMEM((pieces, 3, share, piece), bf16),
            pltpu.VMEM((CHUNKS, part_rows, width), bf16),
            pltpu.VMEM((CHUNKS, part_rows, width), bf16),
            pltpu.VMEM((3, rows, local), bf16),
        ]
        + [dma(CHUNKS)] * 2
        + [dma(pieces)] * 4
        + [dma(pieces, 3)] * 2
        + summed_scratch((8, width)),
        (
            d_query, d_kv, n_one, w_query, w_key, w_value, inputs, row(ln1_gain), d_hidden,
            vectors, grad_ffn.reshape((4,) + split + (piece,)),
            grad_out_t.reshape(split + (local,)),
        ),
    )
    index = lax.axis_index("dp")
    pos = lax.rem(index, SEQ_DEV)
    if not single:
        placed = lax.dynamic_update_slice(
            jnp.zeros((pieces, width, piece), f32), scattered, (0, pos * share, 0)
        )
        scattered = lax.psum_scatter(placed, "dp", scatter_dimension=1, tiled=True)
        vector_sums = lax.psum(jnp.where(pos == 0, vector_sums, 0.0), "dp")
        share = width // dp_size
        pos = index
    grad_up = jnp.concatenate([scattered[0], scattered[1]], axis=1)
    grad_down = jnp.concatenate([scattered[2].T, scattered[3].T], axis=0)
    grad_out = scattered[4][:, :local].T
    grad_query = scattered[4][:, local:]
    grad_key = scattered[5][:, :local]
    grad_value = scattered[5][:, local:]
    loss_value = jnp.sum(vector_sums[2]) / (2.0 * count[0, 0])
    cut = lambda k: lax.dynamic_slice(vector_sums[k], (pos * share,), (share,))
    return (
        output, loss_value, input_grad, cut(3), cut(4), grad_query, grad_key, grad_value, grad_out,
        cut(0), cut(1), grad_up, grad_down,
    )


def solution(mesh):
    return jax.shard_map(
        per_device,
        mesh=mesh,
        in_specs=(
            P("dp", None), P(), P(), P(None, "tensor"), P(None, "tensor"), P(None, "tensor"),
            P("tensor", None), P(), P(), P(None, "tensor"), P("tensor", None), P("dp", None),
            P("dp"),
        ),
        out_specs=(
            P("dp", None), P(), P("dp", None), P("dp"), P("dp"), P("dp", "tensor"),
            P("dp", "tensor"), P("dp", "tensor"), P("tensor", "dp"), P("dp"), P("dp"),
            P("dp", "tensor"), P("tensor", "dp"),
        ),
        check_vma=False,
    )
```

```python
import functools

import jax
import jax.numpy as jnp
from jax import lax
from jax.experimental import pallas as pl
from jax.experimental.pallas import tpu as pltpu
from jax.sharding import PartitionSpec as P

HEAD_DIM = 128
SEQ_DEV = 16
EPSILON = 1e-05
NEGATIVE = -1e30
LOG_SCALE = 1.4426950408889634 * HEAD_DIM ** (-0.5)
HEAD_SCALE = HEAD_DIM ** (-0.5)
CHUNKS = 4
STEPS = 4
f32 = jnp.float32
bf16 = jnp.bfloat16


def nn(a, b):
    return lax.dot_general(a, b, (((1,), (0,)), ((), ())), preferred_element_type=f32)


def nt(a, b):
    return lax.dot_general(a, b, (((1,), (1,)), ((), ())), preferred_element_type=f32)


def tn(a, b):
    return lax.dot_general(a, b, (((0,), (0,)), ((), ())), preferred_element_type=f32)


def remote(src, dst, send_sem, recv_sem, device):
    return pltpu.make_async_remote_copy(
        src_ref=src,
        dst_ref=dst,
        send_sem=send_sem,
        recv_sem=recv_sem,
        device_id=device,
        device_id_type=pl.DeviceIdType.MESH,
    )


class Place:
    def __init__(self):
        index = lax.axis_index("dp")
        self.pos = lax.rem(index, SEQ_DEV)
        self.base = index - self.pos
        self.slab = lax.div(self.pos, 4)
        self.seat = lax.rem(self.pos, 4)
        self.side = lax.axis_index("tensor")
        seat = self.seat
        self.core_seat = seat + 1 - 2 * lax.rem(seat, 2)
        self.x_seat = lax.rem(seat + 2, 4)
        self.far_seat = 3 - seat

    def dev(self, slab, seat):
        return {"dp": self.base + slab * 4 + seat, "tensor": self.side}

    def other_side(self):
        return {"dp": self.base + self.pos, "tensor": 1 - self.side}

    def turned(self, slab):
        even = lax.rem(slab, 2) == 0
        return jnp.where(even, self.seat, self.far_seat)

    def peers(self, same, far, near, side):
        found = []
        for step in range(1, 4):
            other = lax.rem(self.slab + step, 4)
            if same:
                found.append(self.dev(other, self.seat))
            if far:
                found.append(self.dev(other, self.far_seat))
        if far:
            found.append(self.dev(self.slab, self.far_seat))
        if near:
            found.append(self.dev(self.slab, self.core_seat))
            found.append(self.dev(self.slab, self.x_seat))
        if side:
            found.append(self.other_side())
        return found


def greet(peers):
    barrier = pltpu.get_barrier_semaphore()
    for peer in peers:
        pl.semaphore_signal(
            barrier, inc=1, device_id=peer, device_id_type=pl.DeviceIdType.MESH
        )
    return functools.partial(pl.semaphore_wait, barrier, len(peers))


def norm_stats(values):
    average = jnp.mean(values, axis=-1, keepdims=True)
    centred = values - average
    inverse = lax.rsqrt(jnp.mean(centred * centred, axis=-1, keepdims=True) + EPSILON)
    return centred * inverse, inverse


class Summed:
    def __init__(self, at, tile, core_in, x_buf, x_in, z_buf, z_in, send, recv):
        self.at, self.tile = at, tile
        self.core_in, self.x_buf, self.x_in = core_in, x_buf, x_in
        self.z_buf, self.z_in = z_buf, z_in
        self.send, self.recv = send, recv

    def hop(self, src, dst, k, device):
        return remote(src, dst, self.send.at[k], self.recv.at[k], device)

    def near(self):
        at = self.at
        return self.hop(self.tile, self.core_in, 0, at.dev(at.slab, at.core_seat))

    def wide(self):
        at = self.at
        return self.hop(self.x_buf, self.x_in, 1, at.dev(at.slab, at.x_seat))

    def far(self, step):
        at = self.at
        device = at.dev(lax.rem(at.slab + step, 4), at.seat)
        return self.hop(self.z_buf, self.z_in.at[at.slab], 1 + step, device)

    def one(self):
        self.near().start()

    def two(self):
        self.near().wait()
        self.x_buf[...] = self.tile[...] + self.core_in[...]
        self.wide().start()

    def three(self):
        self.wide().wait()
        total = self.x_buf[...] + self.x_in[...]
        self.z_buf[...] = total
        self.z_in[self.at.slab] = total
        for step in range(1, 4):
            self.far(step).start()

    def four(self):
        at = self.at
        for step in range(1, 4):
            self.far(step).wait_send()
            source = lax.rem(at.slab - step + 4, 4)
            slot = self.z_in.at[source]
            self.hop(slot, slot, 1 + step, at.dev(source, at.seat)).wait_recv()
        return (self.z_in[0] + self.z_in[1]) + (self.z_in[2] + self.z_in[3])


def summed_scratch(shape):
    return [
        pltpu.VMEM(shape, f32),
        pltpu.VMEM(shape, f32),
        pltpu.VMEM(shape, f32),
        pltpu.VMEM(shape, f32),
        pltpu.VMEM(shape, f32),
        pltpu.VMEM((4,) + shape, f32),
        pltpu.SemaphoreType.DMA((5,)),
        pltpu.SemaphoreType.DMA((5,)),
    ]


class Scatter:
    def __init__(self, at, rc, s1, rx, s2, ra, s3, rb, send, recv):
        self.at = at
        self.core = lax.rem(at.seat, 2)
        self.wide = lax.div(at.seat, 2)
        self.low = lax.rem(at.slab, 2)
        self.high = lax.div(at.slab, 2)
        self.rc, self.s1, self.rx, self.s2 = rc, s1, rx, s2
        self.ra, self.s3, self.rb = ra, s3, rb
        self.send, self.recv = send, recv

    def hop(self, stage, k, src, dst, device):
        return remote(src, dst, self.send.at[stage, k], self.recv.at[stage, k], device)

    def c_copy(self, k, source):
        at = self.at
        device = at.dev(at.slab, at.core_seat)
        return self.hop(0, k, source.at[:, :, 1 - self.core], self.rc.at[k], device)

    def x_copy(self, k):
        at = self.at
        device = at.dev(at.slab, at.x_seat)
        return self.hop(1, k, self.s1.at[k, :, 1 - self.wide], self.rx.at[k], device)

    def a_copy(self, k):
        at = self.at
        device = at.dev(at.slab + 1 - 2 * self.low, at.seat)
        return self.hop(2, k, self.s2.at[k, :, 1 - self.low], self.ra.at[k], device)

    def b_copy(self, k):
        at = self.at
        device = at.dev(lax.rem(at.slab + 2, 4), at.seat)
        return self.hop(3, k, self.s3.at[k, 1 - self.high], self.rb.at[k], device)

    def core_add(self, k, source):
        self.c_copy(k, source).wait_recv()

        def one(i, _):
            self.s1[k, i] = (
                source[i, :, self.core].astype(f32) + self.rc[k, i].astype(f32)
            ).astype(bf16)
            return 0

        lax.fori_loop(0, 4, one, 0)

    def x_add(self, k):
        self.x_copy(k).wait_recv()
        for i in range(4):
            self.s2[k, i // 2, i % 2] = (
                self.s1[k, i, self.wide].astype(f32) + self.rx[k, i].astype(f32)
            ).astype(bf16)

    def a_add(self, k):
        self.a_copy(k).wait_recv()
        for i in range(2):
            self.s3[k, i] = (
                self.s2[k, i, self.low].astype(f32) + self.ra[k, i].astype(f32)
            ).astype(bf16)

    def b_add(self, k):
        self.b_copy(k).wait_recv()
        return self.s3[k, self.high].astype(f32) + self.rb[k].astype(f32)


def attend_mask(size, rows, per, step, mine):
    key = lax.broadcasted_iota(jnp.int32, (size, 1), 0)
    key = lax.div(key, per) * rows + lax.rem(key, per) + step * per
    query = lax.broadcasted_iota(jnp.int32, (1, rows), 1) + mine * rows
    return key <= query


def forward_kernel(
    x_ref, gain_ref, bias_ref, wq_ref, wk_ref, wv_ref, wo_ref, mask_ref,
    none_ref, kv_ref, q_ref, ot_ref, ls_ref, ctx_ref, cnt_ref, wo_in_ref,
    kvs, qs, os, top, low,
    z_send, z_recv, q_send, q_recv, c_send, c_recv, x_send, x_recv, f_send, f_recv,
    o_send, o_recv, w_sem,
    tile, core_in, x_buf, x_in, z_buf, z_in, t_send, t_recv,
):
    at = Place()
    rows = x_ref.shape[0]
    per = rows // STEPS
    slab, seat = at.slab, at.seat
    even = lax.rem(slab, 2) == 0
    odd = jnp.logical_not(even)
    goal = at.turned(slab)
    ready = greet(at.peers(True, True, True, True))

    def order(k):
        down = jnp.where(3 - k > slab, 3 - k, 2 - k)
        up = jnp.where(k < slab, k, k + 1)
        return jnp.where(slab < 2, down, up)

    def q_copy(h):
        return remote(qs.at[h], q_ref.at[slab], q_send.at[h], q_recv.at[slab], at.dev(h, goal))

    def kv_copy(h, t):
        return remote(
            kvs.at[h, :, t], kv_ref.at[:, slab, seat, t], z_send.at[t, h], z_recv.at[t, slab],
            at.dev(h, seat),
        )

    def near_copy(t):
        part = kv_ref.at[:, :, seat, t]
        return remote(part, part, c_send.at[t], c_recv.at[t], at.dev(slab, at.core_seat))

    def wide_copy(t):
        part = kv_ref.at[:, :, seat, t]
        return remote(part, part, x_send.at[t], x_recv.at[t], at.dev(slab, at.x_seat))

    def pass_copy(t):
        part = kv_ref.at[:, :, at.x_seat, t]
        return remote(part, part, f_send.at[t], f_recv.at[t], at.dev(slab, at.core_seat))

    normed, _ = norm_stats(x_ref[...])
    n_one = (normed * gain_ref[...] + bias_ref[...]).astype(bf16)
    none_ref[...] = n_one
    query = nn(n_one, wq_ref[...]).astype(bf16)
    for h in range(4):
        qs[h] = query[:, h * HEAD_DIM : (h + 1) * HEAD_DIM]
    ready()
    for k in range(3):
        q_copy(order(k)).start()

    @pl.when(even)
    def _():
        q_ref[slab] = qs[slab]

    @pl.when(odd)
    def _():
        q_copy(slab).start()

    for j, w_ref in enumerate((wk_ref, wv_ref)):
        made = nn(none_ref[...], w_ref[...]).astype(bf16)
        for h in range(4):
            kvs[h, j] = made[:, h * HEAD_DIM : (h + 1) * HEAD_DIM].reshape(STEPS, per, HEAD_DIM)
    for t in range(STEPS):
        for k in range(3):
            kv_copy(order(k), t).start()
    kv_ref[:, slab, seat] = kvs[slab]
    w_copy = remote(wo_ref, wo_in_ref, w_sem.at[0], w_sem.at[1], at.other_side())
    w_copy.start()
    count = jnp.sum(mask_ref[...].astype(f32), axis=1, keepdims=True)
    tile[...] = jnp.broadcast_to(count, tile.shape)
    total = Summed(at, tile, core_in, x_buf, x_in, z_buf, z_in, t_send, t_recv)
    total.one()
    top[...] = jnp.full_like(top, NEGATIVE)
    low[...] = jnp.zeros_like(low)
    ot_ref[...] = jnp.zeros_like(ot_ref)

    def relay(t):
        for step in range(1, 4):
            source = lax.rem(slab + step, 4)
            part = kv_ref.at[:, source, seat, t]
            remote(
                part, part, z_send.at[t, source], z_recv.at[t, source], at.dev(source, seat)
            ).wait_recv()
        near_copy(t).start()
        wide_copy(t).start()

    def hand_on(t):
        part = kv_ref.at[:, :, at.x_seat, t]
        remote(part, part, x_send.at[t], x_recv.at[t], at.dev(slab, at.x_seat)).wait_recv()
        pass_copy(t).start()

    def arrive(t):
        device = at.dev(slab, at.core_seat)
        part = kv_ref.at[:, :, at.core_seat, t]
        remote(part, part, c_send.at[t], c_recv.at[t], device).wait_recv()
        part = kv_ref.at[:, :, at.far_seat, t]
        remote(part, part, f_send.at[t], f_recv.at[t], device).wait_recv()

    def unit(slot, keys, values, allowed):
        scores = nt(keys, q_ref[slot]) * LOG_SCALE
        if allowed is not None:
            scores = jnp.where(allowed, scores, NEGATIVE)
        before = top[slot]
        after = jnp.maximum(before, jnp.max(scores, axis=0, keepdims=True))
        prob = jnp.exp2(scores - after)
        shrink = jnp.exp2(before - after)
        low[slot] = low[slot] * shrink + jnp.sum(prob, axis=0, keepdims=True)
        top[slot] = after
        ot_ref[slot] = ot_ref[slot] * shrink + tn(values, prob.astype(bf16))

    def o_copy(slot):
        return remote(
            os.at[slot], ctx_ref.at[slab], o_send.at[slot], o_recv.at[slab],
            at.dev(slot, at.turned(slot)),
        )

    def slot_step(slot, t):
        if slot > 0:
            size = 4 * slot * per
            unit(
                slot,
                kv_ref[0, 0:slot, :, t].reshape(size, HEAD_DIM),
                kv_ref[1, 0:slot, :, t].reshape(size, HEAD_DIM),
                None,
            )
        mine = at.turned(slot)
        for blocks, chosen in ((2, mine < 2), (4, mine >= 2)):

            @pl.when(chosen)
            def _():
                size = blocks * per
                unit(
                    slot,
                    kv_ref[0, slot, 0:blocks, t].reshape(size, HEAD_DIM),
                    kv_ref[1, slot, 0:blocks, t].reshape(size, HEAD_DIM),
                    attend_mask(size, rows, per, t, mine),
                )

        @pl.when(t == STEPS - 1)
        def _():
            done = ot_ref[slot] / low[slot]
            ot_ref[slot] = done
            ls_ref[slot] = top[slot] + jnp.log2(low[slot])
            os[slot] = done.T.astype(bf16)
            home = jnp.logical_and(slab == slot, even)

            @pl.when(home)
            def _():
                ctx_ref[slab] = os[slot]

            @pl.when(jnp.logical_not(home))
            def _():
                o_copy(slot).start()

    for step in range(1, 4):
        source = lax.rem(slab + step, 4)
        part = q_ref.at[source]
        remote(
            part, part, q_send.at[source], q_recv.at[source], at.dev(source, seat)
        ).wait_recv()

    @pl.when(odd)
    def _():
        part = q_ref.at[slab]
        remote(part, part, q_send.at[slab], q_recv.at[slab], at.dev(slab, seat)).wait_recv()

    relay(0)
    total.two()
    relay(1)
    hand_on(0)

    def go(t, _):
        arrive(t)
        slot_step(3, t)

        @pl.when(t + 2 < STEPS)
        def _():
            relay(t + 2)

        @pl.when(t + 1 < STEPS)
        def _():
            hand_on(t + 1)

        @pl.when(t == 0)
        def _():
            total.three()

        slot_step(0, t)
        slot_step(2, t)
        slot_step(1, t)
        return 0

    lax.fori_loop(0, STEPS, go, 0)
    cnt_ref[...] = total.four()
    for k in range(3):
        q_copy(order(k)).wait_send()

    @pl.when(odd)
    def _():
        q_copy(slab).wait_send()

    def finish(t, _):
        for k in range(3):
            kv_copy(order(k), t).wait_send()
        near_copy(t).wait_send()
        wide_copy(t).wait_send()
        pass_copy(t).wait_send()
        return 0

    lax.fori_loop(0, STEPS, finish, 0)
    w_copy.wait()
    for k in range(4):
        home = jnp.logical_and(slab == k, even)

        @pl.when(jnp.logical_not(home))
        def _():
            o_copy(k).wait_send()
            part = ctx_ref.at[k]
            remote(part, part, o_send.at[k], o_recv.at[k], at.dev(k, seat)).wait_recv()


def heads_row(ref, rows_at):
    return jnp.concatenate([ref[h, rows_at, :] for h in range(4)], axis=1)


def middle_kernel(
    token_total,
    ctx_ref, x_hbm, wo_hbm, wo_in_hbm, gain_ref, bias_ref, wup_hbm, wdn_hbm, teach_hbm,
    mask_ref, cnt_ref,
    out_ref, dh_ref, do_ref, up_ref, dn_ref, go_ref, vec_ref,
    x_buf, wo, wo_in, wup, wdn, teach, load,
    ctx_in, normed_s, inv_s, n2s, acts, gfs, dpres, gas, dcs,
    fs, fr, bs, br,
    e_send, e_recv, f_send, f_recv, b_send, b_recv, d_send, d_recv,
    gt, rc, s1, rx, g_send, g_recv,
):
    at = Place()
    slab, seat = at.slab, at.seat
    rows = out_ref.shape[0]
    part_rows = rows // CHUNKS
    ready = greet(at.peers(True, True, True, True))
    loads = [
        pltpu.make_async_copy(src, dst, load.at[k])
        for k, (src, dst) in enumerate(
            (
                (wo_hbm, wo), (wo_in_hbm, wo_in), (x_hbm, x_buf), (wup_hbm, wup),
                (wdn_hbm, wdn), (teach_hbm, teach),
            )
        )
    ]
    for copy in loads:
        copy.start()
    ready()

    def e_copy(c):
        part = pl.ds(pl.multiple_of(c * part_rows, part_rows), part_rows)
        return remote(
            ctx_ref.at[:, part, :], ctx_in.at[:, part, :], e_send.at[c], e_recv.at[c],
            at.other_side(),
        )

    def f_copy(c):
        return remote(fs.at[c], fr.at[c], f_send.at[c], f_recv.at[c], at.other_side())

    def b_copy(c):
        return remote(bs.at[c], br.at[c], b_send.at[c], b_recv.at[c], at.other_side())

    for c in range(CHUNKS):
        e_copy(c).start()
    for k in range(3):
        loads[k].wait()

    def forward(c, _):
        part = pl.ds(pl.multiple_of(c * part_rows, part_rows), part_rows)
        e_copy(c).wait()
        hidden = x_buf[part, :] + (
            nn(heads_row(ctx_ref, part), wo[...]) + nn(heads_row(ctx_in, part), wo_in[...])
        )
        out_ref[part, :] = hidden
        normed, inverse = norm_stats(hidden)
        normed_s[part, :] = normed
        inv_s[part, :] = inverse
        n_two = (normed * gain_ref[...] + bias_ref[...]).astype(bf16)
        n2s[part, :] = n_two

        @pl.when(c == 0)
        def _():
            loads[3].wait()
            loads[4].wait()

        active = jnp.maximum(nn(n_two, wup[...]), 0.0).astype(bf16)
        acts[part, :] = active
        fs[c] = nn(active, wdn[...]).astype(bf16)
        f_copy(c).start()
        return 0

    lax.fori_loop(0, CHUNKS, forward, 0)
    loads[5].wait()
    scale = token_total / cnt_ref[0:1, 0:1]
    vec_ref[...] = jnp.zeros_like(vec_ref)

    def back_one(c, _):
        part = pl.ds(pl.multiple_of(c * part_rows, part_rows), part_rows)
        f_copy(c).wait()
        output = out_ref[part, :] + (fs[c].astype(f32) + fr[c].astype(f32))
        out_ref[part, :] = output
        misfit = output - teach[part, :]
        held = misfit * mask_ref[part, :]
        vec_ref[2:3, :] += jnp.sum(held * misfit, axis=0, keepdims=True)
        d_output = scale * held
        dh_ref[part, :] = d_output
        g_ffn = d_output.astype(bf16)
        gfs[part, :] = g_ffn
        d_active = nt(g_ffn, wdn[...])
        d_pre = jnp.where(acts[part, :] > 0, d_active, 0.0).astype(bf16)
        dpres[part, :] = d_pre
        bs[c] = nt(d_pre, wup[...]).astype(bf16)
        b_copy(c).start()
        return 0

    lax.fori_loop(0, CHUNKS, back_one, 0)
    scatter = Scatter(at, rc, s1, rx, dn_ref, None, None, None, g_send, g_recv)
    split = gt.shape[1:5]
    half = gt.shape[5] // 2
    for k in range(4):
        slot = gt.at[k % 2]
        if k >= 2:
            scatter.c_copy(k - 2, slot).wait_send()
        for j in range(2):
            cols = slice((k % 2) * 2 * half + j * half, (k % 2) * 2 * half + (j + 1) * half)
            if k < 2:
                made = tn(gfs[...], acts[:, cols])
            else:
                made = tn(n2s[...], dpres[:, cols])
            gt[k % 2, :, :, :, :, j * half : (j + 1) * half] = made.astype(bf16).reshape(
                split + (half,)
            )
        scatter.c_copy(k, slot).start()
        if k >= 1:
            scatter.core_add(k - 1, gt.at[(k - 1) % 2])
            if k - 1 < 2:
                scatter.x_copy(k - 1).start()
    scatter.core_add(3, gt.at[1])
    scatter.c_copy(2, gt.at[0]).wait_send()
    scatter.c_copy(3, gt.at[1]).wait_send()
    for k in range(2):
        up_ref[k] = s1[2 + k]

    def d_copy(c, h):
        part = pl.ds(pl.multiple_of(c * part_rows, part_rows), part_rows)
        return remote(
            dcs.at[h, part, :], do_ref.at[slab, part, :], d_send.at[c, h], d_recv.at[c, slab],
            at.dev(h, at.turned(slab)),
        )

    even = lax.rem(slab, 2) == 0

    def back_two(c, _):
        part = pl.ds(pl.multiple_of(c * part_rows, part_rows), part_rows)
        b_copy(c).wait()
        d_two = bs[c].astype(f32) + br[c].astype(f32)
        normed = normed_s[part, :]
        scaled = d_two * gain_ref[...]
        first = jnp.mean(scaled, axis=-1, keepdims=True)
        second = jnp.mean(scaled * normed, axis=-1, keepdims=True)
        d_hidden = dh_ref[part, :] + inv_s[part, :] * (scaled - first - normed * second)
        vec_ref[0:1, :] += jnp.sum(d_two * normed, axis=0, keepdims=True)
        vec_ref[1:2, :] += jnp.sum(d_two, axis=0, keepdims=True)
        dh_ref[part, :] = d_hidden
        g_attn = d_hidden.astype(bf16)
        gas[part, :] = g_attn
        d_context = nt(g_attn, wo[...]).astype(bf16)
        for h in range(4):
            dcs[h, part, :] = d_context[:, h * HEAD_DIM : (h + 1) * HEAD_DIM]
            home = jnp.logical_and(slab == h, even)

            @pl.when(home)
            def _():
                do_ref[slab, part, :] = dcs[h, part, :]

            @pl.when(jnp.logical_not(home))
            def _():
                d_copy(c, h).start()

        return 0

    lax.fori_loop(0, CHUNKS, back_two, 0)
    go_ref[...] = tn(gas[...], heads_row(ctx_ref, slice(None))).astype(bf16)
    for k in range(2):
        scatter.x_add(k)
        scatter.x_copy(k).wait_send()

    def finish(c, _):
        part = pl.ds(pl.multiple_of(c * part_rows, part_rows), part_rows)
        for h in range(4):
            home = jnp.logical_and(slab == h, even)

            @pl.when(jnp.logical_not(home))
            def _():
                d_copy(c, h).wait_send()
                slot = do_ref.at[h, part, :]
                remote(
                    slot, slot, d_send.at[c, h], d_recv.at[c, h], at.dev(h, seat)
                ).wait_recv()

        return 0

    lax.fori_loop(0, CHUNKS, finish, 0)


def backward_kernel(
    kv_ref, q_ref, ot_ref, ls_ref, do_ref, up_ref, dn_ref,
    dq_ref, dkv_ref, gd_ref, s2_ref,
    grads, acc, delta, near_out, near_in, wide_out, wide_in, home_out, dqs, kept,
    n_send, n_recv, w_send, w_recv, h_send, h_recv, d_send, d_recv,
    rx, ra, s3, rb, up_send, up_recv, dn_send, dn_recv,
):
    at = Place()
    slab, seat = at.slab, at.seat
    core, wide = lax.rem(seat, 2), lax.div(seat, 2)
    rows = q_ref.shape[1]
    per = rows // STEPS
    even = lax.rem(slab, 2) == 0
    ready = greet(at.peers(True, True, True, False))
    up = Scatter(at, None, up_ref, rx, s2_ref, None, None, None, up_send, up_recv)
    down = Scatter(at, None, None, None, dn_ref, ra, s3, rb, dn_send, dn_recv)
    acc[...] = jnp.zeros_like(acc)
    for slot in range(4):
        delta[slot] = jnp.sum(do_ref[slot].astype(f32).T * ot_ref[slot], axis=0, keepdims=True)
    ready()
    for k in range(2):
        down.a_copy(k).start()
        up.x_copy(k).start()

    def unit(slot, t, buf, first, slabs, blocks, allowed):
        size = slabs * blocks * per
        pick = (slice(first, first + slabs), slice(0, blocks))
        keys = kv_ref[(0,) + pick + (t,)].reshape(size, HEAD_DIM)
        values = kv_ref[(1,) + pick + (t,)].reshape(size, HEAD_DIM)
        query = q_ref[slot]
        d_out = do_ref[slot]
        scores = nt(keys, query) * LOG_SCALE - ls_ref[slot]
        if allowed is not None:
            scores = jnp.where(allowed, scores, NEGATIVE)
        prob = jnp.exp2(scores)
        d_probs = nt(values, d_out)
        d_scores = (prob * (d_probs - delta[slot])).astype(bf16)
        shape = (slabs, blocks, per, HEAD_DIM)
        grads[(buf, 1) + pick] += nn(prob.astype(bf16), d_out).reshape(shape)
        grads[(buf, 0) + pick] += nn(d_scores, query).reshape(shape)
        acc[slot] += tn(keys, d_scores)

    def d_copy(slot):
        return remote(
            dqs.at[slot], dq_ref.at[slab], d_send.at[slot], d_recv.at[slab],
            at.dev(slot, at.turned(slot)),
        )

    def slot_step(slot, t, buf):
        if slot > 0:
            unit(slot, t, buf, 0, slot, 4, None)
        mine = at.turned(slot)
        for blocks, chosen in ((2, mine < 2), (4, mine >= 2)):

            @pl.when(chosen)
            def _():
                allowed = attend_mask(blocks * per, rows, per, t, mine)
                unit(slot, t, buf, slot, 1, blocks, allowed)

        @pl.when(t == STEPS - 1)
        def _():
            dqs[slot] = (acc[slot] * HEAD_SCALE).T.astype(bf16)
            home = jnp.logical_and(slab == slot, even)

            @pl.when(home)
            def _():
                dq_ref[slab] = dqs[slot]

            @pl.when(jnp.logical_not(home))
            def _():
                d_copy(slot).start()

    def part(buf, x, c):
        return grads[buf, :, :, 2 * x + c]

    def near_copy(t):
        return remote(
            near_out.at[t], near_in.at[t], n_send.at[t], n_recv.at[t], at.dev(slab, at.core_seat)
        )

    def wide_copy(t):
        return remote(
            wide_out.at[t], wide_in.at[t], w_send.at[t], w_recv.at[t], at.dev(slab, at.x_seat)
        )

    def home_copy(t, k):
        return remote(
            home_out.at[t, :, k], dkv_ref.at[slab, :, t], h_send.at[t, k], h_recv.at[t, slab],
            at.dev(k, seat),
        )

    def near_stage(t, buf):
        near_copy(t).wait_recv()
        wide_out[t] = (part(buf, 1 - wide, core) + near_in[t, 1 - wide].astype(f32)).astype(bf16)
        wide_copy(t).start()
        kept[...] = part(buf, wide, core) + near_in[t, wide].astype(f32)

    def wide_stage(t):
        wide_copy(t).wait_recv()
        home_out[t, 0] = ((kept[0] + wide_in[t, 0].astype(f32)) * HEAD_SCALE).astype(bf16)
        home_out[t, 1] = (kept[1] + wide_in[t, 1].astype(f32)).astype(bf16)
        dkv_ref[slab, :, t] = home_out[t, :, slab]
        for step in range(1, 4):
            home_copy(t, lax.rem(slab + step, 4)).start()

    def go(t, _):
        buf = lax.rem(t, 2)
        grads[buf] = jnp.zeros_like(grads[buf])
        slot_step(3, t, buf)

        @pl.when(t > 0)
        def _():
            near_stage(t - 1, 1 - buf)

        slot_step(0, t, buf)
        slot_step(2, t, buf)

        @pl.when(t > 0)
        def _():
            wide_stage(t - 1)

        slot_step(1, t, buf)
        for x in range(2):
            near_out[t, x] = part(buf, x, 1 - core).astype(bf16)
        near_copy(t).start()
        for k in range(2):

            @pl.when(t == k + 1)
            def _():
                down.a_add(k)
                down.b_copy(k).start()

        return 0

    lax.fori_loop(0, STEPS, go, 0)
    near_stage(STEPS - 1, (STEPS - 1) % 2)
    half = gd_ref.shape[0] // 2
    for k in range(2):
        up.x_add(k)
        gd_ref[k * half : (k + 1) * half, :] = down.b_add(k).T
    wide_stage(STEPS - 1)
    for k in range(2):
        down.a_copy(k).wait_send()
        down.b_copy(k).wait_send()
        up.x_copy(k).wait_send()

    def finish(t, _):
        near_copy(t).wait_send()
        wide_copy(t).wait_send()
        for step in range(1, 4):
            k = lax.rem(slab + step, 4)
            home_copy(t, k).wait_send()
            slot = dkv_ref.at[k, :, t]
            remote(slot, slot, h_send.at[t, k], h_recv.at[t, k], at.dev(k, seat)).wait_recv()
        return 0

    lax.fori_loop(0, STEPS, finish, 0)
    for k in range(4):
        home = jnp.logical_and(slab == k, even)

        @pl.when(jnp.logical_not(home))
        def _():
            d_copy(k).wait_send()
            slot = dq_ref.at[k]
            remote(slot, slot, d_send.at[k], d_recv.at[k], at.dev(k, seat)).wait_recv()


def tail_kernel(
    dq_ref, dkv_ref, n_one_ref, wq_ref, wk_ref, wv_ref, x_ref, gain_ref, dh_ref, vec_ref, go_ref,
    cnt_ref, up_ref,
    ig_ref, gq_ref, gk_ref, gv_ref, go_out, gu_ref, g1_ref, b1_ref, g2_ref, b2_ref, loss_ref,
    vsum_ref,
    ga, rc, s1, rx, s2, ra, s3, rb, g_send, g_recv, ua, u3, ub, u_send, u_recv, bs, br, dcat,
    b_send, b_recv,
    tile, core_in, x_buf, x_in, z_buf, z_in, t_send, t_recv,
):
    at = Place()
    rows = x_ref.shape[0]
    part_rows = rows // CHUNKS
    ready = greet(at.peers(True, False, True, True))
    scatter = Scatter(at, rc, s1, rx, s2, ra, s3, rb, g_send, g_recv)
    up = Scatter(at, None, None, None, up_ref, ua, u3, ub, u_send, u_recv)

    def b_copy(c):
        return remote(bs.at[c], br.at[c], b_send.at[c], b_recv.at[c], at.other_side())

    dcat[0] = heads_row(dq_ref, slice(None))
    for j in range(2):
        dcat[1 + j] = jnp.concatenate([dkv_ref[h, j] for h in range(4)], axis=1)
    ready()
    scatter.c_copy(0, go_ref).start()
    for k in range(2):
        up.a_copy(k).start()

    def side_part(c, _):
        part = pl.ds(pl.multiple_of(c * part_rows, part_rows), part_rows)
        bs[c] = (
            nt(dcat[0, part, :], wq_ref[...])
            + nt(dcat[1, part, :], wk_ref[...])
            + nt(dcat[2, part, :], wv_ref[...])
        ).astype(bf16)
        b_copy(c).start()
        return 0

    lax.fori_loop(0, CHUNKS, side_part, 0)
    scatter.core_add(0, go_ref)
    scatter.x_copy(0).start()
    for j in range(3):
        ga[j] = tn(n_one_ref[...], dcat[j]).astype(bf16).reshape(ga.shape[1:])
        scatter.c_copy(j + 1, ga.at[j]).start()
        if j > 0:
            scatter.core_add(j, ga.at[j - 1])
            scatter.x_copy(j).start()
    scatter.core_add(3, ga.at[2])
    scatter.x_copy(3).start()
    for k in range(2):
        up.a_add(k)
        up.b_copy(k).start()
    tile[...] = vec_ref[...]
    tile[3:5, :] = jnp.zeros_like(tile[3:5, :])
    scatter.x_add(0)
    scatter.a_copy(0).start()

    def side_sum(c, _):
        part = pl.ds(pl.multiple_of(c * part_rows, part_rows), part_rows)
        b_copy(c).wait()
        d_one = bs[c].astype(f32) + br[c].astype(f32)
        normed, inverse = norm_stats(x_ref[part, :])
        scaled = d_one * gain_ref[...]
        first = jnp.mean(scaled, axis=-1, keepdims=True)
        second = jnp.mean(scaled * normed, axis=-1, keepdims=True)
        ig_ref[part, :] = dh_ref[part, :] + inverse * (scaled - first - normed * second)
        tile[3:4, :] += jnp.sum(d_one * normed, axis=0, keepdims=True)
        tile[4:5, :] += jnp.sum(d_one, axis=0, keepdims=True)
        for k in range(1, 4):

            @pl.when(c == k)
            def _():
                scatter.x_add(k)
                scatter.a_copy(k).start()
                scatter.a_add(k - 1)
                scatter.b_copy(k - 1).start()

        return 0

    lax.fori_loop(0, CHUNKS, side_sum, 0)
    total = Summed(at, tile, core_in, x_buf, x_in, z_buf, z_in, t_send, t_recv)
    total.one()
    half = gu_ref.shape[1] // 2
    for k in range(2):
        gu_ref[:, k * half : (k + 1) * half] = up.b_add(k)
    total.two()
    scatter.a_add(3)
    scatter.b_copy(3).start()
    go_out[...] = scatter.b_add(0).T
    total.three()
    gq_ref[...] = scatter.b_add(1)
    gk_ref[...] = scatter.b_add(2)
    gv_ref[...] = scatter.b_add(3)
    vsum_ref[...] = total.four()
    share = gq_ref.shape[0]
    for k in range(SEQ_DEV):

        @pl.when(at.pos == k)
        def _():
            for line, ref in ((3, g1_ref), (4, b1_ref), (0, g2_ref), (1, b2_ref)):
                ref[...] = vsum_ref[line : line + 1, k * share : (k + 1) * share]

    loss_ref[...] = jnp.sum(vsum_ref[2:3, :], axis=1, keepdims=True) / (2.0 * cnt_ref[0:1, 0:1])
    for k in range(4):
        scatter.c_copy(k, go_ref if k == 0 else ga.at[k - 1]).wait_send()
        scatter.x_copy(k).wait_send()
        scatter.a_copy(k).wait_send()
        scatter.b_copy(k).wait_send()
    for k in range(2):
        up.a_copy(k).wait_send()
        up.b_copy(k).wait_send()


def in_vmem():
    return pl.BlockSpec(memory_space=pltpu.VMEM)


def in_hbm():
    return pl.BlockSpec(memory_space=pl.ANY)


def dma(*shape):
    return pltpu.SemaphoreType.DMA(shape)


def call(kernel, name, ident, outs, ins, scratch, args, flops=0):
    return pl.pallas_call(
        kernel,
        name=name,
        out_shape=outs,
        in_specs=ins,
        out_specs=tuple(in_vmem() for _ in outs),
        scratch_shapes=scratch,
        compiler_params=pltpu.CompilerParams(
            collective_id=ident, has_side_effects=True, vmem_limit_bytes=62 * 2**20
        ),
        cost_estimate=pl.CostEstimate(flops=flops, bytes_accessed=2**24, transcendentals=0),
    )(*args)


def per_device(
    inputs, ln1_gain, ln1_bias, w_query, w_key, w_value, w_out, ln2_gain, ln2_bias, w_up, w_down,
    teacher, valid_mask,
):
    rows, width = inputs.shape
    local = w_query.shape[1]
    heads = local // HEAD_DIM
    hidden_units = w_up.shape[1]
    dp_size = lax.axis_size("dp")
    single = dp_size == SEQ_DEV
    share = width // SEQ_DEV
    out = jax.ShapeDtypeStruct
    row = lambda vector: vector.reshape(1, width)
    step_rows = rows // STEPS
    part_rows = rows // CHUNKS

    n_one, kv_all, q_all, o_t, log_sum, ctx, count, wo_in = call(
        forward_kernel, "forward", 1,
        (
            out((rows, width), bf16),
            out((2, 4, 4, STEPS, step_rows, HEAD_DIM), bf16),
            out((4, rows, HEAD_DIM), bf16),
            out((4, HEAD_DIM, rows), f32),
            out((4, 1, rows), f32),
            out((heads, rows, HEAD_DIM), bf16),
            out((8, 128), f32),
            out((local, width), bf16),
        ),
        [in_vmem()] * 8,
        [
            pltpu.VMEM((heads, 2, STEPS, step_rows, HEAD_DIM), bf16),
            pltpu.VMEM((heads, rows, HEAD_DIM), bf16),
            pltpu.VMEM((4, rows, HEAD_DIM), bf16),
            pltpu.VMEM((4, 1, rows), f32),
            pltpu.VMEM((4, 1, rows), f32),
            dma(STEPS, 4), dma(STEPS, 4), dma(4), dma(4),
        ]
        + [dma(STEPS)] * 6
        + [dma(4)] * 2
        + [dma(2)]
        + summed_scratch((8, 128)),
        (
            inputs, row(ln1_gain), row(ln1_bias), w_query, w_key, w_value, w_out,
            valid_mask.reshape(1, rows),
        ),
    )
    if not single:
        count = jnp.full((8, 128), lax.psum(jnp.sum(valid_mask.astype(f32)), "dp"))
    share = width // SEQ_DEV
    split = (4, 2, 2, share)
    piece = hidden_units // 2
    output, d_hidden, do_all, up_part, down_part, grad_out_t, vectors = call(
        functools.partial(middle_kernel, float(rows * dp_size)), "middle", 2,
        (
            out((rows, width), f32),
            out((rows, width), f32),
            out((4, rows, HEAD_DIM), bf16),
            out((2, 4, 2, share, piece), bf16),
            out((2, 2, 2, share, piece), bf16),
            out((width, local), bf16),
            out((8, width), f32),
        ),
        [
            in_vmem(), in_hbm(), in_hbm(), in_hbm(), in_vmem(), in_vmem(), in_hbm(), in_hbm(),
            in_hbm(), in_vmem(), in_vmem(),
        ],
        [
            pltpu.VMEM((rows, width), f32),
            pltpu.VMEM((local, width), bf16),
            pltpu.VMEM((local, width), bf16),
            pltpu.VMEM((width, hidden_units), bf16),
            pltpu.VMEM((hidden_units, width), bf16),
            pltpu.VMEM((rows, width), f32),
            dma(6),
            pltpu.VMEM((heads, rows, HEAD_DIM), bf16),
            pltpu.VMEM((rows, width), f32),
            pltpu.VMEM((rows, 1), f32),
            pltpu.VMEM((rows, width), bf16),
            pltpu.VMEM((rows, hidden_units), bf16),
            pltpu.VMEM((rows, width), bf16),
            pltpu.VMEM((rows, hidden_units), bf16),
            pltpu.VMEM((rows, width), bf16),
            pltpu.VMEM((heads, rows, HEAD_DIM), bf16),
        ]
        + [pltpu.VMEM((CHUNKS, part_rows, width), bf16)] * 4
        + [dma(CHUNKS)] * 6
        + [dma(CHUNKS, 4)] * 2
        + [
            pltpu.VMEM((2,) + split + (piece,), bf16),
            pltpu.VMEM((4, 4, 2, share, piece), bf16),
            pltpu.VMEM((4, 4, 2, share, piece), bf16),
            pltpu.VMEM((2, 4, share, piece), bf16),
            dma(2, 4), dma(2, 4),
        ],
        (
            ctx, inputs, w_out, wo_in, row(ln2_gain), row(ln2_bias), w_up, w_down, teacher,
            valid_mask.astype(f32).reshape(rows, 1), count,
        ),
    )
    d_query, d_kv, grad_down, up_part = call(
        backward_kernel, "backward", 3,
        (
            out((heads, rows, HEAD_DIM), bf16),
            out((heads, 2, STEPS, step_rows, HEAD_DIM), bf16),
            out((hidden_units, share), f32),
            out((2, 2, 2, share, piece), bf16),
        ),
        [in_vmem()] * 7,
        [
            pltpu.VMEM((2, 2, 4, 4, step_rows, HEAD_DIM), f32),
            pltpu.VMEM((4, HEAD_DIM, rows), f32),
            pltpu.VMEM((4, 1, rows), f32),
            pltpu.VMEM((STEPS, 2, 2, 4, step_rows, HEAD_DIM), bf16),
            pltpu.VMEM((STEPS, 2, 2, 4, step_rows, HEAD_DIM), bf16),
            pltpu.VMEM((STEPS, 2, 4, step_rows, HEAD_DIM), bf16),
            pltpu.VMEM((STEPS, 2, 4, step_rows, HEAD_DIM), bf16),
            pltpu.VMEM((STEPS, 2, 4, step_rows, HEAD_DIM), bf16),
            pltpu.VMEM((4, rows, HEAD_DIM), bf16),
            pltpu.VMEM((2, 4, step_rows, HEAD_DIM), f32),
            dma(STEPS), dma(STEPS), dma(STEPS), dma(STEPS), dma(STEPS, 4), dma(STEPS, 4),
            dma(4), dma(4),
            pltpu.VMEM((2, 4, share, piece), bf16),
            pltpu.VMEM((2, 2, share, piece), bf16),
            pltpu.VMEM((2, 2, share, piece), bf16),
            pltpu.VMEM((2, share, piece), bf16),
            dma(4, 2), dma(4, 2), dma(4, 2), dma(4, 2),
        ],
        (kv_all, q_all, o_t, log_sum, do_all, up_part, down_part),
    )
    (
        input_grad, grad_query, grad_key, grad_value, grad_out, grad_up, gain_one, bias_one,
        gain_two, bias_two, loss, sums,
    ) = call(
        tail_kernel, "tail", 4,
        (out((rows, width), f32),)
        + (out((share, local), f32),) * 3
        + (out((local, share), f32), out((share, hidden_units), f32))
        + (out((1, share), f32),) * 4
        + (out((1, 1), f32), out((8, width), f32)),
        [in_vmem()] * 13,
        [
            pltpu.VMEM((3,) + split + (local,), bf16),
            pltpu.VMEM((4, 4, 2, share, local), bf16),
            pltpu.VMEM((4, 4, 2, share, local), bf16),
            pltpu.VMEM((4, 4, share, local), bf16),
            pltpu.VMEM((4, 2, 2, share, local), bf16),
            pltpu.VMEM((4, 2, share, local), bf16),
            pltpu.VMEM((4, 2, share, local), bf16),
            pltpu.VMEM((4, share, local), bf16),
            dma(4, 4), dma(4, 4),
            pltpu.VMEM((2, 2, share, piece), bf16),
            pltpu.VMEM((2, 2, share, piece), bf16),
            pltpu.VMEM((2, share, piece), bf16),
            dma(4, 2), dma(4, 2),
            pltpu.VMEM((CHUNKS, part_rows, width), bf16),
            pltpu.VMEM((CHUNKS, part_rows, width), bf16),
            pltpu.VMEM((3, rows, local), bf16),
            dma(CHUNKS), dma(CHUNKS),
        ]
        + summed_scratch((8, width)),
        (
            d_query, d_kv.reshape(heads, 2, rows, HEAD_DIM), n_one, w_query, w_key, w_value,
            inputs, row(ln1_gain), d_hidden, vectors, grad_out_t.reshape(split + (local,)), count,
            up_part,
        ),
    )
    small = [gain_one, bias_one, gain_two, bias_two]
    small = [vector.reshape(share) for vector in small]
    loss_value = loss.reshape(())
    if not single:
        index = lax.axis_index("dp")
        first = lax.rem(index, SEQ_DEV) * share

        def spread(part, axis):
            shape = list(part.shape)
            shape[axis] = width
            at = [0, 0]
            at[axis] = first
            placed = lax.dynamic_update_slice(jnp.zeros(shape, f32), part, tuple(at))
            return lax.psum_scatter(placed, "dp", scatter_dimension=axis, tiled=True)

        grad_query, grad_key, grad_value, grad_up = (
            spread(part, 0) for part in (grad_query, grad_key, grad_value, grad_up)
        )
        grad_out, grad_down = spread(grad_out, 1), spread(grad_down, 1)
        sums = lax.psum(jnp.where(first == 0, sums, 0.0), "dp")
        length = width // dp_size
        small = [lax.dynamic_slice(sums[k], (index * length,), (length,)) for k in (3, 4, 0, 1)]
        loss_value = jnp.sum(sums[2]) / (2.0 * count[0, 0])
    return (
        output, loss_value, input_grad, small[0], small[1], grad_query, grad_key, grad_value,
        grad_out, small[2], small[3], grad_up, grad_down,
    )


def solution(mesh):
    return jax.shard_map(
        per_device,
        mesh=mesh,
        in_specs=(
            P("dp", None), P(), P(), P(None, "tensor"), P(None, "tensor"), P(None, "tensor"),
            P("tensor", None), P(), P(), P(None, "tensor"), P("tensor", None), P("dp", None),
            P("dp"),
        ),
        out_specs=(
            P("dp", None), P(), P("dp", None), P("dp"), P("dp"), P("dp", "tensor"),
            P("dp", "tensor"), P("dp", "tensor"), P("tensor", "dp"), P("dp"), P("dp"),
            P("dp", "tensor"), P("tensor", "dp"),
        ),
        check_vma=False,
    )
```

```python
import functools

import jax
import jax.numpy as jnp
from jax import lax
from jax.experimental import pallas as pl
from jax.experimental.pallas import tpu as pltpu
from jax.sharding import PartitionSpec as P

HEAD_DIM = 128
SEQ_DEV = 16
EPSILON = 1e-05
NEGATIVE = -1e30
LOG_SCALE = 1.4426950408889634 * HEAD_DIM ** (-0.5)
HEAD_SCALE = HEAD_DIM ** (-0.5)
CHUNKS = 4
STEPS = 4
FSTEPS = 4
f32 = jnp.float32
bf16 = jnp.bfloat16


def nn(a, b):
    return lax.dot_general(a, b, (((1,), (0,)), ((), ())), preferred_element_type=f32)


def nt(a, b):
    return lax.dot_general(a, b, (((1,), (1,)), ((), ())), preferred_element_type=f32)


def tn(a, b):
    return lax.dot_general(a, b, (((0,), (0,)), ((), ())), preferred_element_type=f32)


def remote(src, dst, send_sem, recv_sem, device):
    return pltpu.make_async_remote_copy(
        src_ref=src,
        dst_ref=dst,
        send_sem=send_sem,
        recv_sem=recv_sem,
        device_id=device,
        device_id_type=pl.DeviceIdType.MESH,
    )


class Place:
    def __init__(self):
        index = lax.axis_index("dp")
        self.pos = lax.rem(index, SEQ_DEV)
        self.base = index - self.pos
        self.slab = lax.div(self.pos, 4)
        self.seat = lax.rem(self.pos, 4)
        self.side = lax.axis_index("tensor")
        seat = self.seat
        self.core_seat = seat + 1 - 2 * lax.rem(seat, 2)
        self.x_seat = lax.rem(seat + 2, 4)
        self.far_seat = 3 - seat

    def dev(self, slab, seat):
        return {"dp": self.base + slab * 4 + seat, "tensor": self.side}

    def other_side(self):
        return {"dp": self.base + self.pos, "tensor": 1 - self.side}

    def turned(self, slab):
        even = lax.rem(slab, 2) == 0
        return jnp.where(even, self.seat, self.far_seat)

    def peers(self, same, far, near, side):
        found = []
        for step in range(1, 4):
            other = lax.rem(self.slab + step, 4)
            if same:
                found.append(self.dev(other, self.seat))
            if far:
                found.append(self.dev(other, self.far_seat))
        if far:
            found.append(self.dev(self.slab, self.far_seat))
        if near:
            found.append(self.dev(self.slab, self.core_seat))
            found.append(self.dev(self.slab, self.x_seat))
        if side:
            found.append(self.other_side())
        return found


def greet(peers):
    barrier = pltpu.get_barrier_semaphore()
    for peer in peers:
        pl.semaphore_signal(
            barrier, inc=1, device_id=peer, device_id_type=pl.DeviceIdType.MESH
        )
    return functools.partial(pl.semaphore_wait, barrier, len(peers))


def norm_stats(values):
    average = jnp.mean(values, axis=-1, keepdims=True)
    centred = values - average
    inverse = lax.rsqrt(jnp.mean(centred * centred, axis=-1, keepdims=True) + EPSILON)
    return centred * inverse, inverse


class Summed:
    def __init__(self, at, tile, core_in, x_buf, x_in, z_buf, z_in, send, recv):
        self.at, self.tile = at, tile
        self.core_in, self.x_buf, self.x_in = core_in, x_buf, x_in
        self.z_buf, self.z_in = z_buf, z_in
        self.send, self.recv = send, recv

    def hop(self, src, dst, k, device):
        return remote(src, dst, self.send.at[k], self.recv.at[k], device)

    def near(self):
        at = self.at
        return self.hop(self.tile, self.core_in, 0, at.dev(at.slab, at.core_seat))

    def wide(self):
        at = self.at
        return self.hop(self.x_buf, self.x_in, 1, at.dev(at.slab, at.x_seat))

    def far(self, step):
        at = self.at
        device = at.dev(lax.rem(at.slab + step, 4), at.seat)
        return self.hop(self.z_buf, self.z_in.at[at.slab], 1 + step, device)

    def one(self):
        self.near().start()

    def two(self):
        self.near().wait()
        self.x_buf[...] = self.tile[...] + self.core_in[...]
        self.wide().start()

    def three(self):
        self.wide().wait()
        total = self.x_buf[...] + self.x_in[...]
        self.z_buf[...] = total
        self.z_in[self.at.slab] = total
        for step in range(1, 4):
            self.far(step).start()

    def four(self):
        at = self.at
        for step in range(1, 4):
            self.far(step).wait_send()
            source = lax.rem(at.slab - step + 4, 4)
            slot = self.z_in.at[source]
            self.hop(slot, slot, 1 + step, at.dev(source, at.seat)).wait_recv()
        return (self.z_in[0] + self.z_in[1]) + (self.z_in[2] + self.z_in[3])


def summed_scratch(shape):
    return [
        pltpu.VMEM(shape, f32),
        pltpu.VMEM(shape, f32),
        pltpu.VMEM(shape, f32),
        pltpu.VMEM(shape, f32),
        pltpu.VMEM(shape, f32),
        pltpu.VMEM((4,) + shape, f32),
        pltpu.SemaphoreType.DMA((5,)),
        pltpu.SemaphoreType.DMA((5,)),
    ]


class Scatter:
    def __init__(self, at, rc, s1, rx, s2, ra, s3, rb, send, recv):
        self.at = at
        self.core = lax.rem(at.seat, 2)
        self.wide = lax.div(at.seat, 2)
        self.low = lax.rem(at.slab, 2)
        self.high = lax.div(at.slab, 2)
        self.rc, self.s1, self.rx, self.s2 = rc, s1, rx, s2
        self.ra, self.s3, self.rb = ra, s3, rb
        self.send, self.recv = send, recv

    def hop(self, stage, k, src, dst, device):
        return remote(src, dst, self.send.at[stage, k], self.recv.at[stage, k], device)

    def c_copy(self, k, source):
        at = self.at
        device = at.dev(at.slab, at.core_seat)
        return self.hop(0, k, source.at[:, :, 1 - self.core], self.rc.at[k], device)

    def x_copy(self, k):
        at = self.at
        device = at.dev(at.slab, at.x_seat)
        return self.hop(1, k, self.s1.at[k, :, 1 - self.wide], self.rx.at[k], device)

    def a_copy(self, k):
        at = self.at
        device = at.dev(at.slab + 1 - 2 * self.low, at.seat)
        return self.hop(2, k, self.s2.at[k, :, 1 - self.low], self.ra.at[k], device)

    def b_copy(self, k):
        at = self.at
        device = at.dev(lax.rem(at.slab + 2, 4), at.seat)
        return self.hop(3, k, self.s3.at[k, 1 - self.high], self.rb.at[k], device)

    def core_add(self, k, source):
        self.c_copy(k, source).wait_recv()

        def one(i, _):
            self.s1[k, i] = (
                source[i, :, self.core].astype(f32) + self.rc[k, i].astype(f32)
            ).astype(bf16)
            return 0

        lax.fori_loop(0, 4, one, 0)

    def x_add(self, k):
        self.x_copy(k).wait_recv()
        for i in range(4):
            self.s2[k, i // 2, i % 2] = (
                self.s1[k, i, self.wide].astype(f32) + self.rx[k, i].astype(f32)
            ).astype(bf16)

    def a_add(self, k):
        self.a_copy(k).wait_recv()
        for i in range(2):
            self.s3[k, i] = (
                self.s2[k, i, self.low].astype(f32) + self.ra[k, i].astype(f32)
            ).astype(bf16)

    def b_add(self, k):
        self.b_copy(k).wait_recv()
        return self.s3[k, self.high].astype(f32) + self.rb[k].astype(f32)


def attend_mask(size, rows, per, step, mine):
    key = lax.broadcasted_iota(jnp.int32, (size, 1), 0)
    key = lax.div(key, per) * rows + lax.rem(key, per) + step * per
    query = lax.broadcasted_iota(jnp.int32, (1, rows), 1) + mine * rows
    return key <= query


def forward_kernel(
    x_ref, gain_ref, bias_ref, wq_ref, wk_ref, wv_ref, wo_ref, mask_ref,
    none_ref, kv_ref, q_ref, ot_ref, ls_ref, ctx_ref, ctx_in_ref, cnt_ref, wo_in_ref,
    kvs, qs, os, top, low,
    z_send, z_recv, q_send, q_recv, c_send, c_recv, x_send, x_recv, f_send, f_recv,
    o_send, o_recv, e_send, e_recv, w_sem,
    tile, core_in, x_buf, x_in, z_buf, z_in, t_send, t_recv,
):
    at = Place()
    rows = x_ref.shape[0]
    per = rows // FSTEPS
    slab, seat = at.slab, at.seat
    even = lax.rem(slab, 2) == 0
    odd = jnp.logical_not(even)
    goal = at.turned(slab)
    ready = greet(at.peers(True, True, True, True))

    def order(k):
        down = jnp.where(3 - k > slab, 3 - k, 2 - k)
        up = jnp.where(k < slab, k, k + 1)
        return jnp.where(slab < 2, down, up)

    def q_copy(h):
        return remote(qs.at[h], q_ref.at[slab], q_send.at[h], q_recv.at[slab], at.dev(h, goal))

    def kv_copy(h, t):
        return remote(
            kvs.at[h, :, t], kv_ref.at[:, slab, seat, t], z_send.at[t, h], z_recv.at[t, slab],
            at.dev(h, seat),
        )

    def near_copy(t):
        part = kv_ref.at[:, :, seat, t]
        return remote(part, part, c_send.at[t], c_recv.at[t], at.dev(slab, at.core_seat))

    def wide_copy(t):
        part = kv_ref.at[:, :, seat, t]
        return remote(part, part, x_send.at[t], x_recv.at[t], at.dev(slab, at.x_seat))

    def pass_copy(t):
        part = kv_ref.at[:, :, at.x_seat, t]
        return remote(part, part, f_send.at[t], f_recv.at[t], at.dev(slab, at.core_seat))

    normed, _ = norm_stats(x_ref[...])
    n_one = (normed * gain_ref[...] + bias_ref[...]).astype(bf16)
    none_ref[...] = n_one
    query = nn(n_one, wq_ref[...]).astype(bf16)
    for h in range(4):
        qs[h] = query[:, h * HEAD_DIM : (h + 1) * HEAD_DIM]
    ready()
    for k in range(3):
        q_copy(order(k)).start()

    @pl.when(even)
    def _():
        q_ref[slab] = qs[slab]

    @pl.when(odd)
    def _():
        q_copy(slab).start()

    for j, w_ref in enumerate((wk_ref, wv_ref)):
        made = nn(none_ref[...], w_ref[...]).astype(bf16)
        for h in range(4):
            kvs[h, j] = made[:, h * HEAD_DIM : (h + 1) * HEAD_DIM].reshape(FSTEPS, per, HEAD_DIM)
    for t in range(FSTEPS):
        for k in range(3):
            kv_copy(order(k), t).start()
    kv_ref[:, slab, seat] = kvs[slab]
    w_copy = remote(wo_ref, wo_in_ref, w_sem.at[0], w_sem.at[1], at.other_side())
    w_copy.start()
    count = jnp.sum(mask_ref[...].astype(f32), axis=1, keepdims=True)
    tile[...] = jnp.broadcast_to(count, tile.shape)
    total = Summed(at, tile, core_in, x_buf, x_in, z_buf, z_in, t_send, t_recv)
    total.one()
    top[...] = jnp.full_like(top, NEGATIVE)
    low[...] = jnp.zeros_like(low)
    ot_ref[...] = jnp.zeros_like(ot_ref)

    def relay(t):
        for step in range(1, 4):
            source = lax.rem(slab + step, 4)
            part = kv_ref.at[:, source, seat, t]
            remote(
                part, part, z_send.at[t, source], z_recv.at[t, source], at.dev(source, seat)
            ).wait_recv()
        near_copy(t).start()
        wide_copy(t).start()

    def hand_on(t):
        part = kv_ref.at[:, :, at.x_seat, t]
        remote(part, part, x_send.at[t], x_recv.at[t], at.dev(slab, at.x_seat)).wait_recv()
        pass_copy(t).start()

    def arrive(t):
        device = at.dev(slab, at.core_seat)
        part = kv_ref.at[:, :, at.core_seat, t]
        remote(part, part, c_send.at[t], c_recv.at[t], device).wait_recv()
        part = kv_ref.at[:, :, at.far_seat, t]
        remote(part, part, f_send.at[t], f_recv.at[t], device).wait_recv()

    def unit(slot, parts):
        scored = []
        after = before = top[slot]
        for keys, _, allowed in parts:
            scores = nt(keys, q_ref[slot]) * LOG_SCALE
            if allowed is not None:
                scores = jnp.where(allowed, scores, NEGATIVE)
            after = jnp.maximum(after, jnp.max(scores, axis=0, keepdims=True))
            scored.append(scores)
        shrink = jnp.exp2(before - after)
        total_low = low[slot] * shrink
        total = ot_ref[slot] * shrink
        for scores, (_, values, _) in zip(scored, parts):
            prob = jnp.exp2(scores - after)
            total_low = total_low + jnp.sum(prob, axis=0, keepdims=True)
            total = total + tn(values, prob.astype(bf16))
        low[slot] = total_low
        top[slot] = after
        ot_ref[slot] = total

    def o_copy(slot):
        return remote(
            os.at[slot], ctx_ref.at[slab], o_send.at[slot], o_recv.at[slab],
            at.dev(slot, at.turned(slot)),
        )

    def slot_step(slot, t):
        mine = at.turned(slot)

        def taken(pick, size, allowed):
            keys = kv_ref[(0,) + pick + (t,)].reshape(size, HEAD_DIM)
            values = kv_ref[(1,) + pick + (t,)].reshape(size, HEAD_DIM)
            return keys, values, allowed

        for blocks, chosen in ((2, mine < 2), (4, mine >= 2)):

            @pl.when(chosen)
            def _():
                parts = []
                if slot > 0:
                    parts.append(taken((slice(0, slot), slice(0, 4)), 4 * slot * per, None))
                size = blocks * per
                allowed = attend_mask(size, rows, per, t, mine)
                parts.append(taken((slot, slice(0, blocks)), size, allowed))
                unit(slot, parts)

        @pl.when(t == FSTEPS - 1)
        def _():
            done = ot_ref[slot] / low[slot]
            ot_ref[slot] = done
            ls_ref[slot] = top[slot] + jnp.log2(low[slot])
            os[slot] = done.T.astype(bf16)
            home = jnp.logical_and(slab == slot, even)

            @pl.when(home)
            def _():
                ctx_ref[slab] = os[slot]

            @pl.when(jnp.logical_not(home))
            def _():
                o_copy(slot).start()

    for step in range(1, 4):
        source = lax.rem(slab + step, 4)
        part = q_ref.at[source]
        remote(
            part, part, q_send.at[source], q_recv.at[source], at.dev(source, seat)
        ).wait_recv()

    @pl.when(odd)
    def _():
        part = q_ref.at[slab]
        remote(part, part, q_send.at[slab], q_recv.at[slab], at.dev(slab, seat)).wait_recv()

    relay(0)
    total.two()
    relay(1)
    hand_on(0)

    def go(t, _):
        arrive(t)
        slot_step(3, t)

        @pl.when(t + 2 < FSTEPS)
        def _():
            relay(t + 2)

        @pl.when(t == 0)
        def _():
            total.three()

        slot_step(0, t)
        slot_step(2, t)

        @pl.when(t + 1 < FSTEPS)
        def _():
            hand_on(t + 1)

        slot_step(1, t)
        return 0

    lax.fori_loop(0, FSTEPS, go, 0)
    cnt_ref[...] = total.four()
    for k in range(3):
        q_copy(order(k)).wait_send()

    @pl.when(odd)
    def _():
        q_copy(slab).wait_send()

    def finish(t, _):
        for k in range(3):
            kv_copy(order(k), t).wait_send()
        near_copy(t).wait_send()
        wide_copy(t).wait_send()
        pass_copy(t).wait_send()
        return 0

    def e_copy(k):
        return remote(ctx_ref.at[k], ctx_in_ref.at[k], e_send.at[k], e_recv.at[k], at.other_side())

    for step in range(4):
        k = lax.rem(slab + step, 4)
        home = jnp.logical_and(step == 0, even)

        @pl.when(jnp.logical_not(home))
        def _():
            part = ctx_ref.at[k]
            remote(part, part, o_send.at[k], o_recv.at[k], at.dev(k, seat)).wait_recv()

        e_copy(k).start()
    lax.fori_loop(0, FSTEPS, finish, 0)
    w_copy.wait()
    for k in range(4):
        home = jnp.logical_and(slab == k, even)

        @pl.when(jnp.logical_not(home))
        def _():
            o_copy(k).wait_send()

        e_copy(k).wait()


def heads_row(ref, rows_at):
    return jnp.concatenate([ref[h, rows_at, :] for h in range(4)], axis=1)


def middle_kernel(
    token_total,
    ctx_ref, ctx_in, x_hbm, wo_hbm, wo_in_hbm, gain_ref, bias_ref, wup_hbm, wdn_hbm, teach_hbm,
    mask_ref, cnt_ref,
    out_ref, dh_ref, do_ref, one_ref, two_ref, go_ref, vec_ref,
    x_buf, wo, wo_in, wup, wdn, teach, load,
    normed_s, inv_s, n2s, acts, gfs, dpres, gas, dcs,
    fs, fr, bs, br,
    f_send, f_recv, b_send, b_recv, d_send, d_recv,
    gt, rc, s1, rx, g_send, g_recv,
):
    at = Place()
    slab, seat = at.slab, at.seat
    rows = out_ref.shape[0]
    part_rows = rows // CHUNKS
    ready = greet(at.peers(True, True, True, True))
    loads = [
        pltpu.make_async_copy(src, dst, load.at[k])
        for k, (src, dst) in enumerate(
            (
                (wo_hbm, wo), (wo_in_hbm, wo_in), (x_hbm, x_buf), (wup_hbm, wup),
                (wdn_hbm, wdn), (teach_hbm, teach),
            )
        )
    ]
    for copy in loads:
        copy.start()
    ready()

    def f_copy(c):
        return remote(fs.at[c], fr.at[c], f_send.at[c], f_recv.at[c], at.other_side())

    def b_copy(c):
        return remote(bs.at[c], br.at[c], b_send.at[c], b_recv.at[c], at.other_side())

    for k in range(3):
        loads[k].wait()

    def forward(c, _):
        part = pl.ds(pl.multiple_of(c * part_rows, part_rows), part_rows)
        hidden = x_buf[part, :] + (
            nn(heads_row(ctx_ref, part), wo[...]) + nn(heads_row(ctx_in, part), wo_in[...])
        )
        out_ref[part, :] = hidden
        normed, inverse = norm_stats(hidden)
        normed_s[part, :] = normed
        inv_s[part, :] = inverse
        n_two = (normed * gain_ref[...] + bias_ref[...]).astype(bf16)
        n2s[part, :] = n_two

        @pl.when(c == 0)
        def _():
            loads[3].wait()
            loads[4].wait()

        active = jnp.maximum(nn(n_two, wup[...]), 0.0).astype(bf16)
        acts[part, :] = active
        fs[c] = nn(active, wdn[...]).astype(bf16)
        f_copy(c).start()
        return 0

    lax.fori_loop(0, CHUNKS, forward, 0)
    loads[5].wait()
    scale = token_total / cnt_ref[0:1, 0:1]
    vec_ref[...] = jnp.zeros_like(vec_ref)

    def back_one(c, _):
        part = pl.ds(pl.multiple_of(c * part_rows, part_rows), part_rows)
        f_copy(c).wait()
        output = out_ref[part, :] + (fs[c].astype(f32) + fr[c].astype(f32))
        out_ref[part, :] = output
        misfit = output - teach[part, :]
        held = misfit * mask_ref[part, :]
        vec_ref[2:3, :] += jnp.sum(held * misfit, axis=0, keepdims=True)
        d_output = scale * held
        dh_ref[part, :] = d_output
        g_ffn = d_output.astype(bf16)
        gfs[part, :] = g_ffn
        d_active = nt(g_ffn, wdn[...])
        d_pre = jnp.where(acts[part, :] > 0, d_active, 0.0).astype(bf16)
        dpres[part, :] = d_pre
        bs[c] = nt(d_pre, wup[...]).astype(bf16)
        b_copy(c).start()
        return 0

    lax.fori_loop(0, CHUNKS, back_one, 0)
    scatter = Scatter(at, rc, s1, rx, two_ref, None, None, None, g_send, g_recv)
    split = gt.shape[1:5]
    half = gt.shape[5] // 2
    for k in range(4):
        slot = gt.at[k % 2]
        if k >= 2:
            scatter.c_copy(k - 2, slot).wait_send()
        for j in range(2):
            cols = slice((k % 2) * 2 * half + j * half, (k % 2) * 2 * half + (j + 1) * half)
            if k < 2:
                made = tn(gfs[...], acts[:, cols])
            else:
                made = tn(n2s[...], dpres[:, cols])
            gt[k % 2, :, :, :, :, j * half : (j + 1) * half] = made.astype(bf16).reshape(
                split + (half,)
            )
        scatter.c_copy(k, slot).start()
        if k >= 1:
            scatter.core_add(k - 1, gt.at[(k - 1) % 2])
            if k == 1:
                scatter.x_copy(0).start()
    scatter.core_add(3, gt.at[1])
    scatter.c_copy(2, gt.at[0]).wait_send()
    scatter.c_copy(3, gt.at[1]).wait_send()
    for k in range(3):
        one_ref[k] = s1[1 + k]

    def d_copy(c, h):
        part = pl.ds(pl.multiple_of(c * part_rows, part_rows), part_rows)
        return remote(
            dcs.at[h, part, :], do_ref.at[slab, part, :], d_send.at[c, h], d_recv.at[c, slab],
            at.dev(h, at.turned(slab)),
        )

    even = lax.rem(slab, 2) == 0

    def back_two(c, _):
        part = pl.ds(pl.multiple_of(c * part_rows, part_rows), part_rows)
        b_copy(c).wait()
        d_two = bs[c].astype(f32) + br[c].astype(f32)
        normed = normed_s[part, :]
        scaled = d_two * gain_ref[...]
        first = jnp.mean(scaled, axis=-1, keepdims=True)
        second = jnp.mean(scaled * normed, axis=-1, keepdims=True)
        d_hidden = dh_ref[part, :] + inv_s[part, :] * (scaled - first - normed * second)
        vec_ref[0:1, :] += jnp.sum(d_two * normed, axis=0, keepdims=True)
        vec_ref[1:2, :] += jnp.sum(d_two, axis=0, keepdims=True)
        dh_ref[part, :] = d_hidden
        g_attn = d_hidden.astype(bf16)
        gas[part, :] = g_attn
        d_context = nt(g_attn, wo[...]).astype(bf16)
        for h in range(4):
            dcs[h, part, :] = d_context[:, h * HEAD_DIM : (h + 1) * HEAD_DIM]
            home = jnp.logical_and(slab == h, even)

            @pl.when(home)
            def _():
                do_ref[slab, part, :] = dcs[h, part, :]

            @pl.when(jnp.logical_not(home))
            def _():
                d_copy(c, h).start()

        return 0

    lax.fori_loop(0, CHUNKS, back_two, 0)
    go_ref[...] = tn(gas[...], heads_row(ctx_ref, slice(None))).astype(bf16)
    scatter.x_add(0)
    scatter.x_copy(0).wait_send()

    def finish(c, _):
        part = pl.ds(pl.multiple_of(c * part_rows, part_rows), part_rows)
        for h in range(4):
            home = jnp.logical_and(slab == h, even)

            @pl.when(jnp.logical_not(home))
            def _():
                d_copy(c, h).wait_send()
                slot = do_ref.at[h, part, :]
                remote(
                    slot, slot, d_send.at[c, h], d_recv.at[c, h], at.dev(h, seat)
                ).wait_recv()

        return 0

    lax.fori_loop(0, CHUNKS, finish, 0)


def backward_kernel(
    kv_ref, q_ref, ot_ref, ls_ref, do_ref, part_one, part_two, go_ref,
    n_one_hbm, wq_hbm, wk_hbm, wv_hbm, x_hbm, dh_hbm, gain_ref, vec_ref, cnt_ref,
    ig_ref, gq_ref, gk_ref, gv_ref, go_out, gu_ref, gd_ref, g1_ref, b1_ref, g2_ref, b2_ref,
    loss_ref, vsum_ref,
    dq_ref, dkv_ref, acc, delta, near_out, near_in, wide_out, wide_in, home_out, dqs,
    n_send, n_recv, w_send, w_recv, h_send, h_recv, d_send, d_recv,
    a_one, s3_one, b_one, one_send, one_recv,
    rx, s2, ra, s3, rb, two_send, two_recv,
    gc, g1, gx, g2, gg, g3, gb, g_send, g_recv, bs, br,
    b_send, b_recv, load,
    tile, core_in, x_buf, x_in, z_buf, z_in, t_send, t_recv,
):
    at = Place()
    slab, seat = at.slab, at.seat
    core, wide = lax.rem(seat, 2), lax.div(seat, 2)
    rows = q_ref.shape[1]
    per = rows // STEPS
    part_rows = rows // CHUNKS
    even = lax.rem(slab, 2) == 0
    ready = greet(at.peers(True, True, True, True))
    first = Scatter(at, None, None, None, part_two, a_one, s3_one, b_one, one_send, one_recv)
    rest = Scatter(at, None, part_one, rx, s2, ra, s3, rb, two_send, two_recv)
    own = Scatter(at, gc, g1, gx, g2, gg, g3, gb, g_send, g_recv)
    acc[...] = jnp.zeros_like(acc)
    for slot in range(4):
        delta[slot] = jnp.sum(do_ref[slot].astype(f32).T * ot_ref[slot], axis=0, keepdims=True)
    ready()
    own.c_copy(0, go_ref).start()
    first.a_copy(0).start()
    rest.x_copy(0).start()

    def b_copy(c):
        return remote(bs.at[c], br.at[c], b_send.at[c], b_recv.at[c], at.other_side())

    def attention(grads, kept):
        def unit(slot, t, buf, start, slabs, blocks, allowed):
            size = slabs * blocks * per
            pick = (slice(start, start + slabs), slice(0, blocks))
            keys = kv_ref[(0,) + pick + (t,)].reshape(size, HEAD_DIM)
            values = kv_ref[(1,) + pick + (t,)].reshape(size, HEAD_DIM)
            query = q_ref[slot]
            d_out = do_ref[slot]
            scores = nt(keys, query) * LOG_SCALE - ls_ref[slot]
            if allowed is not None:
                scores = jnp.where(allowed, scores, NEGATIVE)
            prob = jnp.exp2(scores)
            d_probs = nt(values, d_out)
            d_scores = (prob * (d_probs - delta[slot])).astype(bf16)
            shape = (slabs, blocks, per, HEAD_DIM)
            grads[(buf, 1) + pick] += nn(prob.astype(bf16), d_out).reshape(shape)
            grads[(buf, 0) + pick] += nn(d_scores, query).reshape(shape)
            acc[slot] += tn(keys, d_scores)

        def d_copy(slot):
            return remote(
                dqs.at[slot], dq_ref.at[slab], d_send.at[slot], d_recv.at[slab],
                at.dev(slot, at.turned(slot)),
            )

        def slot_step(slot, t, buf):
            if slot > 0:
                unit(slot, t, buf, 0, slot, 4, None)
            mine = at.turned(slot)
            for blocks, chosen in ((2, mine < 2), (4, mine >= 2)):

                @pl.when(chosen)
                def _():
                    allowed = attend_mask(blocks * per, rows, per, t, mine)
                    unit(slot, t, buf, slot, 1, blocks, allowed)

            @pl.when(t == STEPS - 1)
            def _():
                dqs[slot] = (acc[slot] * HEAD_SCALE).T.astype(bf16)
                home = jnp.logical_and(slab == slot, even)

                @pl.when(home)
                def _():
                    dq_ref[slab] = dqs[slot]

                @pl.when(jnp.logical_not(home))
                def _():
                    d_copy(slot).start()

        def part(buf, x, c):
            return grads[buf, :, :, 2 * x + c]

        def near_copy(t):
            return remote(
                near_out.at[lax.rem(t, 2)], near_in.at[lax.rem(t, 2)], n_send.at[t], n_recv.at[t], at.dev(slab, at.core_seat)
            )

        def wide_copy(t):
            return remote(
                wide_out.at[t], wide_in.at[t], w_send.at[t], w_recv.at[t], at.dev(slab, at.x_seat)
            )

        def home_copy(t, k):
            return remote(
                home_out.at[t, :, k], dkv_ref.at[slab, :, t], h_send.at[t, k], h_recv.at[t, slab],
                at.dev(k, seat),
            )

        def near_stage(t, buf):
            near_copy(t).wait_recv()
            wide_out[t] = (part(buf, 1 - wide, core) + near_in[buf, 1 - wide].astype(f32)).astype(bf16)
            wide_copy(t).start()
            kept[buf] = part(buf, wide, core) + near_in[buf, wide].astype(f32)

        def wide_stage(t, buf):
            wide_copy(t).wait_recv()
            home_out[t, 0] = ((kept[buf, 0] + wide_in[t, 0].astype(f32)) * HEAD_SCALE).astype(bf16)
            home_out[t, 1] = (kept[buf, 1] + wide_in[t, 1].astype(f32)).astype(bf16)
            dkv_ref[slab, :, t] = home_out[t, :, slab]
            for step in range(1, 4):
                home_copy(t, lax.rem(slab + step, 4)).start()

        def go(t, _):
            buf = lax.rem(t, 2)
            grads[buf] = jnp.zeros_like(grads[buf])
            slot_step(3, t, buf)

            @pl.when(t > 1)
            def _():
                wide_stage(t - 2, buf)

            @pl.when(t > 0)
            def _():
                near_stage(t - 1, 1 - buf)

            slot_step(0, t, buf)

            @pl.when(t == 0)
            def _():
                own.core_add(0, go_ref)
                own.x_copy(0).start()

            @pl.when(t == 1)
            def _():
                first.a_add(0)
                first.b_copy(0).start()

            @pl.when(t == 2)
            def _():
                rest.x_add(0)
                rest.a_copy(0).start()

            @pl.when(t == 3)
            def _():
                own.x_add(0)
                own.a_copy(0).start()

            slot_step(2, t, buf)
            slot_step(1, t, buf)

            @pl.when(t > 1)
            def _():
                near_copy(t - 2).wait_send()

            for x in range(2):
                near_out[buf, x] = part(buf, x, 1 - core).astype(bf16)
            near_copy(t).start()
            return 0

        lax.fori_loop(0, STEPS, go, 0)
        wide_stage(STEPS - 2, STEPS % 2)
        near_stage(STEPS - 1, (STEPS - 1) % 2)
        rest.x_copy(1).start()
        rest.x_copy(2).start()
        rest.a_add(0)
        rest.b_copy(0).start()
        own.a_add(0)
        own.b_copy(0).start()
        gd_ref[:, : gd_ref.shape[1] // 2] = first.b_add(0)
        wide_stage(STEPS - 1, (STEPS - 1) % 2)

        def finish(t, _):
            wide_copy(t).wait_send()
            for step in range(1, 4):
                k = lax.rem(slab + step, 4)
                home_copy(t, k).wait_send()
                slot = dkv_ref.at[k, :, t]
                remote(slot, slot, h_send.at[t, k], h_recv.at[t, k], at.dev(k, seat)).wait_recv()
            return 0

        lax.fori_loop(0, STEPS, finish, 0)
        near_copy(STEPS - 2).wait_send()
        near_copy(STEPS - 1).wait_send()
        for k in range(4):
            home = jnp.logical_and(slab == k, even)

            @pl.when(jnp.logical_not(home))
            def _():
                d_copy(k).wait_send()
                slot = dq_ref.at[k]
                remote(slot, slot, d_send.at[k], d_recv.at[k], at.dev(k, seat)).wait_recv()

    pl.run_scoped(
        attention,
        pltpu.VMEM((2, 2, 4, 4, per, HEAD_DIM), f32),
        pltpu.VMEM((2, 2, 4, per, HEAD_DIM), f32),
    )

    def ending(n_one, wq, wk, wv, x, dh, dcat, ga):
        loads = [
            pltpu.make_async_copy(src, dst, load.at[k])
            for k, (src, dst) in enumerate(
                (
                    (wq_hbm, wq), (wk_hbm, wk), (wv_hbm, wv), (n_one_hbm, n_one), (x_hbm, x),
                    (dh_hbm, dh),
                )
            )
        ]
        for copy in loads:
            copy.start()
        dcat[0] = heads_row(dq_ref, slice(None))
        for j in range(2):
            dcat[1 + j] = jnp.concatenate(
                [dkv_ref[h, j].reshape(rows, HEAD_DIM) for h in range(4)], axis=1
            )
        for k in range(3):
            loads[k].wait()

        def side_part(c, _):
            part = pl.ds(pl.multiple_of(c * part_rows, part_rows), part_rows)
            bs[c] = (
                nt(dcat[0, part, :], wq[...])
                + nt(dcat[1, part, :], wk[...])
                + nt(dcat[2, part, :], wv[...])
            ).astype(bf16)
            b_copy(c).start()
            return 0

        lax.fori_loop(0, CHUNKS, side_part, 0)
        loads[3].wait()
        for j in range(3):
            ga[j] = tn(n_one[...], dcat[j]).astype(bf16).reshape(ga.shape[1:])
            own.c_copy(j + 1, ga.at[j]).start()
            if j > 0:
                own.core_add(j, ga.at[j - 1])
                own.x_copy(j).start()
        own.core_add(3, ga.at[2])
        own.x_copy(3).start()
        for k in range(1, 3):
            rest.x_add(k)
            rest.a_copy(k).start()
        tile[...] = vec_ref[...]
        tile[3:5, :] = jnp.zeros_like(tile[3:5, :])
        loads[4].wait()
        loads[5].wait()

        def side_sum(c, _):
            part = pl.ds(pl.multiple_of(c * part_rows, part_rows), part_rows)
            b_copy(c).wait()
            d_one = bs[c].astype(f32) + br[c].astype(f32)
            normed, inverse = norm_stats(x[part, :])
            scaled = d_one * gain_ref[...]
            first_mean = jnp.mean(scaled, axis=-1, keepdims=True)
            second_mean = jnp.mean(scaled * normed, axis=-1, keepdims=True)
            ig_ref[part, :] = dh[part, :] + inverse * (scaled - first_mean - normed * second_mean)
            tile[3:4, :] += jnp.sum(d_one * normed, axis=0, keepdims=True)
            tile[4:5, :] += jnp.sum(d_one, axis=0, keepdims=True)
            for k in range(1, 4):

                @pl.when(c == k * CHUNKS // 4)
                def _():
                    own.x_add(k)
                    own.a_copy(k).start()
                    if k < 3:
                        rest.a_add(k)
                        rest.b_copy(k).start()
                    if k > 1:
                        own.a_add(k - 1)
                        own.b_copy(k - 1).start()

            return 0

        lax.fori_loop(0, CHUNKS, side_sum, 0)
        total = Summed(at, tile, core_in, x_buf, x_in, z_buf, z_in, t_send, t_recv)
        total.one()
        half = gu_ref.shape[1] // 2
        gd_ref[:, half:] = rest.b_add(0)
        total.two()
        for k in range(2):
            gu_ref[:, k * half : (k + 1) * half] = rest.b_add(1 + k)
        go_out[...] = own.b_add(0)
        own.a_add(3)
        own.b_copy(3).start()
        total.three()
        gq_ref[...] = own.b_add(1)
        gk_ref[...] = own.b_add(2)
        gv_ref[...] = own.b_add(3)
        vsum_ref[...] = total.four()
        share = gq_ref.shape[0]
        for k in range(SEQ_DEV):

            @pl.when(at.pos == k)
            def _():
                for line, ref in ((3, g1_ref), (4, b1_ref), (0, g2_ref), (1, b2_ref)):
                    ref[...] = vsum_ref[line : line + 1, k * share : (k + 1) * share]

        loss_ref[...] = jnp.sum(vsum_ref[2:3, :], axis=1, keepdims=True) / (
            2.0 * cnt_ref[0:1, 0:1]
        )
        for k in range(4):
            own.c_copy(k, go_ref if k == 0 else ga.at[k - 1]).wait_send()
            own.x_copy(k).wait_send()
            own.a_copy(k).wait_send()
            own.b_copy(k).wait_send()
        for k in range(3):
            rest.x_copy(k).wait_send()
            rest.a_copy(k).wait_send()
            rest.b_copy(k).wait_send()
        first.a_copy(0).wait_send()
        first.b_copy(0).wait_send()

    width, local = wq_hbm.shape
    pl.run_scoped(
        ending,
        pltpu.VMEM((rows, width), bf16),
        pltpu.VMEM((width, local), bf16),
        pltpu.VMEM((width, local), bf16),
        pltpu.VMEM((width, local), bf16),
        pltpu.VMEM((rows, width), f32),
        pltpu.VMEM((rows, width), f32),
        pltpu.VMEM((3, rows, local), bf16),
        pltpu.VMEM((3,) + go_ref.shape, bf16),
    )


def copy_kernel(count, *refs):
    ins, outs, held, load, store = (
        refs[:count], refs[count : 2 * count], refs[2 * count : 3 * count], refs[-2], refs[-1],
    )
    loads = [pltpu.make_async_copy(a, h, load.at[k]) for k, (a, h) in enumerate(zip(ins, held))]
    stores = [pltpu.make_async_copy(h, o, store.at[k]) for k, (h, o) in enumerate(zip(held, outs))]
    for copy in loads:
        copy.start()
    for one, two in zip(loads, stores):
        one.wait()
        two.start()
    for copy in stores:
        copy.wait()


def in_vmem():
    return pl.BlockSpec(memory_space=pltpu.VMEM)


def in_hbm():
    return pl.BlockSpec(memory_space=pl.ANY)


def dma(*shape):
    return pltpu.SemaphoreType.DMA(shape)


def call(kernel, name, ident, outs, ins, scratch, args, flops=0):
    return pl.pallas_call(
        kernel,
        name=name,
        out_shape=outs,
        in_specs=ins,
        out_specs=tuple(in_vmem() for _ in outs),
        scratch_shapes=scratch,
        compiler_params=pltpu.CompilerParams(
            collective_id=ident, has_side_effects=True, vmem_limit_bytes=62 * 2**20
        ),
        cost_estimate=pl.CostEstimate(flops=flops, bytes_accessed=2**24, transcendentals=0),
    )(*args)


def per_device(
    inputs, ln1_gain, ln1_bias, w_query, w_key, w_value, w_out, ln2_gain, ln2_bias, w_up, w_down,
    teacher, valid_mask,
):
    rows, width = inputs.shape
    local = w_query.shape[1]
    heads = local // HEAD_DIM
    hidden_units = w_up.shape[1]
    dp_size = lax.axis_size("dp")
    single = dp_size == SEQ_DEV
    share = width // SEQ_DEV
    out = jax.ShapeDtypeStruct
    row = lambda vector: vector.reshape(1, width)
    step_rows = rows // STEPS
    part_rows = rows // CHUNKS

    n_one, kv_all, q_all, o_t, log_sum, ctx, ctx_in, count, wo_in = call(
        forward_kernel, "forward", 1,
        (
            out((rows, width), bf16),
            out((2, 4, 4, FSTEPS, rows // FSTEPS, HEAD_DIM), bf16),
            out((4, rows, HEAD_DIM), bf16),
            out((4, HEAD_DIM, rows), f32),
            out((4, 1, rows), f32),
            out((heads, rows, HEAD_DIM), bf16),
            out((heads, rows, HEAD_DIM), bf16),
            out((8, 128), f32),
            out((local, width), bf16),
        ),
        [in_vmem()] * 8,
        [
            pltpu.VMEM((heads, 2, FSTEPS, rows // FSTEPS, HEAD_DIM), bf16),
            pltpu.VMEM((heads, rows, HEAD_DIM), bf16),
            pltpu.VMEM((4, rows, HEAD_DIM), bf16),
            pltpu.VMEM((4, 1, rows), f32),
            pltpu.VMEM((4, 1, rows), f32),
            dma(FSTEPS, 4), dma(FSTEPS, 4), dma(4), dma(4),
        ]
        + [dma(FSTEPS)] * 6
        + [dma(4)] * 4
        + [dma(2)]
        + summed_scratch((8, 128)),
        (
            inputs, row(ln1_gain), row(ln1_bias), w_query, w_key, w_value, w_out,
            valid_mask.reshape(1, rows),
        ),
    )
    if not single:
        count = jnp.full((8, 128), lax.psum(jnp.sum(valid_mask.astype(f32)), "dp"))
    share = width // SEQ_DEV
    split = (4, 2, 2, share)
    piece = hidden_units // 2
    output, d_hidden, do_all, part_one, part_two, grad_out_t, vectors = call(
        functools.partial(middle_kernel, float(rows * dp_size)), "middle", 2,
        (
            out((rows, width), f32),
            out((rows, width), f32),
            out((4, rows, HEAD_DIM), bf16),
            out((3, 4, 2, share, piece), bf16),
            out((1, 2, 2, share, piece), bf16),
            out((width, local), bf16),
            out((8, width), f32),
        ),
        [
            in_vmem(), in_vmem(), in_hbm(), in_hbm(), in_hbm(), in_vmem(), in_vmem(), in_hbm(),
            in_hbm(), in_hbm(), in_vmem(), in_vmem(),
        ],
        [
            pltpu.VMEM((rows, width), f32),
            pltpu.VMEM((local, width), bf16),
            pltpu.VMEM((local, width), bf16),
            pltpu.VMEM((width, hidden_units), bf16),
            pltpu.VMEM((hidden_units, width), bf16),
            pltpu.VMEM((rows, width), f32),
            dma(6),
            pltpu.VMEM((rows, width), f32),
            pltpu.VMEM((rows, 1), f32),
            pltpu.VMEM((rows, width), bf16),
            pltpu.VMEM((rows, hidden_units), bf16),
            pltpu.VMEM((rows, width), bf16),
            pltpu.VMEM((rows, hidden_units), bf16),
            pltpu.VMEM((rows, width), bf16),
            pltpu.VMEM((heads, rows, HEAD_DIM), bf16),
        ]
        + [pltpu.VMEM((CHUNKS, part_rows, width), bf16)] * 4
        + [dma(CHUNKS)] * 4
        + [dma(CHUNKS, 4)] * 2
        + [
            pltpu.VMEM((2,) + split + (piece,), bf16),
            pltpu.VMEM((4, 4, 2, share, piece), bf16),
            pltpu.VMEM((4, 4, 2, share, piece), bf16),
            pltpu.VMEM((1, 4, share, piece), bf16),
            dma(2, 4), dma(2, 4),
        ],
        (
            ctx, ctx_in, inputs, w_out, wo_in, row(ln2_gain), row(ln2_bias), w_up, w_down, teacher,
            valid_mask.astype(f32).reshape(rows, 1), count,
        ),
    )
    (
        input_grad, grad_query, grad_key, grad_value, grad_out_t, grad_up, grad_down_t, gain_one,
        bias_one, gain_two, bias_two, loss, sums,
    ) = call(
        backward_kernel, "backward", 3,
        (out((rows, width), f32),)
        + (out((share, local), f32),) * 4
        + (out((share, hidden_units), f32),) * 2
        + (out((1, share), f32),) * 4
        + (out((1, 1), f32), out((8, width), f32)),
        [in_vmem()] * 8 + [in_hbm()] * 6 + [in_vmem()] * 3,
        [
            pltpu.VMEM((heads, rows, HEAD_DIM), bf16),
            pltpu.VMEM((heads, 2, STEPS, step_rows, HEAD_DIM), bf16),
            pltpu.VMEM((4, HEAD_DIM, rows), f32),
            pltpu.VMEM((4, 1, rows), f32),
            pltpu.VMEM((2, 2, 2, 4, step_rows, HEAD_DIM), bf16),
            pltpu.VMEM((2, 2, 2, 4, step_rows, HEAD_DIM), bf16),
            pltpu.VMEM((STEPS, 2, 4, step_rows, HEAD_DIM), bf16),
            pltpu.VMEM((STEPS, 2, 4, step_rows, HEAD_DIM), bf16),
            pltpu.VMEM((STEPS, 2, 4, step_rows, HEAD_DIM), bf16),
            pltpu.VMEM((4, rows, HEAD_DIM), bf16),
            dma(STEPS), dma(STEPS), dma(STEPS), dma(STEPS), dma(STEPS, 4), dma(STEPS, 4),
            dma(4), dma(4),
            pltpu.VMEM((1, 2, share, piece), bf16),
            pltpu.VMEM((1, 2, share, piece), bf16),
            pltpu.VMEM((1, share, piece), bf16),
            dma(4, 1), dma(4, 1),
            pltpu.VMEM((3, 4, share, piece), bf16),
            pltpu.VMEM((3, 2, 2, share, piece), bf16),
            pltpu.VMEM((3, 2, share, piece), bf16),
            pltpu.VMEM((3, 2, share, piece), bf16),
            pltpu.VMEM((3, share, piece), bf16),
            dma(4, 3), dma(4, 3),
            pltpu.VMEM((4, 4, 2, share, local), bf16),
            pltpu.VMEM((4, 4, 2, share, local), bf16),
            pltpu.VMEM((4, 4, share, local), bf16),
            pltpu.VMEM((4, 2, 2, share, local), bf16),
            pltpu.VMEM((4, 2, share, local), bf16),
            pltpu.VMEM((4, 2, share, local), bf16),
            pltpu.VMEM((4, share, local), bf16),
            dma(4, 4), dma(4, 4),
            pltpu.VMEM((CHUNKS, part_rows, width), bf16),
            pltpu.VMEM((CHUNKS, part_rows, width), bf16),
            dma(CHUNKS), dma(CHUNKS), dma(6),
        ]
        + summed_scratch((8, width)),
        (
            kv_all.reshape(2, 4, 4, STEPS, step_rows, HEAD_DIM), q_all, o_t, log_sum, do_all,
            part_one, part_two, grad_out_t.reshape(split + (local,)), n_one, w_query, w_key,
            w_value, inputs, d_hidden, row(ln1_gain), vectors, count,
        ),
    )
    if single:
        leaving = (
            output, input_grad, grad_query, grad_key, grad_value, grad_out_t, grad_up, grad_down_t,
            gain_one, bias_one, gain_two, bias_two, loss,
        )
        (
            output, input_grad, grad_query, grad_key, grad_value, grad_out_t, grad_up, grad_down_t,
            gain_one, bias_one, gain_two, bias_two, loss,
        ) = pl.pallas_call(
            functools.partial(copy_kernel, len(leaving)),
            name="leave",
            out_shape=tuple(out(array.shape, array.dtype) for array in leaving),
            in_specs=[in_hbm()] * len(leaving),
            out_specs=tuple(in_hbm() for _ in leaving),
            scratch_shapes=[pltpu.VMEM(array.shape, array.dtype) for array in leaving]
            + [dma(len(leaving)), dma(len(leaving))],
        )(*leaving)
    grad_down, grad_out = grad_down_t.T, grad_out_t.T
    small = [gain_one, bias_one, gain_two, bias_two]
    small = [vector.reshape(share) for vector in small]
    loss_value = loss.reshape(())
    if not single:
        index = lax.axis_index("dp")
        first = lax.rem(index, SEQ_DEV) * share

        def spread(part, axis):
            shape = list(part.shape)
            shape[axis] = width
            at = [0, 0]
            at[axis] = first
            placed = lax.dynamic_update_slice(jnp.zeros(shape, f32), part, tuple(at))
            return lax.psum_scatter(placed, "dp", scatter_dimension=axis, tiled=True)

        grad_query, grad_key, grad_value, grad_up = (
            spread(part, 0) for part in (grad_query, grad_key, grad_value, grad_up)
        )
        grad_out, grad_down = spread(grad_out, 1), spread(grad_down, 1)
        sums = lax.psum(jnp.where(first == 0, sums, 0.0), "dp")
        length = width // dp_size
        small = [lax.dynamic_slice(sums[k], (index * length,), (length,)) for k in (3, 4, 0, 1)]
        loss_value = jnp.sum(sums[2]) / (2.0 * count[0, 0])
    return (
        output, loss_value, input_grad, small[0], small[1], grad_query, grad_key, grad_value,
        grad_out, small[2], small[3], grad_up, grad_down,
    )


def solution(mesh):
    return jax.shard_map(
        per_device,
        mesh=mesh,
        in_specs=(
            P("dp", None), P(), P(), P(None, "tensor"), P(None, "tensor"), P(None, "tensor"),
            P("tensor", None), P(), P(), P(None, "tensor"), P("tensor", None), P("dp", None),
            P("dp"),
        ),
        out_specs=(
            P("dp", None), P(), P("dp", None), P("dp"), P("dp"), P("dp", "tensor"),
            P("dp", "tensor"), P("dp", "tensor"), P("tensor", "dp"), P("dp"), P("dp"),
            P("dp", "tensor"), P("tensor", "dp"),
        ),
        check_vma=False,
    )
```

```python
import functools

import jax
import jax.numpy as jnp
from jax import lax
from jax.experimental import pallas as pl
from jax.experimental.pallas import tpu as pltpu
from jax.sharding import PartitionSpec as P

HEAD_DIM = 128
SEQ_DEV = 16
EPSILON = 1e-05
NEGATIVE = -1e30
LOG_SCALE = 1.4426950408889634 * HEAD_DIM ** (-0.5)
HEAD_SCALE = HEAD_DIM ** (-0.5)
CHUNKS = 4
STEPS = 4
FSTEPS = 4
f32 = jnp.float32
bf16 = jnp.bfloat16


def nn(a, b):
    return lax.dot_general(a, b, (((1,), (0,)), ((), ())), preferred_element_type=f32)


def nt(a, b):
    return lax.dot_general(a, b, (((1,), (1,)), ((), ())), preferred_element_type=f32)


def tn(a, b):
    return lax.dot_general(a, b, (((0,), (0,)), ((), ())), preferred_element_type=f32)


def remote(src, dst, send_sem, recv_sem, device):
    return pltpu.make_async_remote_copy(
        src_ref=src,
        dst_ref=dst,
        send_sem=send_sem,
        recv_sem=recv_sem,
        device_id=device,
        device_id_type=pl.DeviceIdType.MESH,
    )


class Place:
    def __init__(self):
        index = lax.axis_index("dp")
        self.pos = lax.rem(index, SEQ_DEV)
        self.base = index - self.pos
        self.slab = lax.div(self.pos, 4)
        self.seat = lax.rem(self.pos, 4)
        self.side = lax.axis_index("tensor")
        seat = self.seat
        self.core_seat = seat + 1 - 2 * lax.rem(seat, 2)
        self.x_seat = lax.rem(seat + 2, 4)
        self.far_seat = 3 - seat

    def dev(self, slab, seat):
        return {"dp": self.base + slab * 4 + seat, "tensor": self.side}

    def other_side(self):
        return {"dp": self.base + self.pos, "tensor": 1 - self.side}

    def turned(self, slab):
        even = lax.rem(slab, 2) == 0
        return jnp.where(even, self.seat, self.far_seat)

    def peers(self, same, far, near, side):
        found = []
        for step in range(1, 4):
            other = lax.rem(self.slab + step, 4)
            if same:
                found.append(self.dev(other, self.seat))
            if far:
                found.append(self.dev(other, self.far_seat))
        if far:
            found.append(self.dev(self.slab, self.far_seat))
        if near:
            found.append(self.dev(self.slab, self.core_seat))
            found.append(self.dev(self.slab, self.x_seat))
        if side:
            found.append(self.other_side())
        return found


def greet(peers):
    barrier = pltpu.get_barrier_semaphore()
    for peer in peers:
        pl.semaphore_signal(
            barrier, inc=1, device_id=peer, device_id_type=pl.DeviceIdType.MESH
        )
    return functools.partial(pl.semaphore_wait, barrier, len(peers))


def norm_stats(values):
    average = jnp.mean(values, axis=-1, keepdims=True)
    centred = values - average
    inverse = lax.rsqrt(jnp.mean(centred * centred, axis=-1, keepdims=True) + EPSILON)
    return centred * inverse, inverse


class Summed:
    def __init__(self, at, tile, core_in, x_buf, x_in, z_buf, z_in, send, recv):
        self.at, self.tile = at, tile
        self.core_in, self.x_buf, self.x_in = core_in, x_buf, x_in
        self.z_buf, self.z_in = z_buf, z_in
        self.send, self.recv = send, recv

    def hop(self, src, dst, k, device):
        return remote(src, dst, self.send.at[k], self.recv.at[k], device)

    def near(self):
        at = self.at
        return self.hop(self.tile, self.core_in, 0, at.dev(at.slab, at.core_seat))

    def wide(self):
        at = self.at
        return self.hop(self.x_buf, self.x_in, 1, at.dev(at.slab, at.x_seat))

    def far(self, step):
        at = self.at
        device = at.dev(lax.rem(at.slab + step, 4), at.seat)
        return self.hop(self.z_buf, self.z_in.at[at.slab], 1 + step, device)

    def one(self):
        self.near().start()

    def two(self):
        self.near().wait()
        self.x_buf[...] = self.tile[...] + self.core_in[...]
        self.wide().start()

    def three(self):
        self.wide().wait()
        total = self.x_buf[...] + self.x_in[...]
        self.z_buf[...] = total
        self.z_in[self.at.slab] = total
        for step in range(1, 4):
            self.far(step).start()

    def four(self):
        at = self.at
        for step in range(1, 4):
            self.far(step).wait_send()
            source = lax.rem(at.slab - step + 4, 4)
            slot = self.z_in.at[source]
            self.hop(slot, slot, 1 + step, at.dev(source, at.seat)).wait_recv()
        return (self.z_in[0] + self.z_in[1]) + (self.z_in[2] + self.z_in[3])


def summed_scratch(shape):
    return [
        pltpu.VMEM(shape, f32),
        pltpu.VMEM(shape, f32),
        pltpu.VMEM(shape, f32),
        pltpu.VMEM(shape, f32),
        pltpu.VMEM(shape, f32),
        pltpu.VMEM((4,) + shape, f32),
        pltpu.SemaphoreType.DMA((5,)),
        pltpu.SemaphoreType.DMA((5,)),
    ]


class Scatter:
    def __init__(self, at, rc, s1, rx, s2, ra, s3, rb, send, recv):
        self.at = at
        self.core = lax.rem(at.seat, 2)
        self.wide = lax.div(at.seat, 2)
        self.low = lax.rem(at.slab, 2)
        self.high = lax.div(at.slab, 2)
        self.rc, self.s1, self.rx, self.s2 = rc, s1, rx, s2
        self.ra, self.s3, self.rb = ra, s3, rb
        self.send, self.recv = send, recv

    def hop(self, stage, k, src, dst, device):
        return remote(src, dst, self.send.at[stage, k], self.recv.at[stage, k], device)

    def c_copy(self, k, source):
        at = self.at
        device = at.dev(at.slab, at.core_seat)
        return self.hop(0, k, source.at[:, :, 1 - self.core], self.rc.at[k], device)

    def x_copy(self, k):
        at = self.at
        device = at.dev(at.slab, at.x_seat)
        return self.hop(1, k, self.s1.at[k, :, 1 - self.wide], self.rx.at[k], device)

    def a_copy(self, k):
        at = self.at
        device = at.dev(at.slab + 1 - 2 * self.low, at.seat)
        return self.hop(2, k, self.s2.at[k, :, 1 - self.low], self.ra.at[k], device)

    def b_copy(self, k):
        at = self.at
        device = at.dev(lax.rem(at.slab + 2, 4), at.seat)
        return self.hop(3, k, self.s3.at[k, 1 - self.high], self.rb.at[k], device)

    def core_add(self, k, source):
        self.c_copy(k, source).wait_recv()

        def one(i, _):
            self.s1[k, i] = (
                source[i, :, self.core].astype(f32) + self.rc[k, i].astype(f32)
            ).astype(bf16)
            return 0

        lax.fori_loop(0, 4, one, 0)

    def x_add(self, k):
        self.x_copy(k).wait_recv()
        for i in range(4):
            self.s2[k, i // 2, i % 2] = (
                self.s1[k, i, self.wide].astype(f32) + self.rx[k, i].astype(f32)
            ).astype(bf16)

    def a_add(self, k):
        self.a_copy(k).wait_recv()
        for i in range(2):
            self.s3[k, i] = (
                self.s2[k, i, self.low].astype(f32) + self.ra[k, i].astype(f32)
            ).astype(bf16)

    def b_add(self, k):
        self.b_copy(k).wait_recv()
        return self.s3[k, self.high].astype(f32) + self.rb[k].astype(f32)


def attend_mask(size, rows, per, step, mine):
    key = lax.broadcasted_iota(jnp.int32, (size, 1), 0)
    key = lax.div(key, per) * rows + lax.rem(key, per) + step * per
    query = lax.broadcasted_iota(jnp.int32, (1, rows), 1) + mine * rows
    return key <= query


def forward_kernel(
    x_ref, gain_ref, bias_ref, wq_hbm, wk_hbm, wv_hbm, wo_hbm, mask_ref,
    none_ref, kv_ref, q_ref, ot_ref, ls_ref, ctx_ref, cnt_ref, wo_in_ref,
    kvs, qs, os, top, low,
    z_send, z_recv, q_send, q_recv, c_send, c_recv, x_send, x_recv, f_send, f_recv,
    o_send, o_recv, w_sem, wq_ref, wk_ref, wv_ref, wo_ref, load,
    tile, core_in, x_buf, x_in, z_buf, z_in, t_send, t_recv,
):
    at = Place()
    rows = x_ref.shape[0]
    per = rows // FSTEPS
    slab, seat = at.slab, at.seat
    even = lax.rem(slab, 2) == 0
    odd = jnp.logical_not(even)
    goal = at.turned(slab)
    ready = greet(at.peers(True, True, True, True))
    loads = [
        pltpu.make_async_copy(src, dst, load.at[k])
        for k, (src, dst) in enumerate(
            ((wq_hbm, wq_ref), (wk_hbm, wk_ref), (wv_hbm, wv_ref), (wo_hbm, wo_ref))
        )
    ]
    for copy in loads:
        copy.start()

    def order(k):
        down = jnp.where(3 - k > slab, 3 - k, 2 - k)
        up = jnp.where(k < slab, k, k + 1)
        return jnp.where(slab < 2, down, up)

    def q_copy(h):
        return remote(qs.at[h], q_ref.at[slab], q_send.at[h], q_recv.at[slab], at.dev(h, goal))

    def kv_copy(h, t):
        return remote(
            kvs.at[h, :, t], kv_ref.at[:, slab, seat, t], z_send.at[t, h], z_recv.at[t, slab],
            at.dev(h, seat),
        )

    def near_copy(t):
        part = kv_ref.at[:, :, seat, t]
        return remote(part, part, c_send.at[t], c_recv.at[t], at.dev(slab, at.core_seat))

    def wide_copy(t):
        part = kv_ref.at[:, :, seat, t]
        return remote(part, part, x_send.at[t], x_recv.at[t], at.dev(slab, at.x_seat))

    def pass_copy(t):
        part = kv_ref.at[:, :, at.x_seat, t]
        return remote(part, part, f_send.at[t], f_recv.at[t], at.dev(slab, at.core_seat))

    normed, _ = norm_stats(x_ref[...])
    n_one = (normed * gain_ref[...] + bias_ref[...]).astype(bf16)
    none_ref[...] = n_one
    loads[0].wait()
    query = nn(n_one, wq_ref[...]).astype(bf16)
    for h in range(4):
        qs[h] = query[:, h * HEAD_DIM : (h + 1) * HEAD_DIM]
    ready()
    for k in range(3):
        q_copy(order(k)).start()

    @pl.when(even)
    def _():
        q_ref[slab] = qs[slab]

    @pl.when(odd)
    def _():
        q_copy(slab).start()

    for j, w_ref in enumerate((wk_ref, wv_ref)):
        loads[1 + j].wait()
        made = nn(none_ref[...], w_ref[...]).astype(bf16)
        for h in range(4):
            kvs[h, j] = made[:, h * HEAD_DIM : (h + 1) * HEAD_DIM].reshape(FSTEPS, per, HEAD_DIM)
    for t in range(FSTEPS):
        for k in range(3):
            kv_copy(order(k), t).start()
    kv_ref[:, slab, seat] = kvs[slab]
    loads[3].wait()
    w_copy = remote(wo_ref, wo_in_ref, w_sem.at[0], w_sem.at[1], at.other_side())
    w_copy.start()
    count = jnp.sum(mask_ref[...].astype(f32), axis=1, keepdims=True)
    tile[...] = jnp.broadcast_to(count, tile.shape)
    total = Summed(at, tile, core_in, x_buf, x_in, z_buf, z_in, t_send, t_recv)
    total.one()
    top[...] = jnp.full_like(top, NEGATIVE)
    low[...] = jnp.zeros_like(low)
    ot_ref[...] = jnp.zeros_like(ot_ref)

    def relay(t):
        for step in range(1, 4):
            source = lax.rem(slab + step, 4)
            part = kv_ref.at[:, source, seat, t]
            remote(
                part, part, z_send.at[t, source], z_recv.at[t, source], at.dev(source, seat)
            ).wait_recv()
        near_copy(t).start()
        wide_copy(t).start()

    def hand_on(t):
        part = kv_ref.at[:, :, at.x_seat, t]
        remote(part, part, x_send.at[t], x_recv.at[t], at.dev(slab, at.x_seat)).wait_recv()
        pass_copy(t).start()

    def arrive(t):
        device = at.dev(slab, at.core_seat)
        part = kv_ref.at[:, :, at.core_seat, t]
        remote(part, part, c_send.at[t], c_recv.at[t], device).wait_recv()
        part = kv_ref.at[:, :, at.far_seat, t]
        remote(part, part, f_send.at[t], f_recv.at[t], device).wait_recv()

    def unit(slot, parts):
        scored = []
        after = before = top[slot]
        for keys, _, allowed in parts:
            scores = nt(keys, q_ref[slot]) * LOG_SCALE
            if allowed is not None:
                scores = jnp.where(allowed, scores, NEGATIVE)
            after = jnp.maximum(after, jnp.max(scores, axis=0, keepdims=True))
            scored.append(scores)
        shrink = jnp.exp2(before - after)
        total_low = low[slot] * shrink
        total = ot_ref[slot] * shrink
        for scores, (_, values, _) in zip(scored, parts):
            prob = jnp.exp2(scores - after)
            total_low = total_low + jnp.sum(prob, axis=0, keepdims=True)
            total = total + tn(values, prob.astype(bf16))
        low[slot] = total_low
        top[slot] = after
        ot_ref[slot] = total

    def o_copy(slot):
        return remote(
            os.at[slot], ctx_ref.at[slab], o_send.at[slot], o_recv.at[slab],
            at.dev(slot, at.turned(slot)),
        )

    def slot_step(slot, t):
        mine = at.turned(slot)

        def taken(pick, size, allowed):
            keys = kv_ref[(0,) + pick + (t,)].reshape(size, HEAD_DIM)
            values = kv_ref[(1,) + pick + (t,)].reshape(size, HEAD_DIM)
            return keys, values, allowed

        for blocks, chosen in ((2, mine < 2), (4, mine >= 2)):

            @pl.when(chosen)
            def _():
                parts = []
                if slot > 0:
                    parts.append(taken((slice(0, slot), slice(0, 4)), 4 * slot * per, None))
                size = blocks * per
                allowed = attend_mask(size, rows, per, t, mine)
                parts.append(taken((slot, slice(0, blocks)), size, allowed))
                unit(slot, parts)

        @pl.when(t == FSTEPS - 1)
        def _():
            done = ot_ref[slot] / low[slot]
            ot_ref[slot] = done
            ls_ref[slot] = top[slot] + jnp.log2(low[slot])
            os[slot] = done.T.astype(bf16)
            home = jnp.logical_and(slab == slot, even)

            @pl.when(home)
            def _():
                ctx_ref[slab] = os[slot]

            @pl.when(jnp.logical_not(home))
            def _():
                o_copy(slot).start()

    for step in range(1, 4):
        source = lax.rem(slab + step, 4)
        part = q_ref.at[source]
        remote(
            part, part, q_send.at[source], q_recv.at[source], at.dev(source, seat)
        ).wait_recv()

    @pl.when(odd)
    def _():
        part = q_ref.at[slab]
        remote(part, part, q_send.at[slab], q_recv.at[slab], at.dev(slab, seat)).wait_recv()

    relay(0)
    total.two()
    relay(1)
    hand_on(0)

    def go(t, _):
        arrive(t)
        slot_step(3, t)

        @pl.when(t + 2 < FSTEPS)
        def _():
            relay(t + 2)

        @pl.when(t == 0)
        def _():
            total.three()

        slot_step(0, t)
        slot_step(2, t)

        @pl.when(t + 1 < FSTEPS)
        def _():
            hand_on(t + 1)

        slot_step(1, t)
        return 0

    lax.fori_loop(0, FSTEPS, go, 0)
    cnt_ref[...] = total.four()
    for k in range(3):
        q_copy(order(k)).wait_send()

    @pl.when(odd)
    def _():
        q_copy(slab).wait_send()

    def finish(t, _):
        for k in range(3):
            kv_copy(order(k), t).wait_send()
        near_copy(t).wait_send()
        wide_copy(t).wait_send()
        pass_copy(t).wait_send()
        return 0

    lax.fori_loop(0, FSTEPS, finish, 0)
    w_copy.wait()
    for k in range(4):
        home = jnp.logical_and(slab == k, even)

        @pl.when(jnp.logical_not(home))
        def _():
            o_copy(k).wait_send()
            part = ctx_ref.at[k]
            remote(part, part, o_send.at[k], o_recv.at[k], at.dev(k, seat)).wait_recv()


def heads_row(ref, rows_at):
    return jnp.concatenate([ref[h, rows_at, :] for h in range(4)], axis=1)


def middle_kernel(
    token_total,
    ctx_ref, x_hbm, wo_hbm, wo_in_hbm, gain_ref, bias_ref, wup_hbm, wdn_hbm, teach_hbm,
    mask_ref, cnt_ref,
    out_hbm, dh_ref, do_ref, one_hbm, two_ref, go_ref, vec_ref,
    x_buf, wo, wo_in, wup, wdn, teach, load,
    ctx_in, normed_s, inv_s, n2s, acts, gfs, dpres, gas, dcs,
    fs, fr, bs, br,
    e_send, e_recv, f_send, f_recv, b_send, b_recv, d_send, d_recv,
    gt, rc, s1, rx, g_send, g_recv, out_ref, store,
):
    at = Place()
    slab, seat = at.slab, at.seat
    rows = out_ref.shape[0]
    part_rows = rows // CHUNKS
    ready = greet(at.peers(True, True, True, True))
    loads = [
        pltpu.make_async_copy(src, dst, load.at[k])
        for k, (src, dst) in enumerate(
            (
                (wo_hbm, wo), (wo_in_hbm, wo_in), (x_hbm, x_buf), (wup_hbm, wup),
                (wdn_hbm, wdn), (teach_hbm, teach),
            )
        )
    ]
    for copy in loads:
        copy.start()
    ready()

    def e_copy(c):
        part = pl.ds(pl.multiple_of(c * part_rows, part_rows), part_rows)
        return remote(
            ctx_ref.at[:, part, :], ctx_in.at[:, part, :], e_send.at[c], e_recv.at[c],
            at.other_side(),
        )

    def f_copy(c):
        return remote(fs.at[c], fr.at[c], f_send.at[c], f_recv.at[c], at.other_side())

    def b_copy(c):
        return remote(bs.at[c], br.at[c], b_send.at[c], b_recv.at[c], at.other_side())

    for c in range(CHUNKS):
        e_copy(c).start()
    for k in range(3):
        loads[k].wait()

    def forward(c, _):
        part = pl.ds(pl.multiple_of(c * part_rows, part_rows), part_rows)
        e_copy(c).wait()
        hidden = x_buf[part, :] + (
            nn(heads_row(ctx_ref, part), wo[...]) + nn(heads_row(ctx_in, part), wo_in[...])
        )
        out_ref[part, :] = hidden
        normed, inverse = norm_stats(hidden)
        normed_s[part, :] = normed
        inv_s[part, :] = inverse
        n_two = (normed * gain_ref[...] + bias_ref[...]).astype(bf16)
        n2s[part, :] = n_two

        @pl.when(c == 0)
        def _():
            loads[3].wait()
            loads[4].wait()

        active = jnp.maximum(nn(n_two, wup[...]), 0.0).astype(bf16)
        acts[part, :] = active
        fs[c] = nn(active, wdn[...]).astype(bf16)
        f_copy(c).start()
        return 0

    lax.fori_loop(0, CHUNKS, forward, 0)
    loads[5].wait()
    scale = token_total / cnt_ref[0:1, 0:1]
    vec_ref[...] = jnp.zeros_like(vec_ref)

    def back_one(c, _):
        part = pl.ds(pl.multiple_of(c * part_rows, part_rows), part_rows)
        f_copy(c).wait()
        output = out_ref[part, :] + (fs[c].astype(f32) + fr[c].astype(f32))
        out_ref[part, :] = output
        misfit = output - teach[part, :]
        held = misfit * mask_ref[part, :]
        vec_ref[2:3, :] += jnp.sum(held * misfit, axis=0, keepdims=True)
        d_output = scale * held
        dh_ref[part, :] = d_output
        g_ffn = d_output.astype(bf16)
        gfs[part, :] = g_ffn
        d_active = nt(g_ffn, wdn[...])
        d_pre = jnp.where(acts[part, :] > 0, d_active, 0.0).astype(bf16)
        dpres[part, :] = d_pre
        bs[c] = nt(d_pre, wup[...]).astype(bf16)
        b_copy(c).start()
        return 0

    lax.fori_loop(0, CHUNKS, back_one, 0)
    scatter = Scatter(at, rc, s1, rx, two_ref, None, None, None, g_send, g_recv)
    split = gt.shape[1:5]
    half = gt.shape[5] // 2
    for k in range(4):
        slot = gt.at[k % 2]
        if k >= 2:
            scatter.c_copy(k - 2, slot).wait_send()
        for j in range(2):
            cols = slice((k % 2) * 2 * half + j * half, (k % 2) * 2 * half + (j + 1) * half)
            if k < 2:
                made = tn(gfs[...], acts[:, cols])
            else:
                made = tn(n2s[...], dpres[:, cols])
            gt[k % 2, :, :, :, :, j * half : (j + 1) * half] = made.astype(bf16).reshape(
                split + (half,)
            )
        scatter.c_copy(k, slot).start()
        if k >= 1:
            scatter.core_add(k - 1, gt.at[(k - 1) % 2])
            if k == 1:
                scatter.x_copy(0).start()
    scatter.core_add(3, gt.at[1])
    scatter.c_copy(2, gt.at[0]).wait_send()
    scatter.c_copy(3, gt.at[1]).wait_send()
    stores = [
        pltpu.make_async_copy(out_ref, out_hbm, store.at[0]),
        pltpu.make_async_copy(s1.at[1:4], one_hbm, store.at[1]),
    ]
    for copy in stores:
        copy.start()

    def d_copy(c, h):
        part = pl.ds(pl.multiple_of(c * part_rows, part_rows), part_rows)
        return remote(
            dcs.at[h, part, :], do_ref.at[slab, part, :], d_send.at[c, h], d_recv.at[c, slab],
            at.dev(h, at.turned(slab)),
        )

    even = lax.rem(slab, 2) == 0

    def back_two(c, _):
        part = pl.ds(pl.multiple_of(c * part_rows, part_rows), part_rows)
        b_copy(c).wait()
        d_two = bs[c].astype(f32) + br[c].astype(f32)
        normed = normed_s[part, :]
        scaled = d_two * gain_ref[...]
        first = jnp.mean(scaled, axis=-1, keepdims=True)
        second = jnp.mean(scaled * normed, axis=-1, keepdims=True)
        d_hidden = dh_ref[part, :] + inv_s[part, :] * (scaled - first - normed * second)
        vec_ref[0:1, :] += jnp.sum(d_two * normed, axis=0, keepdims=True)
        vec_ref[1:2, :] += jnp.sum(d_two, axis=0, keepdims=True)
        dh_ref[part, :] = d_hidden
        g_attn = d_hidden.astype(bf16)
        gas[part, :] = g_attn
        d_context = nt(g_attn, wo[...]).astype(bf16)
        for h in range(4):
            dcs[h, part, :] = d_context[:, h * HEAD_DIM : (h + 1) * HEAD_DIM]
            home = jnp.logical_and(slab == h, even)

            @pl.when(home)
            def _():
                do_ref[slab, part, :] = dcs[h, part, :]

            @pl.when(jnp.logical_not(home))
            def _():
                d_copy(c, h).start()

        return 0

    lax.fori_loop(0, CHUNKS, back_two, 0)
    go_ref[...] = tn(gas[...], heads_row(ctx_ref, slice(None))).astype(bf16)
    scatter.x_add(0)
    scatter.x_copy(0).wait_send()
    for copy in stores:
        copy.wait()

    def finish(c, _):
        part = pl.ds(pl.multiple_of(c * part_rows, part_rows), part_rows)
        for h in range(4):
            home = jnp.logical_and(slab == h, even)

            @pl.when(jnp.logical_not(home))
            def _():
                d_copy(c, h).wait_send()
                slot = do_ref.at[h, part, :]
                remote(
                    slot, slot, d_send.at[c, h], d_recv.at[c, h], at.dev(h, seat)
                ).wait_recv()

        return 0

    lax.fori_loop(0, CHUNKS, finish, 0)


def backward_kernel(
    kv_ref, q_ref, ot_ref, ls_ref, do_ref, part_one, part_two, go_ref,
    n_one_hbm, wq_hbm, wk_hbm, wv_hbm, x_hbm, dh_hbm, gain_ref, vec_ref, cnt_ref,
    ig_ref, gq_ref, gk_ref, gv_ref, go_out, gu_ref, gd_ref, g1_ref, b1_ref, g2_ref, b2_ref,
    loss_ref, vsum_ref,
    dq_ref, dkv_ref, acc, delta, near_out, near_in, wide_out, wide_in, home_out, dqs,
    n_send, n_recv, w_send, w_recv, h_send, h_recv, d_send, d_recv,
    a_one, s3_one, b_one, one_send, one_recv,
    rx, s2, ra, s3, rb, two_send, two_recv,
    gc, g1, gx, g2, gg, g3, gb, g_send, g_recv, bs, br,
    b_send, b_recv, load, n_one, wq, wk, wv, x, dh, inv_s, side_in, s_sem,
    tile, core_in, x_buf, x_in, z_buf, z_in, t_send, t_recv,
):
    at = Place()
    slab, seat = at.slab, at.seat
    core, wide = lax.rem(seat, 2), lax.div(seat, 2)
    rows = q_ref.shape[1]
    per = rows // STEPS
    part_rows = rows // CHUNKS
    even = lax.rem(slab, 2) == 0
    ready = greet(at.peers(True, True, True, True))
    first = Scatter(at, None, None, None, part_two, a_one, s3_one, b_one, one_send, one_recv)
    rest = Scatter(at, None, part_one, rx, s2, ra, s3, rb, two_send, two_recv)
    own = Scatter(at, gc, g1, gx, g2, gg, g3, gb, g_send, g_recv)
    loads = [
        pltpu.make_async_copy(src, dst, load.at[k])
        for k, (src, dst) in enumerate(
            (
                (wq_hbm, wq), (wk_hbm, wk), (wv_hbm, wv), (n_one_hbm, n_one), (x_hbm, x),
                (dh_hbm, dh),
            )
        )
    ]
    for copy in loads:
        copy.start()
    acc[...] = jnp.zeros_like(acc)
    for slot in range(4):
        delta[slot] = jnp.sum(do_ref[slot].astype(f32).T * ot_ref[slot], axis=0, keepdims=True)
    ready()
    own.c_copy(0, go_ref).start()
    first.a_copy(0).start()
    rest.x_copy(0).start()

    def b_copy(c):
        return remote(bs.at[c], br.at[c], b_send.at[c], b_recv.at[c], at.other_side())

    def attention(grads, kept):
        def unit(slot, t, buf, start, slabs, blocks, allowed):
            size = slabs * blocks * per
            pick = (slice(start, start + slabs), slice(0, blocks))
            keys = kv_ref[(0,) + pick + (t,)].reshape(size, HEAD_DIM)
            values = kv_ref[(1,) + pick + (t,)].reshape(size, HEAD_DIM)
            query = q_ref[slot]
            d_out = do_ref[slot]
            scores = nt(keys, query) * LOG_SCALE - ls_ref[slot]
            if allowed is not None:
                scores = jnp.where(allowed, scores, NEGATIVE)
            prob = jnp.exp2(scores)
            d_probs = nt(values, d_out)
            d_scores = (prob * (d_probs - delta[slot])).astype(bf16)
            shape = (slabs, blocks, per, HEAD_DIM)
            grads[(buf, 1) + pick] += nn(prob.astype(bf16), d_out).reshape(shape)
            grads[(buf, 0) + pick] += nn(d_scores, query).reshape(shape)
            acc[slot] += tn(keys, d_scores)

        def d_copy(slot):
            return remote(
                dqs.at[slot], dq_ref.at[slab], d_send.at[slot], d_recv.at[slab],
                at.dev(slot, at.turned(slot)),
            )

        def slot_step(slot, t, buf):
            if slot > 0:
                unit(slot, t, buf, 0, slot, 4, None)
            mine = at.turned(slot)
            for blocks, chosen in ((2, mine < 2), (4, mine >= 2)):

                @pl.when(chosen)
                def _():
                    allowed = attend_mask(blocks * per, rows, per, t, mine)
                    unit(slot, t, buf, slot, 1, blocks, allowed)

            @pl.when(t == STEPS - 1)
            def _():
                dqs[slot] = (acc[slot] * HEAD_SCALE).T.astype(bf16)
                home = jnp.logical_and(slab == slot, even)

                @pl.when(home)
                def _():
                    dq_ref[slab] = dqs[slot]

                @pl.when(jnp.logical_not(home))
                def _():
                    d_copy(slot).start()

        def part(buf, x, c):
            return grads[buf, :, :, 2 * x + c]

        def near_copy(t):
            return remote(
                near_out.at[lax.rem(t, 2)], near_in.at[lax.rem(t, 2)], n_send.at[t], n_recv.at[t], at.dev(slab, at.core_seat)
            )

        def wide_copy(t):
            return remote(
                wide_out.at[t], wide_in.at[t], w_send.at[t], w_recv.at[t], at.dev(slab, at.x_seat)
            )

        def home_copy(t, k):
            return remote(
                home_out.at[t, :, k], dkv_ref.at[slab, :, t], h_send.at[t, k], h_recv.at[t, slab],
                at.dev(k, seat),
            )

        def near_stage(t, buf):
            near_copy(t).wait_recv()
            wide_out[t] = (part(buf, 1 - wide, core) + near_in[buf, 1 - wide].astype(f32)).astype(bf16)
            wide_copy(t).start()
            kept[buf] = part(buf, wide, core) + near_in[buf, wide].astype(f32)

        def wide_stage(t, buf):
            wide_copy(t).wait_recv()
            home_out[t, 0] = ((kept[buf, 0] + wide_in[t, 0].astype(f32)) * HEAD_SCALE).astype(bf16)
            home_out[t, 1] = (kept[buf, 1] + wide_in[t, 1].astype(f32)).astype(bf16)
            dkv_ref[slab, :, t] = home_out[t, :, slab]
            for step in range(1, 4):
                home_copy(t, lax.rem(slab + step, 4)).start()

        def go(t, _):
            buf = lax.rem(t, 2)
            grads[buf] = jnp.zeros_like(grads[buf])
            slot_step(3, t, buf)

            @pl.when(t > 1)
            def _():
                wide_stage(t - 2, buf)

            @pl.when(t > 0)
            def _():
                near_stage(t - 1, 1 - buf)

            slot_step(0, t, buf)

            @pl.when(t == 0)
            def _():
                own.core_add(0, go_ref)
                own.x_copy(0).start()

            @pl.when(t == 1)
            def _():
                first.a_add(0)
                first.b_copy(0).start()

            @pl.when(t == 2)
            def _():
                rest.x_add(0)
                rest.a_copy(0).start()

            slot_step(2, t, buf)
            slot_step(1, t, buf)

            @pl.when(t > 1)
            def _():
                near_copy(t - 2).wait_send()

            for x in range(2):
                near_out[buf, x] = part(buf, x, 1 - core).astype(bf16)
            near_copy(t).start()
            return 0

        lax.fori_loop(0, STEPS, go, 0)
        wide_stage(STEPS - 2, STEPS % 2)
        near_stage(STEPS - 1, (STEPS - 1) % 2)
        rest.x_copy(1).start()
        rest.x_copy(2).start()
        for copy in loads:
            copy.wait()
        tile[...] = 0.5 * vec_ref[...]
        tile[3:5, :] = jnp.zeros_like(tile[3:5, :])
        normed, inverse = norm_stats(x[...])
        x[...] = normed
        inv_s[...] = inverse
        wide_stage(STEPS - 1, (STEPS - 1) % 2)
        rest.a_add(0)
        rest.b_copy(0).start()
        own.x_add(0)
        own.a_copy(0).start()
        gd_ref[:, : gd_ref.shape[1] // 2] = first.b_add(0)

        def finish(t, _):
            wide_copy(t).wait_send()
            for step in range(1, 4):
                k = lax.rem(slab + step, 4)
                home_copy(t, k).wait_send()
                slot = dkv_ref.at[k, :, t]
                remote(slot, slot, h_send.at[t, k], h_recv.at[t, k], at.dev(k, seat)).wait_recv()
            return 0

        lax.fori_loop(0, STEPS, finish, 0)
        near_copy(STEPS - 2).wait_send()
        near_copy(STEPS - 1).wait_send()
        for k in range(4):
            home = jnp.logical_and(slab == k, even)

            @pl.when(jnp.logical_not(home))
            def _():
                d_copy(k).wait_send()
                slot = dq_ref.at[k]
                remote(slot, slot, d_send.at[k], d_recv.at[k], at.dev(k, seat)).wait_recv()

        own.a_add(0)
        own.b_copy(0).start()

    pl.run_scoped(
        attention,
        pltpu.VMEM((2, 2, 4, 4, per, HEAD_DIM), f32),
        pltpu.VMEM((2, 2, 4, per, HEAD_DIM), f32),
    )

    def ending(dcat, ga):
        dcat[0] = heads_row(dq_ref, slice(None))
        for j in range(2):
            dcat[1 + j] = jnp.concatenate(
                [dkv_ref[h, j].reshape(rows, HEAD_DIM) for h in range(4)], axis=1
            )
        def side_part(c, _):
            part = pl.ds(pl.multiple_of(c * part_rows, part_rows), part_rows)
            made = (
                nt(dcat[0, part, :], wq[...])
                + nt(dcat[1, part, :], wk[...])
                + nt(dcat[2, part, :], wv[...])
            )
            bs[c] = made.astype(bf16)
            b_copy(c).start()
            tile[3:4, :] += jnp.sum(made * x[part, :], axis=0, keepdims=True)
            tile[4:5, :] += jnp.sum(made, axis=0, keepdims=True)
            return 0

        lax.fori_loop(0, CHUNKS, side_part, 0)
        total = Summed(at, tile, core_in, x_buf, x_in, z_buf, z_in, t_send, t_recv)
        total.one()
        for j in range(3):
            ga[j] = tn(n_one[...], dcat[j]).astype(bf16).reshape(ga.shape[1:])
            own.c_copy(j + 1, ga.at[j]).start()
            if j == 0:
                total.two()
            else:
                own.core_add(j, ga.at[j - 1])
                own.x_copy(j).start()
        own.core_add(3, ga.at[2])
        own.x_copy(3).start()
        rest.x_add(1)
        rest.a_copy(1).start()

        def side_sum(c, _):
            part = pl.ds(pl.multiple_of(c * part_rows, part_rows), part_rows)
            b_copy(c).wait()
            d_one = bs[c].astype(f32) + br[c].astype(f32)
            normed, inverse = x[part, :], inv_s[part, :]
            scaled = d_one * gain_ref[...]
            first_mean = jnp.mean(scaled, axis=-1, keepdims=True)
            second_mean = jnp.mean(scaled * normed, axis=-1, keepdims=True)
            ig_ref[part, :] = dh[part, :] + inverse * (scaled - first_mean - normed * second_mean)

            @pl.when(c == 0)
            def _():
                rest.a_add(1)
                rest.b_copy(1).start()

            @pl.when(c == CHUNKS // 4)
            def _():
                rest.x_add(2)
                rest.a_copy(2).start()
                total.three()

            @pl.when(c == 2 * CHUNKS // 4)
            def _():
                own.x_add(1)
                own.a_copy(1).start()
                rest.a_add(2)
                rest.b_copy(2).start()

            @pl.when(c == 3 * CHUNKS // 4)
            def _():
                own.x_add(2)
                own.a_copy(2).start()
                own.a_add(1)
                own.b_copy(1).start()

            return 0

        lax.fori_loop(0, CHUNKS, side_sum, 0)
        tile[...] = total.four()
        s_copy = remote(tile, side_in, s_sem.at[0], s_sem.at[1], at.other_side())
        s_copy.start()
        own.x_add(3)
        own.a_copy(3).start()
        own.a_add(2)
        own.b_copy(2).start()
        half = gu_ref.shape[1] // 2
        gd_ref[:, half:] = rest.b_add(0)
        for k in range(2):
            gu_ref[:, k * half : (k + 1) * half] = rest.b_add(1 + k)
        go_out[...] = own.b_add(0)
        own.a_add(3)
        own.b_copy(3).start()
        gq_ref[...] = own.b_add(1)
        gk_ref[...] = own.b_add(2)
        s_copy.wait()
        vsum_ref[...] = tile[...] + side_in[...]
        share = gq_ref.shape[0]
        for k in range(SEQ_DEV):

            @pl.when(at.pos == k)
            def _():
                for line, ref in ((3, g1_ref), (4, b1_ref), (0, g2_ref), (1, b2_ref)):
                    ref[...] = vsum_ref[line : line + 1, k * share : (k + 1) * share]

        loss_ref[...] = jnp.sum(vsum_ref[2:3, :], axis=1, keepdims=True) / (
            2.0 * cnt_ref[0:1, 0:1]
        )
        gv_ref[...] = own.b_add(3)
        for k in range(4):
            own.c_copy(k, go_ref if k == 0 else ga.at[k - 1]).wait_send()
            own.x_copy(k).wait_send()
            own.a_copy(k).wait_send()
            own.b_copy(k).wait_send()
        for k in range(3):
            rest.x_copy(k).wait_send()
            rest.a_copy(k).wait_send()
            rest.b_copy(k).wait_send()
        first.a_copy(0).wait_send()
        first.b_copy(0).wait_send()

    local = wq_hbm.shape[1]
    pl.run_scoped(
        ending,
        pltpu.VMEM((3, rows, local), bf16),
        pltpu.VMEM((3,) + go_ref.shape, bf16),
    )


def copy_kernel(count, *refs):
    ins, outs, held, load, store = (
        refs[:count], refs[count : 2 * count], refs[2 * count : 3 * count], refs[-2], refs[-1],
    )
    loads = [pltpu.make_async_copy(a, h, load.at[k]) for k, (a, h) in enumerate(zip(ins, held))]
    stores = [pltpu.make_async_copy(h, o, store.at[k]) for k, (h, o) in enumerate(zip(held, outs))]
    for copy in loads:
        copy.start()
    for one, two in zip(loads, stores):
        one.wait()
        two.start()
    for copy in stores:
        copy.wait()


def in_vmem():
    return pl.BlockSpec(memory_space=pltpu.VMEM)


def in_hbm():
    return pl.BlockSpec(memory_space=pl.ANY)


def dma(*shape):
    return pltpu.SemaphoreType.DMA(shape)


def call(kernel, name, ident, outs, ins, scratch, args, far=()):
    return pl.pallas_call(
        kernel,
        name=name,
        out_shape=outs,
        in_specs=ins,
        out_specs=tuple(in_hbm() if k in far else in_vmem() for k in range(len(outs))),
        scratch_shapes=scratch,
        compiler_params=pltpu.CompilerParams(
            collective_id=ident, has_side_effects=True, vmem_limit_bytes=62 * 2**20
        ),
        cost_estimate=pl.CostEstimate(flops=0, bytes_accessed=2**24, transcendentals=0),
    )(*args)


def per_device(
    inputs, ln1_gain, ln1_bias, w_query, w_key, w_value, w_out, ln2_gain, ln2_bias, w_up, w_down,
    teacher, valid_mask,
):
    rows, width = inputs.shape
    local = w_query.shape[1]
    heads = local // HEAD_DIM
    hidden_units = w_up.shape[1]
    dp_size = lax.axis_size("dp")
    single = dp_size == SEQ_DEV
    share = width // SEQ_DEV
    out = jax.ShapeDtypeStruct
    row = lambda vector: vector.reshape(1, width)
    step_rows = rows // STEPS
    part_rows = rows // CHUNKS

    n_one, kv_all, q_all, o_t, log_sum, ctx, count, wo_in = call(
        forward_kernel, "forward", 1,
        (
            out((rows, width), bf16),
            out((2, 4, 4, FSTEPS, rows // FSTEPS, HEAD_DIM), bf16),
            out((4, rows, HEAD_DIM), bf16),
            out((4, HEAD_DIM, rows), f32),
            out((4, 1, rows), f32),
            out((heads, rows, HEAD_DIM), bf16),
            out((8, 128), f32),
            out((local, width), bf16),
        ),
        [in_vmem()] * 3 + [in_hbm()] * 4 + [in_vmem()],
        [
            pltpu.VMEM((heads, 2, FSTEPS, rows // FSTEPS, HEAD_DIM), bf16),
            pltpu.VMEM((heads, rows, HEAD_DIM), bf16),
            pltpu.VMEM((4, rows, HEAD_DIM), bf16),
            pltpu.VMEM((4, 1, rows), f32),
            pltpu.VMEM((4, 1, rows), f32),
            dma(FSTEPS, 4), dma(FSTEPS, 4), dma(4), dma(4),
        ]
        + [dma(FSTEPS)] * 6
        + [dma(4)] * 2
        + [dma(2)]
        + [pltpu.VMEM((width, local), bf16)] * 3
        + [pltpu.VMEM((local, width), bf16), dma(4)]
        + summed_scratch((8, 128)),
        (
            inputs, row(ln1_gain), row(ln1_bias), w_query, w_key, w_value, w_out,
            valid_mask.reshape(1, rows),
        ),
    )
    if not single:
        count = jnp.full((8, 128), lax.psum(jnp.sum(valid_mask.astype(f32)), "dp"))
    share = width // SEQ_DEV
    split = (4, 2, 2, share)
    piece = hidden_units // 2
    output, d_hidden, do_all, part_one, part_two, grad_out_t, vectors = call(
        functools.partial(middle_kernel, float(rows * dp_size)), "middle", 2,
        (
            out((rows, width), f32),
            out((rows, width), f32),
            out((4, rows, HEAD_DIM), bf16),
            out((3, 4, 2, share, piece), bf16),
            out((1, 2, 2, share, piece), bf16),
            out((width, local), bf16),
            out((8, width), f32),
        ),
        [
            in_vmem(), in_hbm(), in_hbm(), in_hbm(), in_vmem(), in_vmem(), in_hbm(), in_hbm(),
            in_hbm(), in_vmem(), in_vmem(),
        ],
        [
            pltpu.VMEM((rows, width), f32),
            pltpu.VMEM((local, width), bf16),
            pltpu.VMEM((local, width), bf16),
            pltpu.VMEM((width, hidden_units), bf16),
            pltpu.VMEM((hidden_units, width), bf16),
            pltpu.VMEM((rows, width), f32),
            dma(6),
            pltpu.VMEM((heads, rows, HEAD_DIM), bf16),
            pltpu.VMEM((rows, width), f32),
            pltpu.VMEM((rows, 1), f32),
            pltpu.VMEM((rows, width), bf16),
            pltpu.VMEM((rows, hidden_units), bf16),
            pltpu.VMEM((rows, width), bf16),
            pltpu.VMEM((rows, hidden_units), bf16),
            pltpu.VMEM((rows, width), bf16),
            pltpu.VMEM((heads, rows, HEAD_DIM), bf16),
        ]
        + [pltpu.VMEM((CHUNKS, part_rows, width), bf16)] * 4
        + [dma(CHUNKS)] * 6
        + [dma(CHUNKS, 4)] * 2
        + [
            pltpu.VMEM((2,) + split + (piece,), bf16),
            pltpu.VMEM((4, 4, 2, share, piece), bf16),
            pltpu.VMEM((4, 4, 2, share, piece), bf16),
            pltpu.VMEM((1, 4, share, piece), bf16),
            dma(2, 4), dma(2, 4),
            pltpu.VMEM((rows, width), f32),
            dma(2),
        ],
        (
            ctx, inputs, w_out, wo_in, row(ln2_gain), row(ln2_bias), w_up, w_down, teacher,
            valid_mask.astype(f32).reshape(rows, 1), count,
        ),
        far=(0, 3),
    )
    (
        input_grad, grad_query, grad_key, grad_value, grad_out_t, grad_up, grad_down_t, gain_one,
        bias_one, gain_two, bias_two, loss, sums,
    ) = call(
        backward_kernel, "backward", 3,
        (out((rows, width), f32),)
        + (out((share, local), f32),) * 4
        + (out((share, hidden_units), f32),) * 2
        + (out((1, share), f32),) * 4
        + (out((1, 1), f32), out((8, width), f32)),
        [in_vmem()] * 8 + [in_hbm()] * 6 + [in_vmem()] * 3,
        [
            pltpu.VMEM((heads, rows, HEAD_DIM), bf16),
            pltpu.VMEM((heads, 2, STEPS, step_rows, HEAD_DIM), bf16),
            pltpu.VMEM((4, HEAD_DIM, rows), f32),
            pltpu.VMEM((4, 1, rows), f32),
            pltpu.VMEM((2, 2, 2, 4, step_rows, HEAD_DIM), bf16),
            pltpu.VMEM((2, 2, 2, 4, step_rows, HEAD_DIM), bf16),
            pltpu.VMEM((STEPS, 2, 4, step_rows, HEAD_DIM), bf16),
            pltpu.VMEM((STEPS, 2, 4, step_rows, HEAD_DIM), bf16),
            pltpu.VMEM((STEPS, 2, 4, step_rows, HEAD_DIM), bf16),
            pltpu.VMEM((4, rows, HEAD_DIM), bf16),
            dma(STEPS), dma(STEPS), dma(STEPS), dma(STEPS), dma(STEPS, 4), dma(STEPS, 4),
            dma(4), dma(4),
            pltpu.VMEM((1, 2, share, piece), bf16),
            pltpu.VMEM((1, 2, share, piece), bf16),
            pltpu.VMEM((1, share, piece), bf16),
            dma(4, 1), dma(4, 1),
            pltpu.VMEM((3, 4, share, piece), bf16),
            pltpu.VMEM((3, 2, 2, share, piece), bf16),
            pltpu.VMEM((3, 2, share, piece), bf16),
            pltpu.VMEM((3, 2, share, piece), bf16),
            pltpu.VMEM((3, share, piece), bf16),
            dma(4, 3), dma(4, 3),
            pltpu.VMEM((4, 4, 2, share, local), bf16),
            pltpu.VMEM((4, 4, 2, share, local), bf16),
            pltpu.VMEM((4, 4, share, local), bf16),
            pltpu.VMEM((4, 2, 2, share, local), bf16),
            pltpu.VMEM((4, 2, share, local), bf16),
            pltpu.VMEM((4, 2, share, local), bf16),
            pltpu.VMEM((4, share, local), bf16),
            dma(4, 4), dma(4, 4),
            pltpu.VMEM((CHUNKS, part_rows, width), bf16),
            pltpu.VMEM((CHUNKS, part_rows, width), bf16),
            dma(CHUNKS), dma(CHUNKS), dma(6),
            pltpu.VMEM((rows, width), bf16),
            pltpu.VMEM((width, local), bf16),
            pltpu.VMEM((width, local), bf16),
            pltpu.VMEM((width, local), bf16),
            pltpu.VMEM((rows, width), f32),
            pltpu.VMEM((rows, width), f32),
            pltpu.VMEM((rows, 1), f32),
            pltpu.VMEM((8, width), f32),
            dma(2),
        ]
        + summed_scratch((8, width)),
        (
            kv_all.reshape(2, 4, 4, STEPS, step_rows, HEAD_DIM), q_all, o_t, log_sum, do_all,
            part_one, part_two, grad_out_t.reshape(split + (local,)), n_one, w_query, w_key,
            w_value, inputs, d_hidden, row(ln1_gain), vectors, count,
        ),
    )
    if single:
        leaving = (
            output, input_grad, grad_query, grad_key, grad_value, grad_out_t, grad_up, grad_down_t,
            gain_one, bias_one, gain_two, bias_two, loss,
        )
        (
            output, input_grad, grad_query, grad_key, grad_value, grad_out_t, grad_up, grad_down_t,
            gain_one, bias_one, gain_two, bias_two, loss,
        ) = pl.pallas_call(
            functools.partial(copy_kernel, len(leaving)),
            name="leave",
            out_shape=tuple(out(array.shape, array.dtype) for array in leaving),
            in_specs=[in_hbm()] * len(leaving),
            out_specs=tuple(in_hbm() for _ in leaving),
            scratch_shapes=[pltpu.VMEM(array.shape, array.dtype) for array in leaving]
            + [dma(len(leaving)), dma(len(leaving))],
        )(*leaving)
    grad_down, grad_out = grad_down_t.T, grad_out_t.T
    small = [gain_one, bias_one, gain_two, bias_two]
    small = [vector.reshape(share) for vector in small]
    loss_value = loss.reshape(())
    if not single:
        index = lax.axis_index("dp")
        first = lax.rem(index, SEQ_DEV) * share

        def spread(part, axis):
            shape = list(part.shape)
            shape[axis] = width
            at = [0, 0]
            at[axis] = first
            placed = lax.dynamic_update_slice(jnp.zeros(shape, f32), part, tuple(at))
            return lax.psum_scatter(placed, "dp", scatter_dimension=axis, tiled=True)

        grad_query, grad_key, grad_value, grad_up = (
            spread(part, 0) for part in (grad_query, grad_key, grad_value, grad_up)
        )
        grad_out, grad_down = spread(grad_out, 1), spread(grad_down, 1)
        sums = lax.psum(jnp.where(first == 0, sums, 0.0), "dp")
        length = width // dp_size
        small = [lax.dynamic_slice(sums[k], (index * length,), (length,)) for k in (3, 4, 0, 1)]
        loss_value = jnp.sum(sums[2]) / (2.0 * count[0, 0])
    return (
        output, loss_value, input_grad, small[0], small[1], grad_query, grad_key, grad_value,
        grad_out, small[2], small[3], grad_up, grad_down,
    )


def solution(mesh):
    return jax.shard_map(
        per_device,
        mesh=mesh,
        in_specs=(
            P("dp", None), P(), P(), P(None, "tensor"), P(None, "tensor"), P(None, "tensor"),
            P("tensor", None), P(), P(), P(None, "tensor"), P("tensor", None), P("dp", None),
            P("dp"),
        ),
        out_specs=(
            P("dp", None), P(), P("dp", None), P("dp"), P("dp"), P("dp", "tensor"),
            P("dp", "tensor"), P("dp", "tensor"), P("tensor", "dp"), P("dp"), P("dp"),
            P("dp", "tensor"), P("tensor", "dp"),
        ),
        check_vma=False,
    )
```

```python
import functools

import jax
import jax.numpy as jnp
from jax import lax
from jax.experimental import pallas as pl
from jax.experimental.pallas import tpu as pltpu
from jax.sharding import PartitionSpec as P

HEAD_DIM = 128
SEQ_DEV = 16
EPSILON = 1e-05
NEGATIVE = -1e30
LOG_SCALE = 1.4426950408889634 * HEAD_DIM ** (-0.5)
HEAD_SCALE = HEAD_DIM ** (-0.5)
CHUNKS = 4
STEPS = 4
FSTEPS = 4
f32 = jnp.float32
bf16 = jnp.bfloat16


def nn(a, b):
    return lax.dot_general(a, b, (((1,), (0,)), ((), ())), preferred_element_type=f32)


def nt(a, b):
    return lax.dot_general(a, b, (((1,), (1,)), ((), ())), preferred_element_type=f32)


def tn(a, b):
    return lax.dot_general(a, b, (((0,), (0,)), ((), ())), preferred_element_type=f32)


def remote(src, dst, send_sem, recv_sem, device):
    return pltpu.make_async_remote_copy(
        src_ref=src,
        dst_ref=dst,
        send_sem=send_sem,
        recv_sem=recv_sem,
        device_id=device,
        device_id_type=pl.DeviceIdType.MESH,
    )


class Place:
    def __init__(self):
        index = lax.axis_index("dp")
        self.pos = lax.rem(index, SEQ_DEV)
        self.base = index - self.pos
        self.slab = lax.div(self.pos, 4)
        self.seat = lax.rem(self.pos, 4)
        self.side = lax.axis_index("tensor")
        seat = self.seat
        self.core_seat = seat + 1 - 2 * lax.rem(seat, 2)
        self.x_seat = lax.rem(seat + 2, 4)
        self.far_seat = 3 - seat

    def dev(self, slab, seat):
        return {"dp": self.base + slab * 4 + seat, "tensor": self.side}

    def other_side(self):
        return {"dp": self.base + self.pos, "tensor": 1 - self.side}

    def turned(self, slab):
        even = lax.rem(slab, 2) == 0
        return jnp.where(even, self.seat, self.far_seat)

    def peers(self, same, far, near, side):
        found = []
        for step in range(1, 4):
            other = lax.rem(self.slab + step, 4)
            if same:
                found.append(self.dev(other, self.seat))
            if far:
                found.append(self.dev(other, self.far_seat))
        if far:
            found.append(self.dev(self.slab, self.far_seat))
        if near:
            found.append(self.dev(self.slab, self.core_seat))
            found.append(self.dev(self.slab, self.x_seat))
        if side:
            found.append(self.other_side())
        return found


def greet(peers):
    barrier = pltpu.get_barrier_semaphore()
    for peer in peers:
        pl.semaphore_signal(
            barrier, inc=1, device_id=peer, device_id_type=pl.DeviceIdType.MESH
        )
    return functools.partial(pl.semaphore_wait, barrier, len(peers))


def norm_stats(values):
    average = jnp.mean(values, axis=-1, keepdims=True)
    centred = values - average
    inverse = lax.rsqrt(jnp.mean(centred * centred, axis=-1, keepdims=True) + EPSILON)
    return centred * inverse, inverse


class Summed:
    def __init__(self, at, tile, core_in, x_buf, x_in, z_buf, z_in, send, recv):
        self.at, self.tile = at, tile
        self.core_in, self.x_buf, self.x_in = core_in, x_buf, x_in
        self.z_buf, self.z_in = z_buf, z_in
        self.send, self.recv = send, recv

    def hop(self, src, dst, k, device):
        return remote(src, dst, self.send.at[k], self.recv.at[k], device)

    def near(self):
        at = self.at
        return self.hop(self.tile, self.core_in, 0, at.dev(at.slab, at.core_seat))

    def wide(self):
        at = self.at
        return self.hop(self.x_buf, self.x_in, 1, at.dev(at.slab, at.x_seat))

    def far(self, step):
        at = self.at
        device = at.dev(lax.rem(at.slab + step, 4), at.seat)
        return self.hop(self.z_buf, self.z_in.at[at.slab], 1 + step, device)

    def one(self):
        self.near().start()

    def two(self):
        self.near().wait()
        self.x_buf[...] = self.tile[...] + self.core_in[...]
        self.wide().start()

    def three(self):
        self.wide().wait()
        total = self.x_buf[...] + self.x_in[...]
        self.z_buf[...] = total
        self.z_in[self.at.slab] = total
        for step in range(1, 4):
            self.far(step).start()

    def four(self):
        at = self.at
        for step in range(1, 4):
            self.far(step).wait_send()
            source = lax.rem(at.slab - step + 4, 4)
            slot = self.z_in.at[source]
            self.hop(slot, slot, 1 + step, at.dev(source, at.seat)).wait_recv()
        return (self.z_in[0] + self.z_in[1]) + (self.z_in[2] + self.z_in[3])


def summed_scratch(shape):
    return [
        pltpu.VMEM(shape, f32),
        pltpu.VMEM(shape, f32),
        pltpu.VMEM(shape, f32),
        pltpu.VMEM(shape, f32),
        pltpu.VMEM(shape, f32),
        pltpu.VMEM((4,) + shape, f32),
        pltpu.SemaphoreType.DMA((5,)),
        pltpu.SemaphoreType.DMA((5,)),
    ]


class Scatter:
    def __init__(self, at, rc, s1, rx, s2, ra, s3, rb, send, recv):
        self.at = at
        self.core = lax.rem(at.seat, 2)
        self.wide = lax.div(at.seat, 2)
        self.low = lax.rem(at.slab, 2)
        self.high = lax.div(at.slab, 2)
        self.rc, self.s1, self.rx, self.s2 = rc, s1, rx, s2
        self.ra, self.s3, self.rb = ra, s3, rb
        self.send, self.recv = send, recv

    def hop(self, stage, k, src, dst, device):
        return remote(src, dst, self.send.at[stage, k], self.recv.at[stage, k], device)

    def c_copy(self, k, source):
        at = self.at
        device = at.dev(at.slab, at.core_seat)
        return self.hop(0, k, source.at[:, :, 1 - self.core], self.rc.at[k], device)

    def x_copy(self, k):
        at = self.at
        device = at.dev(at.slab, at.x_seat)
        return self.hop(1, k, self.s1.at[k, :, 1 - self.wide], self.rx.at[k], device)

    def a_copy(self, k):
        at = self.at
        device = at.dev(at.slab + 1 - 2 * self.low, at.seat)
        return self.hop(2, k, self.s2.at[k, :, 1 - self.low], self.ra.at[k], device)

    def b_copy(self, k):
        at = self.at
        device = at.dev(lax.rem(at.slab + 2, 4), at.seat)
        return self.hop(3, k, self.s3.at[k, 1 - self.high], self.rb.at[k], device)

    def core_add(self, k, source):
        self.c_copy(k, source).wait_recv()

        def one(i, _):
            self.s1[k, i] = (
                source[i, :, self.core].astype(f32) + self.rc[k, i].astype(f32)
            ).astype(bf16)
            return 0

        lax.fori_loop(0, 4, one, 0)

    def x_add(self, k):
        self.x_copy(k).wait_recv()
        for i in range(4):
            self.s2[k, i // 2, i % 2] = (
                self.s1[k, i, self.wide].astype(f32) + self.rx[k, i].astype(f32)
            ).astype(bf16)

    def a_add(self, k):
        self.a_copy(k).wait_recv()
        for i in range(2):
            self.s3[k, i] = (
                self.s2[k, i, self.low].astype(f32) + self.ra[k, i].astype(f32)
            ).astype(bf16)

    def b_add(self, k):
        self.b_copy(k).wait_recv()
        return self.s3[k, self.high].astype(f32) + self.rb[k].astype(f32)


def attend_mask(size, rows, per, step, mine):
    key = lax.broadcasted_iota(jnp.int32, (size, 1), 0)
    key = lax.div(key, per) * rows + lax.rem(key, per) + step * per
    query = lax.broadcasted_iota(jnp.int32, (1, rows), 1) + mine * rows
    return key <= query


def forward_kernel(
    x_ref, gain_ref, bias_ref, wq_hbm, wk_hbm, wv_hbm, wo_hbm, mask_ref,
    none_ref, kv_ref, q_ref, ot_ref, ls_ref, ctx_ref, cnt_ref, wo_in_ref,
    kvs, qs, os, top, low,
    z_send, z_recv, q_send, q_recv, c_send, c_recv, x_send, x_recv, f_send, f_recv,
    o_send, o_recv, w_sem, wq_ref, wk_ref, wv_ref, wo_ref, load,
    tile, core_in, x_buf, x_in, z_buf, z_in, t_send, t_recv,
):
    at = Place()
    rows = x_ref.shape[0]
    per = rows // FSTEPS
    slab, seat = at.slab, at.seat
    even = lax.rem(slab, 2) == 0
    odd = jnp.logical_not(even)
    goal = at.turned(slab)
    ready = greet(at.peers(True, True, True, True))
    loads = [
        pltpu.make_async_copy(src, dst, load.at[k])
        for k, (src, dst) in enumerate(
            ((wq_hbm, wq_ref), (wk_hbm, wk_ref), (wv_hbm, wv_ref), (wo_hbm, wo_ref))
        )
    ]
    for copy in loads:
        copy.start()

    def order(k):
        down = jnp.where(3 - k > slab, 3 - k, 2 - k)
        up = jnp.where(k < slab, k, k + 1)
        return jnp.where(slab < 2, down, up)

    def q_copy(h):
        return remote(qs.at[h], q_ref.at[slab], q_send.at[h], q_recv.at[slab], at.dev(h, goal))

    def kv_copy(h, t):
        return remote(
            kvs.at[h, :, t], kv_ref.at[:, slab, seat, t], z_send.at[t, h], z_recv.at[t, slab],
            at.dev(h, seat),
        )

    def near_copy(t):
        part = kv_ref.at[:, :, seat, t]
        return remote(part, part, c_send.at[t], c_recv.at[t], at.dev(slab, at.core_seat))

    def wide_copy(t):
        part = kv_ref.at[:, :, seat, t]
        return remote(part, part, x_send.at[t], x_recv.at[t], at.dev(slab, at.x_seat))

    def pass_copy(t):
        part = kv_ref.at[:, :, at.x_seat, t]
        return remote(part, part, f_send.at[t], f_recv.at[t], at.dev(slab, at.core_seat))

    normed, _ = norm_stats(x_ref[...])
    n_one = (normed * gain_ref[...] + bias_ref[...]).astype(bf16)
    none_ref[...] = n_one
    loads[0].wait()
    query = nn(n_one, wq_ref[...]).astype(bf16)
    for h in range(4):
        qs[h] = query[:, h * HEAD_DIM : (h + 1) * HEAD_DIM]
    ready()
    for k in range(3):
        q_copy(order(k)).start()

    @pl.when(even)
    def _():
        q_ref[slab] = qs[slab]

    @pl.when(odd)
    def _():
        q_copy(slab).start()

    for j, w_ref in enumerate((wk_ref, wv_ref)):
        loads[1 + j].wait()
        made = nn(none_ref[...], w_ref[...]).astype(bf16)
        for h in range(4):
            kvs[h, j] = made[:, h * HEAD_DIM : (h + 1) * HEAD_DIM].reshape(FSTEPS, per, HEAD_DIM)
    for t in range(FSTEPS):
        for k in range(3):
            kv_copy(order(k), t).start()
    kv_ref[:, slab, seat] = kvs[slab]
    loads[3].wait()
    w_copy = remote(wo_ref, wo_in_ref, w_sem.at[0], w_sem.at[1], at.other_side())
    w_copy.start()
    count = jnp.sum(mask_ref[...].astype(f32), axis=1, keepdims=True)
    tile[...] = jnp.broadcast_to(count, tile.shape)
    total = Summed(at, tile, core_in, x_buf, x_in, z_buf, z_in, t_send, t_recv)
    total.one()
    top[...] = jnp.full_like(top, NEGATIVE)
    low[...] = jnp.zeros_like(low)
    ot_ref[...] = jnp.zeros_like(ot_ref)

    def relay(t):
        for step in range(1, 4):
            source = lax.rem(slab + step, 4)
            part = kv_ref.at[:, source, seat, t]
            remote(
                part, part, z_send.at[t, source], z_recv.at[t, source], at.dev(source, seat)
            ).wait_recv()
        near_copy(t).start()
        wide_copy(t).start()

    def hand_on(t):
        part = kv_ref.at[:, :, at.x_seat, t]
        remote(part, part, x_send.at[t], x_recv.at[t], at.dev(slab, at.x_seat)).wait_recv()
        pass_copy(t).start()

    def arrive(t):
        device = at.dev(slab, at.core_seat)
        part = kv_ref.at[:, :, at.core_seat, t]
        remote(part, part, c_send.at[t], c_recv.at[t], device).wait_recv()
        part = kv_ref.at[:, :, at.far_seat, t]
        remote(part, part, f_send.at[t], f_recv.at[t], device).wait_recv()

    def unit(slot, parts):
        scored = []
        after = before = top[slot]
        for keys, _, allowed in parts:
            scores = nt(keys, q_ref[slot]) * LOG_SCALE
            if allowed is not None:
                scores = jnp.where(allowed, scores, NEGATIVE)
            after = jnp.maximum(after, jnp.max(scores, axis=0, keepdims=True))
            scored.append(scores)
        shrink = jnp.exp2(before - after)
        total_low = low[slot] * shrink
        total = ot_ref[slot] * shrink
        for scores, (_, values, _) in zip(scored, parts):
            prob = jnp.exp2(scores - after)
            total_low = total_low + jnp.sum(prob, axis=0, keepdims=True)
            total = total + tn(values, prob.astype(bf16))
        low[slot] = total_low
        top[slot] = after
        ot_ref[slot] = total

    def o_copy(slot):
        return remote(
            os.at[slot], ctx_ref.at[slab], o_send.at[slot], o_recv.at[slab],
            at.dev(slot, at.turned(slot)),
        )

    def slot_step(slot, t):
        mine = at.turned(slot)

        def taken(pick, size, allowed):
            keys = kv_ref[(0,) + pick + (t,)].reshape(size, HEAD_DIM)
            values = kv_ref[(1,) + pick + (t,)].reshape(size, HEAD_DIM)
            return keys, values, allowed

        for blocks, chosen in ((2, mine < 2), (4, mine >= 2)):

            @pl.when(chosen)
            def _():
                parts = []
                if slot > 0:
                    parts.append(taken((slice(0, slot), slice(0, 4)), 4 * slot * per, None))
                size = blocks * per
                allowed = attend_mask(size, rows, per, t, mine)
                parts.append(taken((slot, slice(0, blocks)), size, allowed))
                unit(slot, parts)

        @pl.when(t == FSTEPS - 1)
        def _():
            done = ot_ref[slot] / low[slot]
            ot_ref[slot] = done
            ls_ref[slot] = top[slot] + jnp.log2(low[slot])
            os[slot] = done.T.astype(bf16)
            home = jnp.logical_and(slab == slot, even)

            @pl.when(home)
            def _():
                ctx_ref[slab] = os[slot]

            @pl.when(jnp.logical_not(home))
            def _():
                o_copy(slot).start()

    for step in range(1, 4):
        source = lax.rem(slab + step, 4)
        part = q_ref.at[source]
        remote(
            part, part, q_send.at[source], q_recv.at[source], at.dev(source, seat)
        ).wait_recv()

    @pl.when(odd)
    def _():
        part = q_ref.at[slab]
        remote(part, part, q_send.at[slab], q_recv.at[slab], at.dev(slab, seat)).wait_recv()

    relay(0)
    total.two()
    relay(1)
    hand_on(0)

    def go(t, _):
        arrive(t)
        slot_step(3, t)

        @pl.when(t + 2 < FSTEPS)
        def _():
            relay(t + 2)

        @pl.when(t == 0)
        def _():
            total.three()

        slot_step(0, t)
        slot_step(2, t)

        @pl.when(t + 1 < FSTEPS)
        def _():
            hand_on(t + 1)

        slot_step(1, t)
        return 0

    lax.fori_loop(0, FSTEPS, go, 0)
    cnt_ref[...] = total.four()
    for k in range(3):
        q_copy(order(k)).wait_send()

    @pl.when(odd)
    def _():
        q_copy(slab).wait_send()

    def finish(t, _):
        for k in range(3):
            kv_copy(order(k), t).wait_send()
        near_copy(t).wait_send()
        wide_copy(t).wait_send()
        pass_copy(t).wait_send()
        return 0

    lax.fori_loop(0, FSTEPS, finish, 0)
    w_copy.wait()
    for k in range(4):
        home = jnp.logical_and(slab == k, even)

        @pl.when(jnp.logical_not(home))
        def _():
            o_copy(k).wait_send()
            part = ctx_ref.at[k]
            remote(part, part, o_send.at[k], o_recv.at[k], at.dev(k, seat)).wait_recv()


def heads_row(ref, rows_at):
    return jnp.concatenate([ref[h, rows_at, :] for h in range(4)], axis=1)


def middle_kernel(
    token_total,
    ctx_ref, x_hbm, wo_hbm, wo_in_hbm, gain_ref, bias_ref, wup_hbm, wdn_hbm, teach_hbm,
    mask_ref, cnt_ref,
    out_hbm, dh_ref, do_ref, one_hbm, two_ref, go_ref, vec_ref,
    x_buf, wo, wo_in, wup, wdn, teach, load,
    ctx_in, normed_s, inv_s, n2s, acts, gfs, dpres, gas, dcs,
    fs, fr, bs, br,
    e_send, e_recv, f_send, f_recv, b_send, b_recv, d_send, d_recv,
    gt, rc, s1, rx, g_send, g_recv, out_ref, store,
):
    at = Place()
    slab, seat = at.slab, at.seat
    rows = out_ref.shape[0]
    part_rows = rows // CHUNKS
    ready = greet(at.peers(True, True, True, True))
    loads = [
        pltpu.make_async_copy(src, dst, load.at[k])
        for k, (src, dst) in enumerate(
            (
                (wo_hbm, wo), (wo_in_hbm, wo_in), (x_hbm, x_buf), (wup_hbm, wup),
                (wdn_hbm, wdn), (teach_hbm, teach),
            )
        )
    ]
    for copy in loads:
        copy.start()
    ready()

    def e_copy(c):
        part = pl.ds(pl.multiple_of(c * part_rows, part_rows), part_rows)
        return remote(
            ctx_ref.at[:, part, :], ctx_in.at[:, part, :], e_send.at[c], e_recv.at[c],
            at.other_side(),
        )

    def f_copy(c):
        return remote(fs.at[c], fr.at[c], f_send.at[c], f_recv.at[c], at.other_side())

    def b_copy(c):
        return remote(bs.at[c], br.at[c], b_send.at[c], b_recv.at[c], at.other_side())

    for c in range(CHUNKS):
        e_copy(c).start()
    for k in range(3):
        loads[k].wait()

    def forward(c, _):
        part = pl.ds(pl.multiple_of(c * part_rows, part_rows), part_rows)
        e_copy(c).wait()
        hidden = x_buf[part, :] + (
            nn(heads_row(ctx_ref, part), wo[...]) + nn(heads_row(ctx_in, part), wo_in[...])
        )
        out_ref[part, :] = hidden
        normed, inverse = norm_stats(hidden)
        normed_s[part, :] = normed
        inv_s[part, :] = inverse
        n_two = (normed * gain_ref[...] + bias_ref[...]).astype(bf16)
        n2s[part, :] = n_two

        @pl.when(c == 0)
        def _():
            loads[3].wait()
            loads[4].wait()

        active = jnp.maximum(nn(n_two, wup[...]), 0.0).astype(bf16)
        acts[part, :] = active
        fs[c] = nn(active, wdn[...]).astype(bf16)
        f_copy(c).start()
        return 0

    lax.fori_loop(0, CHUNKS, forward, 0)
    loads[5].wait()
    scale = token_total / cnt_ref[0:1, 0:1]
    vec_ref[...] = jnp.zeros_like(vec_ref)

    def back_one(c, _):
        part = pl.ds(pl.multiple_of(c * part_rows, part_rows), part_rows)
        f_copy(c).wait()
        output = out_ref[part, :] + (fs[c].astype(f32) + fr[c].astype(f32))
        out_ref[part, :] = output
        misfit = output - teach[part, :]
        held = misfit * mask_ref[part, :]
        vec_ref[2:3, :] += jnp.sum(held * misfit, axis=0, keepdims=True)
        d_output = scale * held
        dh_ref[part, :] = d_output
        g_ffn = d_output.astype(bf16)
        gfs[part, :] = g_ffn
        d_active = nt(g_ffn, wdn[...])
        d_pre = jnp.where(acts[part, :] > 0, d_active, 0.0).astype(bf16)
        dpres[part, :] = d_pre
        bs[c] = nt(d_pre, wup[...]).astype(bf16)
        b_copy(c).start()
        return 0

    lax.fori_loop(0, CHUNKS, back_one, 0)
    scatter = Scatter(at, rc, s1, rx, two_ref, None, None, None, g_send, g_recv)
    split = gt.shape[1:5]
    half = gt.shape[5] // 2
    for k in range(4):
        slot = gt.at[k % 2]
        if k >= 2:
            scatter.c_copy(k - 2, slot).wait_send()
        left, right = (gfs, acts) if k < 2 else (n2s, dpres)

        def columns(j, _):
            cols = pl.ds(pl.multiple_of((k % 2) * 2 * half + j * half, half), half)
            kept = pl.ds(pl.multiple_of(j * half, half), half)
            made = tn(left[...], right[:, cols]).astype(bf16)
            gt[k % 2, :, :, :, :, kept] = made.reshape(split + (half,))
            return 0

        lax.fori_loop(0, 2, columns, 0)
        scatter.c_copy(k, slot).start()
        if k >= 1:
            scatter.core_add(k - 1, gt.at[(k - 1) % 2])
            if k == 1:
                scatter.x_copy(0).start()
    scatter.core_add(3, gt.at[1])
    scatter.c_copy(2, gt.at[0]).wait_send()
    scatter.c_copy(3, gt.at[1]).wait_send()
    stores = [
        pltpu.make_async_copy(out_ref, out_hbm, store.at[0]),
        pltpu.make_async_copy(s1.at[1:4], one_hbm, store.at[1]),
    ]
    for copy in stores:
        copy.start()

    def d_copy(c, h):
        part = pl.ds(pl.multiple_of(c * part_rows, part_rows), part_rows)
        return remote(
            dcs.at[h, part, :], do_ref.at[slab, part, :], d_send.at[c, h], d_recv.at[c, slab],
            at.dev(h, at.turned(slab)),
        )

    even = lax.rem(slab, 2) == 0

    def back_two(c, _):
        part = pl.ds(pl.multiple_of(c * part_rows, part_rows), part_rows)
        b_copy(c).wait()
        d_two = bs[c].astype(f32) + br[c].astype(f32)
        normed = normed_s[part, :]
        scaled = d_two * gain_ref[...]
        first = jnp.mean(scaled, axis=-1, keepdims=True)
        second = jnp.mean(scaled * normed, axis=-1, keepdims=True)
        d_hidden = dh_ref[part, :] + inv_s[part, :] * (scaled - first - normed * second)
        vec_ref[0:1, :] += jnp.sum(d_two * normed, axis=0, keepdims=True)
        vec_ref[1:2, :] += jnp.sum(d_two, axis=0, keepdims=True)
        dh_ref[part, :] = d_hidden
        g_attn = d_hidden.astype(bf16)
        gas[part, :] = g_attn
        d_context = nt(g_attn, wo[...]).astype(bf16)
        for h in range(4):
            dcs[h, part, :] = d_context[:, h * HEAD_DIM : (h + 1) * HEAD_DIM]
            home = jnp.logical_and(slab == h, even)

            @pl.when(home)
            def _():
                do_ref[slab, part, :] = dcs[h, part, :]

            @pl.when(jnp.logical_not(home))
            def _():
                d_copy(c, h).start()

        return 0

    lax.fori_loop(0, CHUNKS, back_two, 0)
    go_ref[...] = tn(gas[...], heads_row(ctx_ref, slice(None))).astype(bf16)
    scatter.x_add(0)
    scatter.x_copy(0).wait_send()
    for copy in stores:
        copy.wait()

    def finish(c, _):
        part = pl.ds(pl.multiple_of(c * part_rows, part_rows), part_rows)
        for h in range(4):
            home = jnp.logical_and(slab == h, even)

            @pl.when(jnp.logical_not(home))
            def _():
                d_copy(c, h).wait_send()
                slot = do_ref.at[h, part, :]
                remote(
                    slot, slot, d_send.at[c, h], d_recv.at[c, h], at.dev(h, seat)
                ).wait_recv()

        return 0

    lax.fori_loop(0, CHUNKS, finish, 0)


def backward_kernel(
    kv_ref, q_ref, ot_ref, ls_ref, do_ref, part_one, part_two, go_ref,
    n_one_hbm, wq_hbm, wk_hbm, wv_hbm, x_hbm, dh_hbm, gain_ref, vec_ref, cnt_ref,
    ig_ref, gq_ref, gk_ref, gv_ref, go_out, gu_ref, gd_ref, g1_ref, b1_ref, g2_ref, b2_ref,
    loss_ref, vsum_ref,
    dq_ref, dkv_ref, acc, delta, near_out, near_in, wide_out, wide_in, home_out, dqs,
    n_send, n_recv, w_send, w_recv, h_send, h_recv, d_send, d_recv,
    a_one, s3_one, b_one, one_send, one_recv,
    rx, s2, ra, s3, rb, two_send, two_recv,
    gc, g1, gx, g2, gg, g3, gb, g_send, g_recv, bs, br,
    b_send, b_recv, load, n_one, wq, wk, wv, x, dh, inv_s, side_in, s_sem,
    tile, core_in, x_buf, x_in, z_buf, z_in, t_send, t_recv,
):
    at = Place()
    slab, seat = at.slab, at.seat
    core, wide = lax.rem(seat, 2), lax.div(seat, 2)
    rows = q_ref.shape[1]
    per = rows // STEPS
    part_rows = rows // CHUNKS
    even = lax.rem(slab, 2) == 0
    ready = greet(at.peers(True, True, True, True))
    first = Scatter(at, None, None, None, part_two, a_one, s3_one, b_one, one_send, one_recv)
    rest = Scatter(at, None, part_one, rx, s2, ra, s3, rb, two_send, two_recv)
    own = Scatter(at, gc, g1, gx, g2, gg, g3, gb, g_send, g_recv)
    loads = [
        pltpu.make_async_copy(src, dst, load.at[k])
        for k, (src, dst) in enumerate(
            (
                (wq_hbm, wq), (wk_hbm, wk), (wv_hbm, wv), (n_one_hbm, n_one), (x_hbm, x),
                (dh_hbm, dh),
            )
        )
    ]
    for copy in loads:
        copy.start()
    acc[...] = jnp.zeros_like(acc)
    for slot in range(4):
        delta[slot] = jnp.sum(do_ref[slot].astype(f32).T * ot_ref[slot], axis=0, keepdims=True)
    ready()
    own.c_copy(0, go_ref).start()
    first.a_copy(0).start()
    rest.x_copy(0).start()

    def b_copy(c):
        return remote(bs.at[c], br.at[c], b_send.at[c], b_recv.at[c], at.other_side())

    def attention(grads, kept):
        def unit(slot, t, buf, start, slabs, blocks, allowed):
            size = slabs * blocks * per
            pick = (slice(start, start + slabs), slice(0, blocks))
            keys = kv_ref[(0,) + pick + (t,)].reshape(size, HEAD_DIM)
            values = kv_ref[(1,) + pick + (t,)].reshape(size, HEAD_DIM)
            query = q_ref[slot]
            d_out = do_ref[slot]
            scores = nt(keys, query) * LOG_SCALE - ls_ref[slot]
            if allowed is not None:
                scores = jnp.where(allowed, scores, NEGATIVE)
            prob = jnp.exp2(scores)
            d_probs = nt(values, d_out)
            d_scores = (prob * (d_probs - delta[slot])).astype(bf16)
            shape = (slabs, blocks, per, HEAD_DIM)
            grads[(buf, 1) + pick] += nn(prob.astype(bf16), d_out).reshape(shape)
            grads[(buf, 0) + pick] += nn(d_scores, query).reshape(shape)
            acc[slot] += tn(keys, d_scores)

        def d_copy(slot):
            return remote(
                dqs.at[slot], dq_ref.at[slab], d_send.at[slot], d_recv.at[slab],
                at.dev(slot, at.turned(slot)),
            )

        def slot_step(slot, t, buf):
            if slot > 0:
                unit(slot, t, buf, 0, slot, 4, None)
            mine = at.turned(slot)
            for blocks, chosen in ((2, mine < 2), (4, mine >= 2)):

                @pl.when(chosen)
                def _():
                    allowed = attend_mask(blocks * per, rows, per, t, mine)
                    unit(slot, t, buf, slot, 1, blocks, allowed)

            @pl.when(t == STEPS - 1)
            def _():
                dqs[slot] = (acc[slot] * HEAD_SCALE).T.astype(bf16)
                home = jnp.logical_and(slab == slot, even)

                @pl.when(home)
                def _():
                    dq_ref[slab] = dqs[slot]

                @pl.when(jnp.logical_not(home))
                def _():
                    d_copy(slot).start()

        def part(buf, x, c):
            return grads[buf, :, :, 2 * x + c]

        def near_copy(t):
            return remote(
                near_out.at[lax.rem(t, 2)], near_in.at[lax.rem(t, 2)], n_send.at[t], n_recv.at[t], at.dev(slab, at.core_seat)
            )

        def wide_copy(t):
            return remote(
                wide_out.at[t], wide_in.at[t], w_send.at[t], w_recv.at[t], at.dev(slab, at.x_seat)
            )

        def home_copy(t, k):
            return remote(
                home_out.at[t, :, k], dkv_ref.at[slab, :, t], h_send.at[t, k], h_recv.at[t, slab],
                at.dev(k, seat),
            )

        def near_stage(t, buf):
            near_copy(t).wait_recv()
            wide_out[t] = (part(buf, 1 - wide, core) + near_in[buf, 1 - wide].astype(f32)).astype(bf16)
            wide_copy(t).start()
            kept[buf] = part(buf, wide, core) + near_in[buf, wide].astype(f32)

        def wide_stage(t, buf):
            wide_copy(t).wait_recv()
            home_out[t, 0] = ((kept[buf, 0] + wide_in[t, 0].astype(f32)) * HEAD_SCALE).astype(bf16)
            home_out[t, 1] = (kept[buf, 1] + wide_in[t, 1].astype(f32)).astype(bf16)
            dkv_ref[slab, :, t] = home_out[t, :, slab]
            for step in range(1, 4):
                home_copy(t, lax.rem(slab + step, 4)).start()

        def go(t, _):
            buf = lax.rem(t, 2)
            grads[buf] = jnp.zeros_like(grads[buf])
            slot_step(3, t, buf)

            @pl.when(t > 1)
            def _():
                wide_stage(t - 2, buf)

            @pl.when(t > 0)
            def _():
                near_stage(t - 1, 1 - buf)

            slot_step(0, t, buf)

            @pl.when(t == 0)
            def _():
                own.core_add(0, go_ref)
                own.x_copy(0).start()

            @pl.when(t == 1)
            def _():
                first.a_add(0)
                first.b_copy(0).start()

            @pl.when(t == 2)
            def _():
                rest.x_add(0)
                rest.a_copy(0).start()

            slot_step(2, t, buf)
            slot_step(1, t, buf)

            @pl.when(t > 1)
            def _():
                near_copy(t - 2).wait_send()

            for x in range(2):
                near_out[buf, x] = part(buf, x, 1 - core).astype(bf16)
            near_copy(t).start()
            return 0

        lax.fori_loop(0, STEPS, go, 0)
        wide_stage(STEPS - 2, STEPS % 2)
        near_stage(STEPS - 1, (STEPS - 1) % 2)
        rest.x_copy(1).start()
        rest.x_copy(2).start()
        for copy in loads:
            copy.wait()
        tile[...] = 0.5 * vec_ref[...]
        tile[3:5, :] = jnp.zeros_like(tile[3:5, :])
        normed, inverse = norm_stats(x[...])
        x[...] = normed
        inv_s[...] = inverse
        wide_stage(STEPS - 1, (STEPS - 1) % 2)
        rest.a_add(0)
        rest.b_copy(0).start()
        own.x_add(0)
        own.a_copy(0).start()
        gd_ref[:, : gd_ref.shape[1] // 2] = first.b_add(0)

        def finish(t, _):
            wide_copy(t).wait_send()
            for step in range(1, 4):
                k = lax.rem(slab + step, 4)
                home_copy(t, k).wait_send()
                slot = dkv_ref.at[k, :, t]
                remote(slot, slot, h_send.at[t, k], h_recv.at[t, k], at.dev(k, seat)).wait_recv()
            return 0

        lax.fori_loop(0, STEPS, finish, 0)
        near_copy(STEPS - 2).wait_send()
        near_copy(STEPS - 1).wait_send()
        for k in range(4):
            home = jnp.logical_and(slab == k, even)

            @pl.when(jnp.logical_not(home))
            def _():
                d_copy(k).wait_send()
                slot = dq_ref.at[k]
                remote(slot, slot, d_send.at[k], d_recv.at[k], at.dev(k, seat)).wait_recv()

        own.a_add(0)
        own.b_copy(0).start()

    pl.run_scoped(
        attention,
        pltpu.VMEM((2, 2, 4, 4, per, HEAD_DIM), f32),
        pltpu.VMEM((2, 2, 4, per, HEAD_DIM), f32),
    )

    def ending(dcat, ga):
        dcat[0] = heads_row(dq_ref, slice(None))
        for j in range(2):
            dcat[1 + j] = jnp.concatenate(
                [dkv_ref[h, j].reshape(rows, HEAD_DIM) for h in range(4)], axis=1
            )
        def side_part(c, _):
            part = pl.ds(pl.multiple_of(c * part_rows, part_rows), part_rows)
            made = (
                nt(dcat[0, part, :], wq[...])
                + nt(dcat[1, part, :], wk[...])
                + nt(dcat[2, part, :], wv[...])
            )
            bs[c] = made.astype(bf16)
            b_copy(c).start()
            tile[3:4, :] += jnp.sum(made * x[part, :], axis=0, keepdims=True)
            tile[4:5, :] += jnp.sum(made, axis=0, keepdims=True)
            return 0

        lax.fori_loop(0, CHUNKS, side_part, 0)
        total = Summed(at, tile, core_in, x_buf, x_in, z_buf, z_in, t_send, t_recv)
        total.one()
        def weight_part(j, _):
            ga[j] = tn(n_one[...], dcat[j]).astype(bf16).reshape(ga.shape[1:])
            own.c_copy(j + 1, ga.at[j]).start()

            @pl.when(j == 0)
            def _():
                total.two()

            @pl.when(j > 0)
            def _():
                own.core_add(j, ga.at[jnp.maximum(j - 1, 0)])
                own.x_copy(j).start()

            return 0

        lax.fori_loop(0, 3, weight_part, 0)
        own.core_add(3, ga.at[2])
        own.x_copy(3).start()
        rest.x_add(1)
        rest.a_copy(1).start()

        def side_sum(c, _):
            part = pl.ds(pl.multiple_of(c * part_rows, part_rows), part_rows)
            b_copy(c).wait()
            d_one = bs[c].astype(f32) + br[c].astype(f32)
            normed, inverse = x[part, :], inv_s[part, :]
            scaled = d_one * gain_ref[...]
            first_mean = jnp.mean(scaled, axis=-1, keepdims=True)
            second_mean = jnp.mean(scaled * normed, axis=-1, keepdims=True)
            ig_ref[part, :] = dh[part, :] + inverse * (scaled - first_mean - normed * second_mean)

            @pl.when(c == 0)
            def _():
                rest.a_add(1)
                rest.b_copy(1).start()

            @pl.when(c == CHUNKS // 4)
            def _():
                rest.x_add(2)
                rest.a_copy(2).start()
                total.three()

            @pl.when(c == 2 * CHUNKS // 4)
            def _():
                own.x_add(1)
                own.a_copy(1).start()
                rest.a_add(2)
                rest.b_copy(2).start()

            @pl.when(c == 3 * CHUNKS // 4)
            def _():
                own.x_add(2)
                own.a_copy(2).start()
                own.a_add(1)
                own.b_copy(1).start()

            return 0

        lax.fori_loop(0, CHUNKS, side_sum, 0)
        tile[...] = total.four()
        s_copy = remote(tile, side_in, s_sem.at[0], s_sem.at[1], at.other_side())
        s_copy.start()
        own.x_add(3)
        own.a_copy(3).start()
        own.a_add(2)
        own.b_copy(2).start()
        half = gu_ref.shape[1] // 2
        gd_ref[:, half:] = rest.b_add(0)
        for k in range(2):
            gu_ref[:, k * half : (k + 1) * half] = rest.b_add(1 + k)
        go_out[...] = own.b_add(0)
        own.a_add(3)
        own.b_copy(3).start()
        gq_ref[...] = own.b_add(1)
        gk_ref[...] = own.b_add(2)
        s_copy.wait()
        vsum_ref[...] = tile[...] + side_in[...]
        share = gq_ref.shape[0]
        for k in range(SEQ_DEV):

            @pl.when(at.pos == k)
            def _():
                for line, ref in ((3, g1_ref), (4, b1_ref), (0, g2_ref), (1, b2_ref)):
                    ref[...] = vsum_ref[line : line + 1, k * share : (k + 1) * share]

        loss_ref[...] = jnp.sum(vsum_ref[2:3, :], axis=1, keepdims=True) / (
            2.0 * cnt_ref[0:1, 0:1]
        )
        gv_ref[...] = own.b_add(3)
        for k in range(4):
            own.c_copy(k, go_ref if k == 0 else ga.at[k - 1]).wait_send()
            own.x_copy(k).wait_send()
            own.a_copy(k).wait_send()
            own.b_copy(k).wait_send()
        for k in range(3):
            rest.x_copy(k).wait_send()
            rest.a_copy(k).wait_send()
            rest.b_copy(k).wait_send()
        first.a_copy(0).wait_send()
        first.b_copy(0).wait_send()

    local = wq_hbm.shape[1]
    pl.run_scoped(
        ending,
        pltpu.VMEM((3, rows, local), bf16),
        pltpu.VMEM((3,) + go_ref.shape, bf16),
    )


def copy_kernel(count, *refs):
    ins, outs, held, load, store = (
        refs[:count], refs[count : 2 * count], refs[2 * count : 3 * count], refs[-2], refs[-1],
    )
    loads = [pltpu.make_async_copy(a, h, load.at[k]) for k, (a, h) in enumerate(zip(ins, held))]
    stores = [pltpu.make_async_copy(h, o, store.at[k]) for k, (h, o) in enumerate(zip(held, outs))]
    for copy in loads:
        copy.start()
    for one, two in zip(loads, stores):
        one.wait()
        two.start()
    for copy in stores:
        copy.wait()


def in_vmem():
    return pl.BlockSpec(memory_space=pltpu.VMEM)


def in_hbm():
    return pl.BlockSpec(memory_space=pl.ANY)


def dma(*shape):
    return pltpu.SemaphoreType.DMA(shape)


def call(kernel, name, ident, outs, ins, scratch, args, far=()):
    return pl.pallas_call(
        kernel,
        name=name,
        out_shape=outs,
        in_specs=ins,
        out_specs=tuple(in_hbm() if k in far else in_vmem() for k in range(len(outs))),
        scratch_shapes=scratch,
        compiler_params=pltpu.CompilerParams(
            collective_id=ident, has_side_effects=True, vmem_limit_bytes=62 * 2**20
        ),
        cost_estimate=pl.CostEstimate(flops=0, bytes_accessed=2**24, transcendentals=0),
    )(*args)


def per_device(
    inputs, ln1_gain, ln1_bias, w_query, w_key, w_value, w_out, ln2_gain, ln2_bias, w_up, w_down,
    teacher, valid_mask,
):
    rows, width = inputs.shape
    local = w_query.shape[1]
    heads = local // HEAD_DIM
    hidden_units = w_up.shape[1]
    dp_size = lax.axis_size("dp")
    single = dp_size == SEQ_DEV
    share = width // SEQ_DEV
    out = jax.ShapeDtypeStruct
    row = lambda vector: vector.reshape(1, width)
    step_rows = rows // STEPS
    part_rows = rows // CHUNKS

    n_one, kv_all, q_all, o_t, log_sum, ctx, count, wo_in = call(
        forward_kernel, "forward", 1,
        (
            out((rows, width), bf16),
            out((2, 4, 4, FSTEPS, rows // FSTEPS, HEAD_DIM), bf16),
            out((4, rows, HEAD_DIM), bf16),
            out((4, HEAD_DIM, rows), f32),
            out((4, 1, rows), f32),
            out((heads, rows, HEAD_DIM), bf16),
            out((8, 128), f32),
            out((local, width), bf16),
        ),
        [in_vmem()] * 3 + [in_hbm()] * 4 + [in_vmem()],
        [
            pltpu.VMEM((heads, 2, FSTEPS, rows // FSTEPS, HEAD_DIM), bf16),
            pltpu.VMEM((heads, rows, HEAD_DIM), bf16),
            pltpu.VMEM((4, rows, HEAD_DIM), bf16),
            pltpu.VMEM((4, 1, rows), f32),
            pltpu.VMEM((4, 1, rows), f32),
            dma(FSTEPS, 4), dma(FSTEPS, 4), dma(4), dma(4),
        ]
        + [dma(FSTEPS)] * 6
        + [dma(4)] * 2
        + [dma(2)]
        + [pltpu.VMEM((width, local), bf16)] * 3
        + [pltpu.VMEM((local, width), bf16), dma(4)]
        + summed_scratch((8, 128)),
        (
            inputs, row(ln1_gain), row(ln1_bias), w_query, w_key, w_value, w_out,
            valid_mask.reshape(1, rows),
        ),
    )
    if not single:
        count = jnp.full((8, 128), lax.psum(jnp.sum(valid_mask.astype(f32)), "dp"))
    share = width // SEQ_DEV
    split = (4, 2, 2, share)
    piece = hidden_units // 2
    output, d_hidden, do_all, part_one, part_two, grad_out_t, vectors = call(
        functools.partial(middle_kernel, float(rows * dp_size)), "middle", 2,
        (
            out((rows, width), f32),
            out((rows, width), f32),
            out((4, rows, HEAD_DIM), bf16),
            out((3, 4, 2, share, piece), bf16),
            out((1, 2, 2, share, piece), bf16),
            out((width, local), bf16),
            out((8, width), f32),
        ),
        [
            in_vmem(), in_hbm(), in_hbm(), in_hbm(), in_vmem(), in_vmem(), in_hbm(), in_hbm(),
            in_hbm(), in_vmem(), in_vmem(),
        ],
        [
            pltpu.VMEM((rows, width), f32),
            pltpu.VMEM((local, width), bf16),
            pltpu.VMEM((local, width), bf16),
            pltpu.VMEM((width, hidden_units), bf16),
            pltpu.VMEM((hidden_units, width), bf16),
            pltpu.VMEM((rows, width), f32),
            dma(6),
            pltpu.VMEM((heads, rows, HEAD_DIM), bf16),
            pltpu.VMEM((rows, width), f32),
            pltpu.VMEM((rows, 1), f32),
            pltpu.VMEM((rows, width), bf16),
            pltpu.VMEM((rows, hidden_units), bf16),
            pltpu.VMEM((rows, width), bf16),
            pltpu.VMEM((rows, hidden_units), bf16),
            pltpu.VMEM((rows, width), bf16),
            pltpu.VMEM((heads, rows, HEAD_DIM), bf16),
        ]
        + [pltpu.VMEM((CHUNKS, part_rows, width), bf16)] * 4
        + [dma(CHUNKS)] * 6
        + [dma(CHUNKS, 4)] * 2
        + [
            pltpu.VMEM((2,) + split + (piece,), bf16),
            pltpu.VMEM((4, 4, 2, share, piece), bf16),
            pltpu.VMEM((4, 4, 2, share, piece), bf16),
            pltpu.VMEM((1, 4, share, piece), bf16),
            dma(2, 4), dma(2, 4),
            pltpu.VMEM((rows, width), f32),
            dma(2),
        ],
        (
            ctx, inputs, w_out, wo_in, row(ln2_gain), row(ln2_bias), w_up, w_down, teacher,
            valid_mask.astype(f32).reshape(rows, 1), count,
        ),
        far=(0, 3),
    )
    (
        input_grad, grad_query, grad_key, grad_value, grad_out_t, grad_up, grad_down_t, gain_one,
        bias_one, gain_two, bias_two, loss, sums,
    ) = call(
        backward_kernel, "backward", 3,
        (out((rows, width), f32),)
        + (out((share, local), f32),) * 4
        + (out((share, hidden_units), f32),) * 2
        + (out((1, share), f32),) * 4
        + (out((1, 1), f32), out((8, width), f32)),
        [in_vmem()] * 8 + [in_hbm()] * 6 + [in_vmem()] * 3,
        [
            pltpu.VMEM((heads, rows, HEAD_DIM), bf16),
            pltpu.VMEM((heads, 2, STEPS, step_rows, HEAD_DIM), bf16),
            pltpu.VMEM((4, HEAD_DIM, rows), f32),
            pltpu.VMEM((4, 1, rows), f32),
            pltpu.VMEM((2, 2, 2, 4, step_rows, HEAD_DIM), bf16),
            pltpu.VMEM((2, 2, 2, 4, step_rows, HEAD_DIM), bf16),
            pltpu.VMEM((STEPS, 2, 4, step_rows, HEAD_DIM), bf16),
            pltpu.VMEM((STEPS, 2, 4, step_rows, HEAD_DIM), bf16),
            pltpu.VMEM((STEPS, 2, 4, step_rows, HEAD_DIM), bf16),
            pltpu.VMEM((4, rows, HEAD_DIM), bf16),
            dma(STEPS), dma(STEPS), dma(STEPS), dma(STEPS), dma(STEPS, 4), dma(STEPS, 4),
            dma(4), dma(4),
            pltpu.VMEM((1, 2, share, piece), bf16),
            pltpu.VMEM((1, 2, share, piece), bf16),
            pltpu.VMEM((1, share, piece), bf16),
            dma(4, 1), dma(4, 1),
            pltpu.VMEM((3, 4, share, piece), bf16),
            pltpu.VMEM((3, 2, 2, share, piece), bf16),
            pltpu.VMEM((3, 2, share, piece), bf16),
            pltpu.VMEM((3, 2, share, piece), bf16),
            pltpu.VMEM((3, share, piece), bf16),
            dma(4, 3), dma(4, 3),
            pltpu.VMEM((4, 4, 2, share, local), bf16),
            pltpu.VMEM((4, 4, 2, share, local), bf16),
            pltpu.VMEM((4, 4, share, local), bf16),
            pltpu.VMEM((4, 2, 2, share, local), bf16),
            pltpu.VMEM((4, 2, share, local), bf16),
            pltpu.VMEM((4, 2, share, local), bf16),
            pltpu.VMEM((4, share, local), bf16),
            dma(4, 4), dma(4, 4),
            pltpu.VMEM((CHUNKS, part_rows, width), bf16),
            pltpu.VMEM((CHUNKS, part_rows, width), bf16),
            dma(CHUNKS), dma(CHUNKS), dma(6),
            pltpu.VMEM((rows, width), bf16),
            pltpu.VMEM((width, local), bf16),
            pltpu.VMEM((width, local), bf16),
            pltpu.VMEM((width, local), bf16),
            pltpu.VMEM((rows, width), f32),
            pltpu.VMEM((rows, width), f32),
            pltpu.VMEM((rows, 1), f32),
            pltpu.VMEM((8, width), f32),
            dma(2),
        ]
        + summed_scratch((8, width)),
        (
            kv_all.reshape(2, 4, 4, STEPS, step_rows, HEAD_DIM), q_all, o_t, log_sum, do_all,
            part_one, part_two, grad_out_t.reshape(split + (local,)), n_one, w_query, w_key,
            w_value, inputs, d_hidden, row(ln1_gain), vectors, count,
        ),
    )
    if single:
        leaving = (
            output, input_grad, grad_query, grad_key, grad_value, grad_out_t, grad_up, grad_down_t,
            gain_one, bias_one, gain_two, bias_two, loss,
        )
        (
            output, input_grad, grad_query, grad_key, grad_value, grad_out_t, grad_up, grad_down_t,
            gain_one, bias_one, gain_two, bias_two, loss,
        ) = pl.pallas_call(
            functools.partial(copy_kernel, len(leaving)),
            name="leave",
            out_shape=tuple(out(array.shape, array.dtype) for array in leaving),
            in_specs=[in_hbm()] * len(leaving),
            out_specs=tuple(in_hbm() for _ in leaving),
            scratch_shapes=[pltpu.VMEM(array.shape, array.dtype) for array in leaving]
            + [dma(len(leaving)), dma(len(leaving))],
        )(*leaving)
    grad_down, grad_out = grad_down_t.T, grad_out_t.T
    small = [gain_one, bias_one, gain_two, bias_two]
    small = [vector.reshape(share) for vector in small]
    loss_value = loss.reshape(())
    if not single:
        index = lax.axis_index("dp")
        first = lax.rem(index, SEQ_DEV) * share

        def spread(part, axis):
            shape = list(part.shape)
            shape[axis] = width
            at = [0, 0]
            at[axis] = first
            placed = lax.dynamic_update_slice(jnp.zeros(shape, f32), part, tuple(at))
            return lax.psum_scatter(placed, "dp", scatter_dimension=axis, tiled=True)

        grad_query, grad_key, grad_value, grad_up = (
            spread(part, 0) for part in (grad_query, grad_key, grad_value, grad_up)
        )
        grad_out, grad_down = spread(grad_out, 1), spread(grad_down, 1)
        sums = lax.psum(jnp.where(first == 0, sums, 0.0), "dp")
        length = width // dp_size
        small = [lax.dynamic_slice(sums[k], (index * length,), (length,)) for k in (3, 4, 0, 1)]
        loss_value = jnp.sum(sums[2]) / (2.0 * count[0, 0])
    return (
        output, loss_value, input_grad, small[0], small[1], grad_query, grad_key, grad_value,
        grad_out, small[2], small[3], grad_up, grad_down,
    )


def solution(mesh):
    return jax.shard_map(
        per_device,
        mesh=mesh,
        in_specs=(
            P("dp", None), P(), P(), P(None, "tensor"), P(None, "tensor"), P(None, "tensor"),
            P("tensor", None), P(), P(), P(None, "tensor"), P("tensor", None), P("dp", None),
            P("dp"),
        ),
        out_specs=(
            P("dp", None), P(), P("dp", None), P("dp"), P("dp"), P("dp", "tensor"),
            P("dp", "tensor"), P("dp", "tensor"), P("tensor", "dp"), P("dp"), P("dp"),
            P("dp", "tensor"), P("tensor", "dp"),
        ),
        check_vma=False,
    )
```
